256 devices in a mesh: leaf: 32 (over x, y, core), mp: 8 (over z).
Axes of the slice: x: 4, y: 4, z: 8, core: 2. Of those that a mesh axis runs over, the one named last changes fastest.
Arguments:
- activations: bfloat16 [8192, 4096], P('leaf', 'mp'), may hold values from -6 to 6
- w_query: bfloat16 [4096, 2048], P(None, 'mp'), may hold values from -0.0625 to 0.0625
- w_key: bfloat16 [4096, 2048], P(None, 'mp'), may hold values from -0.0625 to 0.0625
- w_value: bfloat16 [4096, 2048], P(None, 'mp'), may hold values from -0.09375 to 0.09375
- w_out: bfloat16 [2048, 4096], P('mp'), may hold values from -0.70710678 to 0.70710678
- norm_gain: float32 [4096], P('mp'), may hold values from 0.1 to 1.9
- key_cache: bfloat16 [256, 256, 2048], P('leaf', None, 'mp'), may hold values from -6 to 6
- value_cache: bfloat16 [256, 256, 2048], P('leaf', None, 'mp'), may hold values from -6 to 6
- parent: int32 [256], replicated, may hold values from 0 to 255, as said below
- node_len: int32 [256], replicated, may hold values from 1 to 256, as said below
- req_leaf: int32 [128], replicated, may hold values from 0 to 255, as said below
Outputs:
- layer_out: bfloat16 [8192, 4096], P('leaf', 'mp')
The draws below stay inside these ranges and needn't reach their ends.
Inputs may be any that keep to these rules, and one draw needn't show every extreme that they name: Exactly 4 nodes are their own parent (the roots); node n's cache is held by leaf index n // 8. Every request's leaf, its parent and that parent's parent are three distinct nodes, the last a root; no request's middle or leaf node is held by a leaf index that holds a root. `node_len`: every root has 256 live rows. `req_leaf`: over the 4 requests of one leaf index, the nodes of their paths counted with repetition lie at most 2 on any one holder, and their middle and leaf nodes at most 2; both bounds are reached on some holder for every leaf index.
All inputs are finite; a program needn't handle non-finite values.
Results may differ from the reference program's by a relative error of at most 0.03.
Values may be sent and summed in bfloat16 or wider, within the bound.
A program may use at most 128 MiB of HBM per device.

```python
import math
import jax
import jax.numpy as jnp
from jax import lax

D = 4096
HD = 128
H = 16
TENANTS = 4
NODE_DEV = 8
REQ_LEN = 64
CAP = 256
REQ_DEV = 4
HS = 2048
TOKENS = 8192
REQS = 128
NODES = 256
N_MP = 8


def tree_layout(key):
    base_key = jax.random.fold_in(key, 91)
    key_perm, key_shift, key_tenant, key_len = jax.random.split(base_key, 4)
    owners = NODES // NODE_DEV
    spread = owners - TENANTS
    owner_order = jax.random.permutation(key_perm, owners).astype(jnp.int32)
    node_ids = jnp.arange(NODES, dtype=jnp.int32)
    holder = node_ids // NODE_DEV
    slot_of = node_ids % NODE_DEV
    rank_of = jnp.zeros((owners,), jnp.int32).at[owner_order].set(jnp.arange(owners, dtype=jnp.int32))
    placed = rank_of[holder]
    root_node = owner_order[:TENANTS] * NODE_DEV
    on_root = placed < TENANTS
    middle_parent = root_node[jnp.minimum(slot_of, TENANTS - 1)]
    next_rank = TENANTS + (jnp.maximum(placed - TENANTS, 0) + 1) % spread
    next_holder = owner_order[next_rank]
    leaf_parent = next_holder * NODE_DEV + slot_of - TENANTS
    parent = jnp.where(on_root, holder * NODE_DEV, jnp.where(slot_of < TENANTS, middle_parent, leaf_parent)).astype(jnp.int32)
    request = jnp.arange(REQS, dtype=jnp.int32)
    sender = request // REQ_DEV
    within = request % REQ_DEV
    offsets = jax.random.randint(key_shift, (owners,), 0, spread)
    turn_shift = jax.random.randint(key_tenant, (owners,), 0, TENANTS)
    tenant = (within + turn_shift[sender]) % TENANTS
    target = owner_order[TENANTS + (offsets[sender] + within) % spread]
    req_leaf = (target * NODE_DEV + TENANTS + tenant).astype(jnp.int32)
    lengths = jax.random.randint(key_len, (NODES,), 1, CAP + 1)
    lengths = jnp.where(on_root & (slot_of == 0), CAP, lengths).astype(jnp.int32)
    return (parent, lengths, req_leaf)


def draw_parent(key, part):
    return tree_layout(key)[0]


def draw_node_len(key, part):
    return tree_layout(key)[1]


def draw_req_leaf(key, part):
    return tree_layout(key)[2]


def draw_activations(key, part):
    own_key = jax.random.fold_in(key, 11)
    values = jax.random.truncated_normal(own_key, -6.0, 6.0, (TOKENS, D), jnp.float32)
    return values.astype(jnp.bfloat16)


def projection_draw(key, salt):
    own_key = jax.random.fold_in(key, salt)
    values = jax.random.truncated_normal(own_key, -4.0, 4.0, (D, HS), jnp.float32) * D ** (-0.5)
    return values.astype(jnp.bfloat16)


def draw_w_query(key, part):
    return projection_draw(key, 12)


def draw_w_key(key, part):
    return projection_draw(key, 13)


def draw_w_out(key, part):
    own_key = jax.random.fold_in(key, 15)
    place = jnp.arange(D, dtype=jnp.float32) / (D - 1)
    column_scale = jnp.exp(place * math.log(4.0))
    noise = jax.random.truncated_normal(own_key, -4.0, 4.0, (HS, D), jnp.float32)
    values = noise * column_scale[None, :] * HS ** (-0.5)
    return values.astype(jnp.bfloat16)


def draw_key_cache(key, part):
    own_key = jax.random.fold_in(key, 14)
    values = jax.random.truncated_normal(own_key, -6.0, 6.0, (NODES, CAP, HS), jnp.float32)
    return values.astype(jnp.bfloat16)


def shard_levels(key, shape, pieces, least, largest):
    def one(dim, shards_of):
        draws = jax.random.uniform(jax.random.fold_in(jax.random.fold_in(key, 6), dim), (shards_of,), jnp.float32, least / len(pieces), largest / len(pieces))
        return jnp.repeat(jnp.exp(draws), shape[dim] // shards_of).reshape((-1,) + (1,) * (len(shape) - dim - 1))

    factor_of = one(*pieces[0])
    for cut in pieces[1:]:
        factor_of = factor_of * one(*cut)
    return factor_of


def bell_draw(rng, extent, scale, limit, shards=(), kind=jnp.bfloat16):
    values = jax.random.normal(rng, extent, jnp.float32) * scale
    if len(shards) > 0:
        values = shard_levels(rng, extent, shards, -0.22, 0.18) * values
    return jnp.clip(values, min=-limit, max=limit).astype(kind)


def setup_inputs(seed: int = 0) -> dict:
    key_of = jax.random.split(jax.random.key(seed), 12)
    return {
        "activations": draw_activations(jax.random.fold_in(key_of[11], 71), 0),
        "w_query": draw_w_query(jax.random.fold_in(key_of[11], 71), 0),
        "w_key": draw_w_key(jax.random.fold_in(key_of[11], 71), 0),
        "w_value": bell_draw(key_of[3], (D, HS), D ** -0.5, 0.09375, ((1, 8),)),
        "w_out": draw_w_out(jax.random.fold_in(key_of[11], 71), 0),
        "norm_gain": jnp.clip(1.0 + 0.18 * jax.random.normal(key_of[5], (D,), jnp.float32), 0.1, 1.9),
        "key_cache": draw_key_cache(jax.random.fold_in(key_of[11], 71), 0),
        "value_cache": bell_draw(key_of[7], (NODES, CAP, HS), 1.0, 6.0, ((0, 32), (2, 8))),
        "parent": draw_parent(jax.random.fold_in(key_of[11], 71), 0),
        "node_len": draw_node_len(jax.random.fold_in(key_of[11], 71), 0),
        "req_leaf": draw_req_leaf(jax.random.fold_in(key_of[11], 71), 0),
    }


rope_base = 500000.0
mask_value = -1e+30
norm_eps = 1e-06

def rotate(values, positions):
    half_width = values.shape[-1] // 2
    inverse_freq = jnp.exp(jnp.arange(half_width, dtype=jnp.float32) * (-2.0 * math.log(rope_base) / values.shape[-1]))
    angles = positions.astype(jnp.float32)[:, None] * inverse_freq[None, :]
    cosine = jnp.cos(angles)[:, None, :]
    sine_part = jnp.sin(angles)[:, None, :]
    front_half = values[..., :half_width]
    back_half = values[..., half_width:]
    return jnp.concatenate([front_half * cosine - back_half * sine_part, back_half * cosine + front_half * sine_part], axis=-1)

def node_partial(queries, keys, values, row_count):
    head_dim = queries.shape[-1]
    scores = jnp.einsum('qhd,khd->hqk', queries.astype(jnp.float32), keys.astype(jnp.float32)) * head_dim ** (-0.5)
    live_mask = jnp.arange(keys.shape[0]) < row_count
    scores = jnp.where(live_mask[None, None, :], scores, mask_value)
    highest = lax.optimization_barrier(jnp.max(scores, axis=-1))
    weights = jnp.exp(scores - highest[..., None])
    totals = lax.optimization_barrier(jnp.sum(weights, axis=-1))
    rounded = lax.optimization_barrier(weights.astype(jnp.bfloat16)).astype(jnp.float32)
    mixture = jnp.einsum('hqk,khd->qhd', rounded, values.astype(jnp.float32))
    result = (mixture / jnp.transpose(totals)[:, :, None]).astype(jnp.bfloat16)
    return (result, jnp.transpose(highest + jnp.log(totals)))

def self_partial(queries, keys, values):
    head_dim = queries.shape[-1]
    row_total = queries.shape[0]
    scores = jnp.einsum('qhd,khd->hqk', queries.astype(jnp.float32), keys.astype(jnp.float32)) * head_dim ** (-0.5)
    causal = jnp.arange(row_total)[:, None] >= jnp.arange(row_total)[None, :]
    scores = jnp.where(causal[None], scores, mask_value)
    highest = lax.optimization_barrier(jnp.max(scores, axis=-1))
    weights = jnp.exp(scores - highest[..., None])
    totals = lax.optimization_barrier(jnp.sum(weights, axis=-1))
    rounded = lax.optimization_barrier(weights.astype(jnp.bfloat16)).astype(jnp.float32)
    mixture = jnp.einsum('hqk,khd->qhd', rounded, values.astype(jnp.float32))
    return (mixture / jnp.transpose(totals)[:, :, None], jnp.transpose(highest + jnp.log(totals)))

def reference(activations, w_query, w_key, w_value, w_out, norm_gain, key_cache, value_cache, parent, node_len, req_leaf):
    middle = parent[req_leaf]
    root_of = parent[middle]
    node_path = jnp.stack([root_of, middle, req_leaf], axis=1)
    prefix = node_len[root_of] + node_len[middle] + node_len[req_leaf]
    position = (prefix[:, None] + jnp.arange(REQ_LEN, dtype=jnp.int32)[None, :]).reshape(TOKENS).astype(jnp.int32)
    query_f = jnp.dot(activations, w_query, preferred_element_type=jnp.float32).reshape(TOKENS, H, HD)
    key_f = jnp.dot(activations, w_key, preferred_element_type=jnp.float32).reshape(TOKENS, H, HD)
    value_f = jnp.dot(activations, w_value, preferred_element_type=jnp.float32)
    queries = rotate(query_f, position).astype(jnp.bfloat16).reshape(REQS, REQ_LEN, H, HD)
    keys = rotate(key_f, position).astype(jnp.bfloat16).reshape(REQS, REQ_LEN, H, HD)
    values = value_f.astype(jnp.bfloat16).reshape(REQS, REQ_LEN, H, HD)
    cached_keys = key_cache.reshape(NODES, CAP, H, HD)
    cached_values = value_cache.reshape(NODES, CAP, H, HD)

    def one_request(request_item):
        block_q, block_k, block_v, path_nodes = request_item
        level_outs = []
        level_lses = []
        for depth_level in range(3):
            chosen = path_nodes[depth_level]
            result, log_total = node_partial(block_q, cached_keys[chosen], cached_values[chosen], node_len[chosen])
            level_outs.append(lax.optimization_barrier(result).astype(jnp.float32))
            level_lses.append(log_total)
        own_out, own_lse = self_partial(block_q, block_k, block_v)
        level_outs.append(own_out)
        level_lses.append(own_lse)
        stacked_lse = jnp.stack(level_lses)
        highest = lax.optimization_barrier(jnp.max(stacked_lse, axis=0))
        factor = jnp.exp(stacked_lse - highest[None])
        merged = lax.optimization_barrier(jnp.sum(factor[..., None] * jnp.stack(level_outs), axis=0)) / lax.optimization_barrier(jnp.sum(factor, axis=0))[..., None]
        return merged.astype(jnp.bfloat16)
    attn = lax.map(one_request, (queries, keys, values, node_path)).reshape(TOKENS, HS)
    group_width = HS // N_MP
    projected = jnp.zeros((TOKENS, D), jnp.float32)
    for group_index in range(N_MP):
        group_part = jnp.dot(attn[:, group_index * group_width:(group_index + 1) * group_width], w_out[group_index * group_width:(group_index + 1) * group_width], preferred_element_type=jnp.float32)
        projected = projected + lax.optimization_barrier(group_part.astype(jnp.bfloat16)).astype(jnp.float32)
    mean_square = lax.optimization_barrier(jnp.mean(projected * projected, axis=1, keepdims=True))
    return (activations.astype(jnp.float32) + norm_gain[None, :] * projected * lax.rsqrt(mean_square + norm_eps)).astype(jnp.bfloat16)
```

```python
import math

import jax
import jax.numpy as jnp
from jax import lax
from jax.sharding import PartitionSpec as P

D = 4096
HD = 128
TENANTS = 4
NODE_DEV = 8
REQ_LEN = 64
REQ_DEV = 4


rope_base = 500000.0
mask_value = -1e30
norm_eps = 1e-06


def rotate(values, positions):
    half_width = values.shape[-1] // 2
    inverse_freq = jnp.exp(
        jnp.arange(half_width, dtype=jnp.float32) * (-2.0 * math.log(rope_base) / values.shape[-1])
    )
    angles = positions.astype(jnp.float32)[:, None] * inverse_freq[None, :]
    cosine = jnp.cos(angles)[:, None, :]
    sine_part = jnp.sin(angles)[:, None, :]
    front_half = values[..., :half_width]
    back_half = values[..., half_width:]
    return jnp.concatenate(
        [front_half * cosine - back_half * sine_part, back_half * cosine + front_half * sine_part],
        axis=-1,
    )


def lookup(table, index):
    hit = index[..., None] == jnp.arange(table.shape[0], dtype=index.dtype)
    return jnp.sum(jnp.where(hit, table, 0), axis=-1).astype(table.dtype)


def node_attention(queries, keys, values, lengths, heads_local):
    blocks, row_total, width = queries.shape
    head_dim = width // heads_local
    query_heads = queries.reshape(blocks, row_total, heads_local, head_dim)
    key_heads = keys.reshape(blocks, keys.shape[1], heads_local, head_dim)
    value_heads = values.reshape(blocks, values.shape[1], heads_local, head_dim)
    scores = jnp.einsum(
        "nqhd,nkhd->nhqk", query_heads, key_heads, preferred_element_type=jnp.float32
    ) * head_dim ** (-0.5)
    live_mask = jnp.arange(keys.shape[1])[None, :] < lengths[:, None]
    scores = jnp.where(live_mask[:, None, None, :], scores, mask_value)
    highest = jnp.max(scores, axis=-1)
    weights = jnp.exp(scores - highest[..., None])
    totals = jnp.sum(weights, axis=-1)
    mixture = jnp.einsum(
        "nhqk,nkhd->nqhd",
        weights.astype(jnp.bfloat16),
        value_heads,
        preferred_element_type=jnp.float32,
    )
    result = (
        (mixture / jnp.transpose(totals, (0, 2, 1))[..., None])
        .astype(jnp.bfloat16)
        .reshape(blocks, row_total, width)
    )
    return (result, jnp.transpose(highest + jnp.log(totals), (0, 2, 1)))


def self_attention(queries, keys, values):
    head_dim = queries.shape[-1]
    row_total = queries.shape[1]
    scores = jnp.einsum(
        "rqhd,rkhd->rhqk", queries, keys, preferred_element_type=jnp.float32
    ) * head_dim ** (-0.5)
    causal = jnp.arange(row_total)[:, None] >= jnp.arange(row_total)[None, :]
    scores = jnp.where(causal[None, None], scores, mask_value)
    highest = jnp.max(scores, axis=-1)
    weights = jnp.exp(scores - highest[..., None])
    totals = jnp.sum(weights, axis=-1)
    mixture = jnp.einsum(
        "rhqk,rkhd->rqhd", weights.astype(jnp.bfloat16), values, preferred_element_type=jnp.float32
    )
    return (
        mixture / jnp.transpose(totals, (0, 2, 1))[..., None],
        jnp.transpose(highest + jnp.log(totals), (0, 2, 1)),
    )


def on_device(
    activations,
    w_query,
    w_key,
    w_value,
    w_out,
    norm_gain,
    key_cache,
    value_cache,
    parent,
    node_len,
    req_leaf,
):
    leaf_count = lax.axis_size("leaf")
    device = lax.axis_index("leaf")
    tok_rows = activations.shape[0]
    width_local = w_query.shape[1]
    heads_local = width_local // HD
    spread = leaf_count - TENANTS
    node_slots = 2 * ((REQ_DEV + spread - 1) // spread)
    all_slots = max(REQ_DEV // TENANTS, node_slots)
    block = REQ_LEN * width_local
    columns = lax.all_gather(activations, "mp", axis=1, tiled=True)
    query_f, key_f, value_f = tuple(
        (
            jnp.dot(columns, matrix, preferred_element_type=jnp.float32)
            for matrix in (w_query, w_key, w_value)
        )
    )
    middle_all = lookup(parent, req_leaf)
    root_all = lookup(parent, middle_all)
    len_of = lambda nodes: lookup(node_len, nodes)
    prefix = len_of(root_all) + len_of(middle_all) + len_of(req_leaf)
    mine_prefix = lax.dynamic_slice_in_dim(prefix, device * REQ_DEV, REQ_DEV)
    position = (mine_prefix[:, None] + jnp.arange(REQ_LEN, dtype=jnp.int32)[None, :]).reshape(
        tok_rows
    )
    queries = rotate(query_f.reshape(tok_rows, heads_local, HD), position).astype(jnp.bfloat16)
    keys = rotate(key_f.reshape(tok_rows, heads_local, HD), position).astype(jnp.bfloat16)
    values = value_f.astype(jnp.bfloat16)
    q_blocks = queries.reshape(REQ_DEV, block)
    self_out, self_lse = self_attention(
        queries.reshape(REQ_DEV, REQ_LEN, heads_local, HD),
        keys.reshape(REQ_DEV, REQ_LEN, heads_local, HD),
        values.reshape(REQ_DEV, REQ_LEN, heads_local, HD),
    )
    levels_all = jnp.stack([root_all, middle_all, req_leaf], axis=0).reshape(3, leaf_count, REQ_DEV)
    level_count = levels_all.shape[0]
    items = level_count * REQ_DEV
    per_sender = jnp.transpose(levels_all, (1, 0, 2)).reshape(leaf_count, items)
    holders = per_sender // NODE_DEV
    earlier = jnp.arange(items)[:, None] > jnp.arange(items)[None, :]
    ranks = jnp.sum(
        earlier[None] & (holders[:, :, None] == holders[:, None, :]), axis=2
    ).astype(jnp.int32)
    slot_ids = jnp.arange(all_slots, dtype=jnp.int32)
    my_holders = lax.dynamic_index_in_dim(holders, device, 0, keepdims=False)
    my_ranks = lax.dynamic_index_in_dim(ranks, device, 0, keepdims=False)
    send_hit = (
        (my_holders[None, None, :] == jnp.arange(leaf_count, dtype=jnp.int32)[:, None, None])
        & (my_ranks[None, None, :] == slot_ids[None, :, None])
    )
    send_item = jnp.sum(jnp.where(send_hit, jnp.arange(items, dtype=jnp.int32), 0), axis=2)
    send_valid = jnp.any(send_hit, axis=2)
    outgoing = jnp.where(
        send_valid.reshape(-1)[:, None],
        jnp.take(q_blocks, (send_item % REQ_DEV).reshape(-1), axis=0),
        jnp.zeros((), jnp.bfloat16),
    ).reshape(leaf_count, all_slots * block)
    arrived = lax.all_to_all(outgoing, "leaf", split_axis=0, concat_axis=0, tiled=True)
    recv_hit = (holders[:, None, :] == device) & (ranks[:, None, :] == slot_ids[None, :, None])
    slot_nodes = jnp.sum(jnp.where(recv_hit, per_sender[:, None, :], 0), axis=2).reshape(-1)
    filled = jnp.any(recv_hit, axis=2).reshape(-1)
    local_slot = jnp.where(filled, slot_nodes - device * NODE_DEV, 0)
    lengths = jnp.where(filled, len_of(slot_nodes), 0)
    node_out, node_lse = node_attention(
        arrived.reshape(leaf_count * all_slots, REQ_LEN, width_local),
        key_cache[local_slot],
        value_cache[local_slot],
        lengths,
        heads_local,
    )
    flat_lse = node_lse.reshape(leaf_count * all_slots, REQ_LEN * heads_local)
    lse_high = lax.reduce_precision(flat_lse, exponent_bits=8, mantissa_bits=7)
    lse_low = (flat_lse - lse_high).astype(jnp.bfloat16)
    payload = jnp.concatenate(
        [
            node_out.reshape(leaf_count * all_slots, block),
            lse_high.astype(jnp.bfloat16),
            lse_low,
        ],
        axis=1,
    )
    piece = payload.shape[1]
    back = lax.all_to_all(
        payload.reshape(leaf_count, all_slots * piece),
        "leaf",
        split_axis=0,
        concat_axis=0,
        tiled=True,
    ).reshape(leaf_count * all_slots, piece)
    got = jnp.take(back, my_holders * all_slots + my_ranks, axis=0)
    got_out = got[:, :block].reshape(level_count, REQ_DEV, REQ_LEN, heads_local, HD)
    lse_width = REQ_LEN * heads_local
    got_lse = (
        got[:, block : block + lse_width].astype(jnp.float32)
        + got[:, block + lse_width :].astype(jnp.float32)
    ).reshape(level_count, REQ_DEV, REQ_LEN, heads_local)
    partial_out = jnp.concatenate([got_out.astype(jnp.float32), self_out[None]], axis=0)
    partial_lse = jnp.concatenate([got_lse, self_lse[None]], axis=0)
    highest = jnp.max(partial_lse, axis=0)
    factor = jnp.exp(partial_lse - highest[None])
    merged = jnp.sum(factor[..., None] * partial_out, axis=0) / jnp.sum(factor, axis=0)[..., None]
    attn = merged.astype(jnp.bfloat16).reshape(tok_rows, width_local)
    partial_value = jnp.dot(attn, w_out, preferred_element_type=jnp.float32)
    projected = lax.psum_scatter(
        partial_value.astype(jnp.bfloat16), "mp", scatter_dimension=1, tiled=True
    ).astype(jnp.float32)
    squares = jnp.sum(
        lax.all_gather(jnp.sum(projected * projected, axis=1), "mp", axis=0), axis=0
    )
    row_scale = lax.rsqrt(squares / D + norm_eps)
    return (
        activations.astype(jnp.float32) + norm_gain[None, :] * projected * row_scale[:, None]
    ).astype(jnp.bfloat16)


def solution(mesh):
    in_specs = (
        P("leaf", "mp"),
        P(None, "mp"),
        P(None, "mp"),
        P(None, "mp"),
        P("mp", None),
        P("mp"),
        P("leaf", None, "mp"),
        P("leaf", None, "mp"),
        P(),
        P(),
        P(),
    )
    out_specs = P("leaf", "mp")
    return jax.shard_map(
        on_device, mesh=mesh, in_specs=in_specs, out_specs=out_specs, check_vma=False
    )
```

```python
import math

import jax
import jax.numpy as jnp
from jax import lax
from jax.experimental import pallas as pl
from jax.experimental.pallas import tpu as pltpu
from jax.sharding import PartitionSpec as P

D = 4096
HD = 128
TENANTS = 4
NODE_DEV = 8
REQ_LEN = 64
REQ_DEV = 4


rope_base = 500000.0
mask_value = -1e30
norm_eps = 1e-06


def rotate(values, positions):
    half_width = values.shape[-1] // 2
    inverse_freq = jnp.exp(
        jnp.arange(half_width, dtype=jnp.float32) * (-2.0 * math.log(rope_base) / values.shape[-1])
    )
    angles = positions.astype(jnp.float32)[:, None] * inverse_freq[None, :]
    cosine = jnp.cos(angles)[:, None, :]
    sine_part = jnp.sin(angles)[:, None, :]
    front_half = values[..., :half_width]
    back_half = values[..., half_width:]
    return jnp.concatenate(
        [front_half * cosine - back_half * sine_part, back_half * cosine + front_half * sine_part],
        axis=-1,
    )


def lookup(table, index):
    hit = index[..., None] == jnp.arange(table.shape[0], dtype=index.dtype)
    return jnp.sum(jnp.where(hit, table, 0), axis=-1).astype(table.dtype)


def node_kernel(slot_ref, len_ref, q_ref, k_ref, v_ref, out_ref, lse_ref):
    slots, rows, width = q_ref.shape
    cache_rows = k_ref.shape[1]
    heads = width // HD

    def body(i, carry):
        node = slot_ref[i]
        length = len_ref[i]

        @pl.when(length > 0)
        def _():
            live = lax.broadcasted_iota(jnp.int32, (rows, cache_rows), 1) < length
            for h in range(heads):
                cols = pl.ds(h * HD, HD)
                q = q_ref[i, :, cols]
                k = k_ref[node, :, cols]
                v = v_ref[node, :, cols]
                s = lax.dot_general(
                    q, k, (((1,), (1,)), ((), ())), preferred_element_type=jnp.float32
                ) * HD ** (-0.5)
                s = jnp.where(live, s, mask_value)
                m = jnp.max(s, axis=1, keepdims=True)
                p = jnp.exp(s - m)
                l = jnp.sum(p, axis=1, keepdims=True)
                o = jnp.dot(p.astype(jnp.bfloat16), v, preferred_element_type=jnp.float32)
                out_ref[i, :, cols] = (o / l).astype(out_ref.dtype)
                lse_ref[i, :, pl.ds(h, 1)] = m + jnp.log(l)

        @pl.when(length == 0)
        def _():
            out_ref[i] = jnp.zeros((rows, width), out_ref.dtype)
            lse_ref[i] = jnp.zeros((rows, heads), lse_ref.dtype)

        return carry

    lax.fori_loop(0, slots, body, 0)


def node_attention(queries, key_cache, value_cache, local_slot, lengths, heads_local):
    slots, rows, width = queries.shape
    nodes, cache_rows, _ = key_cache.shape
    vmem = pl.BlockSpec(memory_space=pltpu.VMEM)
    smem = pl.BlockSpec(memory_space=pltpu.SMEM)
    flops = 4 * slots * rows * cache_rows * width
    return pl.pallas_call(
        node_kernel,
        out_shape=(
            jax.ShapeDtypeStruct((slots, rows, width), jnp.bfloat16),
            jax.ShapeDtypeStruct((slots, rows, heads_local), jnp.float32),
        ),
        in_specs=[smem, smem, vmem, vmem, vmem],
        out_specs=(vmem, vmem),
        cost_estimate=pl.CostEstimate(
            flops=flops,
            transcendentals=slots * rows * cache_rows * heads_local,
            bytes_accessed=2 * queries.size * 2 + 2 * key_cache.size * 2,
        ),
    )(local_slot, lengths, queries, key_cache, value_cache)


def self_attention(queries, keys, values):
    head_dim = queries.shape[-1]
    row_total = queries.shape[1]
    scores = jnp.einsum(
        "rqhd,rkhd->rhqk", queries, keys, preferred_element_type=jnp.float32
    ) * head_dim ** (-0.5)
    causal = jnp.arange(row_total)[:, None] >= jnp.arange(row_total)[None, :]
    scores = jnp.where(causal[None, None], scores, mask_value)
    highest = jnp.max(scores, axis=-1)
    weights = jnp.exp(scores - highest[..., None])
    totals = jnp.sum(weights, axis=-1)
    mixture = jnp.einsum(
        "rhqk,rkhd->rqhd", weights.astype(jnp.bfloat16), values, preferred_element_type=jnp.float32
    )
    return (
        mixture / jnp.transpose(totals, (0, 2, 1))[..., None],
        jnp.transpose(highest + jnp.log(totals), (0, 2, 1)),
    )


def on_device(
    activations,
    w_query,
    w_key,
    w_value,
    w_out,
    norm_gain,
    key_cache,
    value_cache,
    parent,
    node_len,
    req_leaf,
):
    leaf_count = lax.axis_size("leaf")
    device = lax.axis_index("leaf")
    tok_rows = activations.shape[0]
    width_local = w_query.shape[1]
    heads_local = width_local // HD
    spread = leaf_count - TENANTS
    node_slots = 2 * ((REQ_DEV + spread - 1) // spread)
    all_slots = max(REQ_DEV // TENANTS, node_slots)
    block = REQ_LEN * width_local
    columns = lax.all_gather(activations, "mp", axis=1, tiled=True)
    query_f, key_f, value_f = tuple(
        (
            jnp.dot(columns, matrix, preferred_element_type=jnp.float32)
            for matrix in (w_query, w_key, w_value)
        )
    )
    middle_all = lookup(parent, req_leaf)
    root_all = lookup(parent, middle_all)
    len_of = lambda nodes: lookup(node_len, nodes)
    prefix = len_of(root_all) + len_of(middle_all) + len_of(req_leaf)
    mine_prefix = lax.dynamic_slice_in_dim(prefix, device * REQ_DEV, REQ_DEV)
    position = (mine_prefix[:, None] + jnp.arange(REQ_LEN, dtype=jnp.int32)[None, :]).reshape(
        tok_rows
    )
    queries = rotate(query_f.reshape(tok_rows, heads_local, HD), position).astype(jnp.bfloat16)
    keys = rotate(key_f.reshape(tok_rows, heads_local, HD), position).astype(jnp.bfloat16)
    values = value_f.astype(jnp.bfloat16)
    q_blocks = queries.reshape(REQ_DEV, block)
    self_out, self_lse = self_attention(
        queries.reshape(REQ_DEV, REQ_LEN, heads_local, HD),
        keys.reshape(REQ_DEV, REQ_LEN, heads_local, HD),
        values.reshape(REQ_DEV, REQ_LEN, heads_local, HD),
    )
    levels_all = jnp.stack([root_all, middle_all, req_leaf], axis=0).reshape(3, leaf_count, REQ_DEV)
    level_count = levels_all.shape[0]
    items = level_count * REQ_DEV
    per_sender = jnp.transpose(levels_all, (1, 0, 2)).reshape(leaf_count, items)
    holders = per_sender // NODE_DEV
    earlier = jnp.arange(items)[:, None] > jnp.arange(items)[None, :]
    ranks = jnp.sum(
        earlier[None] & (holders[:, :, None] == holders[:, None, :]), axis=2
    ).astype(jnp.int32)
    slot_ids = jnp.arange(all_slots, dtype=jnp.int32)
    my_holders = lax.dynamic_index_in_dim(holders, device, 0, keepdims=False)
    my_ranks = lax.dynamic_index_in_dim(ranks, device, 0, keepdims=False)
    send_hit = (
        (my_holders[None, None, :] == jnp.arange(leaf_count, dtype=jnp.int32)[:, None, None])
        & (my_ranks[None, None, :] == slot_ids[None, :, None])
    )
    send_item = jnp.sum(jnp.where(send_hit, jnp.arange(items, dtype=jnp.int32), 0), axis=2)
    send_valid = jnp.any(send_hit, axis=2)
    pick = (
        send_valid[:, :, None] & (send_item[:, :, None] % REQ_DEV == jnp.arange(REQ_DEV))
    ).reshape(leaf_count * all_slots, REQ_DEV)
    outgoing = (
        jnp.dot(pick.astype(jnp.bfloat16), q_blocks, preferred_element_type=jnp.float32)
        .astype(jnp.bfloat16)
        .reshape(leaf_count, all_slots, REQ_LEN, width_local)
    )
    arrived = lax.all_to_all(outgoing, "leaf", split_axis=0, concat_axis=0, tiled=True)
    recv_hit = (holders[:, None, :] == device) & (ranks[:, None, :] == slot_ids[None, :, None])
    slot_nodes = jnp.sum(jnp.where(recv_hit, per_sender[:, None, :], 0), axis=2).reshape(-1)
    filled = jnp.any(recv_hit, axis=2).reshape(-1)
    local_slot = jnp.where(filled, slot_nodes - device * NODE_DEV, 0)
    lengths = jnp.where(filled, len_of(slot_nodes), 0)
    node_out, node_lse = node_attention(
        arrived.reshape(leaf_count * all_slots, REQ_LEN, width_local),
        key_cache,
        value_cache,
        local_slot,
        lengths,
        heads_local,
    )
    flat_lse = node_lse.reshape(leaf_count * all_slots, REQ_LEN * heads_local)
    lse_high = lax.reduce_precision(flat_lse, exponent_bits=8, mantissa_bits=7)
    lse_low = flat_lse - lse_high
    lse_pair = jnp.stack([lse_high, lse_low], axis=1).astype(jnp.bfloat16)
    back_out = lax.all_to_all(
        node_out.reshape(leaf_count, all_slots, REQ_LEN, width_local),
        "leaf",
        split_axis=0,
        concat_axis=0,
        tiled=True,
    )
    back_lse = lax.all_to_all(
        lse_pair.reshape(leaf_count, all_slots, 2, REQ_LEN * heads_local),
        "leaf",
        split_axis=0,
        concat_axis=0,
        tiled=True,
    )
    take = (
        (my_holders * all_slots + my_ranks)[:, None]
        == jnp.arange(leaf_count * all_slots, dtype=jnp.int32)[None, :]
    ).astype(jnp.bfloat16)
    got_out = (
        jnp.dot(take, back_out.reshape(leaf_count * all_slots, block), preferred_element_type=jnp.float32)
        .reshape(level_count, REQ_DEV, REQ_LEN, heads_local, HD)
    )
    got_pair = jnp.dot(
        take,
        back_lse.reshape(leaf_count * all_slots, 2 * REQ_LEN * heads_local),
        preferred_element_type=jnp.float32,
    ).reshape(items, 2, REQ_LEN * heads_local)
    got_lse = (got_pair[:, 0] + got_pair[:, 1]).reshape(level_count, REQ_DEV, REQ_LEN, heads_local)
    partial_out = jnp.concatenate([got_out, self_out[None]], axis=0)
    partial_lse = jnp.concatenate([got_lse, self_lse[None]], axis=0)
    highest = jnp.max(partial_lse, axis=0)
    factor = jnp.exp(partial_lse - highest[None])
    merged = jnp.sum(factor[..., None] * partial_out, axis=0) / jnp.sum(factor, axis=0)[..., None]
    attn = merged.astype(jnp.bfloat16).reshape(tok_rows, width_local)
    partial_value = jnp.dot(attn, w_out, preferred_element_type=jnp.float32)
    projected = lax.psum_scatter(
        partial_value.astype(jnp.bfloat16), "mp", scatter_dimension=1, tiled=True
    ).astype(jnp.float32)
    squares = lax.psum(jnp.sum(projected * projected, axis=1), "mp")
    row_scale = lax.rsqrt(squares / D + norm_eps)
    return (
        activations.astype(jnp.float32) + norm_gain[None, :] * projected * row_scale[:, None]
    ).astype(jnp.bfloat16)


def solution(mesh):
    in_specs = (
        P("leaf", "mp"),
        P(None, "mp"),
        P(None, "mp"),
        P(None, "mp"),
        P("mp", None),
        P("mp"),
        P("leaf", None, "mp"),
        P("leaf", None, "mp"),
        P(),
        P(),
        P(),
    )
    out_specs = P("leaf", "mp")
    return jax.shard_map(
        on_device, mesh=mesh, in_specs=in_specs, out_specs=out_specs, check_vma=False
    )
```

```python
import math

import jax
import jax.numpy as jnp
from jax import lax
from jax.experimental import pallas as pl
from jax.experimental.pallas import tpu as pltpu
from jax.sharding import PartitionSpec as P

D = 4096
HD = 128
TENANTS = 4
NODE_DEV = 8
REQ_LEN = 64
REQ_DEV = 4


rope_base = 500000.0
mask_value = -1e30
norm_eps = 1e-06


def rotate(values, positions):
    half_width = values.shape[-1] // 2
    inverse_freq = jnp.exp(
        jnp.arange(half_width, dtype=jnp.float32) * (-2.0 * math.log(rope_base) / values.shape[-1])
    )
    angles = positions.astype(jnp.float32)[:, None] * inverse_freq[None, :]
    cosine = jnp.cos(angles)[:, None, :]
    sine_part = jnp.sin(angles)[:, None, :]
    front_half = values[..., :half_width]
    back_half = values[..., half_width:]
    return jnp.concatenate(
        [front_half * cosine - back_half * sine_part, back_half * cosine + front_half * sine_part],
        axis=-1,
    )


def lookup(table, index):
    hit = index[..., None] == jnp.arange(table.shape[0], dtype=index.dtype)
    return jnp.sum(jnp.where(hit, table, 0), axis=-1).astype(table.dtype)


GROUP = 8


def attend(q, k, v, length, rows, cache_rows):
    live = lax.broadcasted_iota(jnp.int32, (rows, cache_rows), 1) < length
    s = lax.dot_general(
        q, k, (((1,), (1,)), ((), ())), preferred_element_type=jnp.float32
    ) * HD ** (-0.5)
    s = jnp.where(live, s, mask_value)
    m = jnp.max(s, axis=1, keepdims=True)
    p = jnp.exp(s - m)
    l = jnp.sum(p, axis=1, keepdims=True)
    o = jnp.dot(p.astype(jnp.bfloat16), v, preferred_element_type=jnp.float32)
    return o / l, m + jnp.log(l)


def node_kernel(
    slot_ref, len_ref, mode_ref, gnode_ref, glen_ref, q_ref, k_ref, v_ref, out_ref, lse_ref
):
    total_rows, width = q_ref.shape
    cache_rows = k_ref.shape[1]
    heads = width // HD
    groups = mode_ref.shape[0]
    span = GROUP * REQ_LEN

    def one_slot(i, carry):
        node = slot_ref[i]
        length = len_ref[i]
        rows = pl.ds(pl.multiple_of(i * REQ_LEN, REQ_LEN), REQ_LEN)

        @pl.when(length > 0)
        def _():
            for h in range(heads):
                cols = pl.ds(h * HD, HD)
                o, lse = attend(
                    q_ref[rows, cols], k_ref[node, :, cols], v_ref[node, :, cols],
                    length, REQ_LEN, cache_rows,
                )
                out_ref[rows, cols] = o.astype(out_ref.dtype)
                lse_ref[rows, pl.ds(h, 1)] = lse

        @pl.when(length == 0)
        def _():
            out_ref[rows, :] = jnp.zeros((REQ_LEN, width), out_ref.dtype)
            lse_ref[rows, :] = jnp.zeros((REQ_LEN, heads), lse_ref.dtype)

        return carry

    def one_group(g, carry):
        mode = mode_ref[g]
        rows = pl.ds(pl.multiple_of(g * span, span), span)

        @pl.when(mode == 0)
        def _():
            out_ref[rows, :] = jnp.zeros((span, width), out_ref.dtype)
            lse_ref[rows, :] = jnp.zeros((span, heads), lse_ref.dtype)

        @pl.when(mode == 1)
        def _():
            node = gnode_ref[g]
            length = glen_ref[g]
            for h in range(heads):
                cols = pl.ds(h * HD, HD)
                o, lse = attend(
                    q_ref[rows, cols], k_ref[node, :, cols], v_ref[node, :, cols],
                    length, span, cache_rows,
                )
                out_ref[rows, cols] = o.astype(out_ref.dtype)
                lse_ref[rows, pl.ds(h, 1)] = lse

        @pl.when(mode == 2)
        def _():
            lax.fori_loop(g * GROUP, (g + 1) * GROUP, one_slot, 0)

        return carry

    lax.fori_loop(0, groups, one_group, 0)


def node_attention(queries, key_cache, value_cache, local_slot, lengths, heads_local):
    slots, rows, width = queries.shape
    nodes, cache_rows, _ = key_cache.shape
    groups = slots // GROUP
    live = (lengths > 0).reshape(groups, GROUP)
    grouped_node = local_slot.reshape(groups, GROUP)
    grouped_len = lengths.reshape(groups, GROUP)
    group_node = jnp.max(jnp.where(live, grouped_node, 0), axis=1)
    group_len = jnp.max(grouped_len, axis=1)
    uniform = jnp.all(~live | (grouped_node == group_node[:, None]), axis=1)
    mode = jnp.where(jnp.any(live, axis=1), jnp.where(uniform, 1, 2), 0).astype(jnp.int32)
    vmem = pl.BlockSpec(memory_space=pltpu.VMEM)
    smem = pl.BlockSpec(memory_space=pltpu.SMEM)
    flops = 4 * slots * rows * cache_rows * width
    out, lse = pl.pallas_call(
        node_kernel,
        out_shape=(
            jax.ShapeDtypeStruct((slots * rows, width), jnp.bfloat16),
            jax.ShapeDtypeStruct((slots * rows, heads_local), jnp.float32),
        ),
        in_specs=[smem] * 5 + [vmem] * 3,
        out_specs=(vmem, vmem),
        cost_estimate=pl.CostEstimate(
            flops=flops,
            transcendentals=slots * rows * cache_rows * heads_local,
            bytes_accessed=2 * queries.size * 2 + 2 * key_cache.size * 2,
        ),
    )(
        local_slot, lengths, mode, group_node, group_len,
        queries.reshape(slots * rows, width), key_cache, value_cache,
    )
    return out.reshape(slots, rows, width), lse.reshape(slots, rows, heads_local)


def sum_kernel(x_ref, out_ref, recv, send_sem, recv_sem):
    n = recv.shape[0]
    me = lax.axis_index("mp")
    barrier = pltpu.get_barrier_semaphore()
    for d in range(1, n):
        pl.semaphore_signal(
            barrier, inc=1, device_id={"mp": lax.rem(me + d, n)},
            device_id_type=pl.DeviceIdType.MESH,
        )
    pl.semaphore_wait(barrier, n - 1)
    copies = []
    for d in range(1, n):
        copy = pltpu.make_async_remote_copy(
            src_ref=x_ref,
            dst_ref=recv.at[d],
            send_sem=send_sem.at[d],
            recv_sem=recv_sem.at[d],
            device_id={"mp": lax.rem(me + d, n)},
            device_id_type=pl.DeviceIdType.MESH,
        )
        copy.start()
        copies.append(copy)
    for copy in copies:
        copy.wait()
    total = x_ref[...]
    for d in range(1, n):
        total = total + recv[d]
    out_ref[...] = total


def mp_sum(x, n):
    vmem = pl.BlockSpec(memory_space=pltpu.VMEM)
    return pl.pallas_call(
        sum_kernel,
        out_shape=jax.ShapeDtypeStruct(x.shape, x.dtype),
        in_specs=[vmem],
        out_specs=vmem,
        scratch_shapes=[
            pltpu.VMEM((n,) + x.shape, x.dtype),
            pltpu.SemaphoreType.DMA((n,)),
            pltpu.SemaphoreType.DMA((n,)),
        ],
        compiler_params=pltpu.CompilerParams(collective_id=0, has_side_effects=True),
    )(x)


def self_attention(queries, keys, values):
    head_dim = queries.shape[-1]
    row_total = queries.shape[1]
    scores = jnp.einsum(
        "rqhd,rkhd->rhqk", queries, keys, preferred_element_type=jnp.float32
    ) * head_dim ** (-0.5)
    causal = jnp.arange(row_total)[:, None] >= jnp.arange(row_total)[None, :]
    scores = jnp.where(causal[None, None], scores, mask_value)
    highest = jnp.max(scores, axis=-1)
    weights = jnp.exp(scores - highest[..., None])
    totals = jnp.sum(weights, axis=-1)
    mixture = jnp.einsum(
        "rhqk,rkhd->rqhd", weights.astype(jnp.bfloat16), values, preferred_element_type=jnp.float32
    )
    return (
        mixture / jnp.transpose(totals, (0, 2, 1))[..., None],
        jnp.transpose(highest + jnp.log(totals), (0, 2, 1)),
    )


def on_device(
    activations,
    w_query,
    w_key,
    w_value,
    w_out,
    norm_gain,
    key_cache,
    value_cache,
    parent,
    node_len,
    req_leaf,
):
    leaf_count = lax.axis_size("leaf")
    device = lax.axis_index("leaf")
    tok_rows = activations.shape[0]
    width_local = w_query.shape[1]
    heads_local = width_local // HD
    spread = leaf_count - TENANTS
    node_slots = 2 * ((REQ_DEV + spread - 1) // spread)
    all_slots = max(REQ_DEV // TENANTS, node_slots)
    block = REQ_LEN * width_local
    columns = lax.all_gather(activations, "mp", axis=1, tiled=True)
    query_f, key_f, value_f = tuple(
        (
            jnp.dot(columns, matrix, preferred_element_type=jnp.float32)
            for matrix in (w_query, w_key, w_value)
        )
    )
    middle_all = lookup(parent, req_leaf)
    root_all = lookup(parent, middle_all)
    len_of = lambda nodes: lookup(node_len, nodes)
    prefix = len_of(root_all) + len_of(middle_all) + len_of(req_leaf)
    mine_prefix = lax.dynamic_slice_in_dim(prefix, device * REQ_DEV, REQ_DEV)
    position = (mine_prefix[:, None] + jnp.arange(REQ_LEN, dtype=jnp.int32)[None, :]).reshape(
        tok_rows
    )
    queries = rotate(query_f.reshape(tok_rows, heads_local, HD), position).astype(jnp.bfloat16)
    keys = rotate(key_f.reshape(tok_rows, heads_local, HD), position).astype(jnp.bfloat16)
    values = value_f.astype(jnp.bfloat16)
    q_blocks = queries.reshape(REQ_DEV, block)
    self_out, self_lse = self_attention(
        queries.reshape(REQ_DEV, REQ_LEN, heads_local, HD),
        keys.reshape(REQ_DEV, REQ_LEN, heads_local, HD),
        values.reshape(REQ_DEV, REQ_LEN, heads_local, HD),
    )
    levels_all = jnp.stack([root_all, middle_all, req_leaf], axis=0).reshape(3, leaf_count, REQ_DEV)
    level_count = levels_all.shape[0]
    items = level_count * REQ_DEV
    per_sender = jnp.transpose(levels_all, (1, 0, 2)).reshape(leaf_count, items)
    holders = per_sender // NODE_DEV
    earlier = jnp.arange(items)[:, None] > jnp.arange(items)[None, :]
    ranks = jnp.sum(
        earlier[None] & (holders[:, :, None] == holders[:, None, :]), axis=2
    ).astype(jnp.int32)
    slot_ids = jnp.arange(all_slots, dtype=jnp.int32)
    my_holders = lax.dynamic_index_in_dim(holders, device, 0, keepdims=False)
    my_ranks = lax.dynamic_index_in_dim(ranks, device, 0, keepdims=False)
    send_hit = (
        (my_holders[None, None, :] == jnp.arange(leaf_count, dtype=jnp.int32)[:, None, None])
        & (my_ranks[None, None, :] == slot_ids[None, :, None])
    )
    send_item = jnp.sum(jnp.where(send_hit, jnp.arange(items, dtype=jnp.int32), 0), axis=2)
    send_valid = jnp.any(send_hit, axis=2)
    pick = (
        send_valid[:, :, None] & (send_item[:, :, None] % REQ_DEV == jnp.arange(REQ_DEV))
    ).reshape(leaf_count * all_slots, REQ_DEV)
    outgoing = (
        jnp.dot(pick.astype(jnp.bfloat16), q_blocks, preferred_element_type=jnp.float32)
        .astype(jnp.bfloat16)
        .reshape(leaf_count, all_slots, REQ_LEN, width_local)
    )
    arrived = lax.all_to_all(outgoing, "leaf", split_axis=0, concat_axis=0, tiled=True)
    recv_hit = (holders[:, None, :] == device) & (ranks[:, None, :] == slot_ids[None, :, None])
    slot_nodes = jnp.sum(jnp.where(recv_hit, per_sender[:, None, :], 0), axis=2).reshape(-1)
    filled = jnp.any(recv_hit, axis=2).reshape(-1)
    local_slot = jnp.where(filled, slot_nodes - device * NODE_DEV, 0)
    lengths = jnp.where(filled, len_of(slot_nodes), 0)
    node_out, node_lse = node_attention(
        arrived.reshape(leaf_count * all_slots, REQ_LEN, width_local),
        key_cache,
        value_cache,
        local_slot,
        lengths,
        heads_local,
    )
    flat_lse = node_lse.reshape(leaf_count * all_slots, REQ_LEN * heads_local)
    lse_high = lax.reduce_precision(flat_lse, exponent_bits=8, mantissa_bits=7)
    lse_low = flat_lse - lse_high
    lse_pair = jnp.stack([lse_high, lse_low], axis=1).astype(jnp.bfloat16)
    back_out = lax.all_to_all(
        node_out.reshape(leaf_count, all_slots, REQ_LEN, width_local),
        "leaf",
        split_axis=0,
        concat_axis=0,
        tiled=True,
    )
    back_lse = lax.all_to_all(
        lse_pair.reshape(leaf_count, all_slots, 2, REQ_LEN * heads_local),
        "leaf",
        split_axis=0,
        concat_axis=0,
        tiled=True,
    )
    take = (
        (my_holders * all_slots + my_ranks)[:, None]
        == jnp.arange(leaf_count * all_slots, dtype=jnp.int32)[None, :]
    ).astype(jnp.bfloat16)
    got_out = (
        jnp.dot(take, back_out.reshape(leaf_count * all_slots, block), preferred_element_type=jnp.float32)
        .reshape(level_count, REQ_DEV, REQ_LEN, heads_local, HD)
    )
    got_pair = jnp.dot(
        take,
        back_lse.reshape(leaf_count * all_slots, 2 * REQ_LEN * heads_local),
        preferred_element_type=jnp.float32,
    ).reshape(items, 2, REQ_LEN * heads_local)
    got_lse = (got_pair[:, 0] + got_pair[:, 1]).reshape(level_count, REQ_DEV, REQ_LEN, heads_local)
    partial_out = jnp.concatenate([got_out, self_out[None]], axis=0)
    partial_lse = jnp.concatenate([got_lse, self_lse[None]], axis=0)
    highest = jnp.max(partial_lse, axis=0)
    factor = jnp.exp(partial_lse - highest[None])
    merged = jnp.sum(factor[..., None] * partial_out, axis=0) / jnp.sum(factor, axis=0)[..., None]
    attn = merged.astype(jnp.bfloat16).reshape(tok_rows, width_local)
    partial_value = jnp.dot(attn, w_out, preferred_element_type=jnp.float32)
    projected = lax.psum_scatter(
        partial_value.astype(jnp.bfloat16), "mp", scatter_dimension=1, tiled=True
    ).astype(jnp.float32)
    squares = mp_sum(
        jnp.sum(projected * projected, axis=1).reshape(1, tok_rows), lax.axis_size("mp")
    ).reshape(tok_rows)
    row_scale = lax.rsqrt(squares / D + norm_eps)
    return (
        activations.astype(jnp.float32) + norm_gain[None, :] * projected * row_scale[:, None]
    ).astype(jnp.bfloat16)


def solution(mesh):
    in_specs = (
        P("leaf", "mp"),
        P(None, "mp"),
        P(None, "mp"),
        P(None, "mp"),
        P("mp", None),
        P("mp"),
        P("leaf", None, "mp"),
        P("leaf", None, "mp"),
        P(),
        P(),
        P(),
    )
    out_specs = P("leaf", "mp")
    return jax.shard_map(
        on_device, mesh=mesh, in_specs=in_specs, out_specs=out_specs, check_vma=False
    )
```

```python
import math

import jax
import jax.numpy as jnp
from jax import lax
from jax.experimental import pallas as pl
from jax.experimental.pallas import tpu as pltpu
from jax.sharding import PartitionSpec as P

D = 4096
HD = 128
TENANTS = 4
NODE_DEV = 8
REQ_LEN = 64
REQ_DEV = 4


rope_base = 500000.0
mask_value = -1e30
norm_eps = 1e-06


def rotate(values, positions):
    half_width = values.shape[-1] // 2
    inverse_freq = jnp.exp(
        jnp.arange(half_width, dtype=jnp.float32) * (-2.0 * math.log(rope_base) / values.shape[-1])
    )
    angles = positions.astype(jnp.float32)[:, None] * inverse_freq[None, :]
    cosine = jnp.cos(angles)[:, None, :]
    sine_part = jnp.sin(angles)[:, None, :]
    front_half = values[..., :half_width]
    back_half = values[..., half_width:]
    return jnp.concatenate(
        [front_half * cosine - back_half * sine_part, back_half * cosine + front_half * sine_part],
        axis=-1,
    )


def lookup(table, index):
    hit = index[..., None] == jnp.arange(table.shape[0], dtype=index.dtype)
    return jnp.sum(jnp.where(hit, table, 0), axis=-1).astype(table.dtype)


GROUP = 8


def attend(q, k, v, length, rows, cache_rows):
    live = lax.broadcasted_iota(jnp.int32, (rows, cache_rows), 1) < length
    s = lax.dot_general(
        q, k, (((1,), (1,)), ((), ())), preferred_element_type=jnp.float32
    ) * HD ** (-0.5)
    s = jnp.where(live, s, mask_value)
    m = jnp.max(s, axis=1, keepdims=True)
    p = jnp.exp(s - m)
    l = jnp.sum(p, axis=1, keepdims=True)
    o = jnp.dot(p.astype(jnp.bfloat16), v, preferred_element_type=jnp.float32)
    return o / l, m + jnp.log(l)


def node_kernel(
    slot_ref, len_ref, mode_ref, gnode_ref, glen_ref, q_ref, k_ref, v_ref, out_ref, lse_ref
):
    total_rows, width = q_ref.shape
    cache_rows = k_ref.shape[1]
    heads = width // HD
    groups = mode_ref.shape[0]
    span = GROUP * REQ_LEN

    def one_slot(i, carry):
        node = slot_ref[i]
        length = len_ref[i]
        rows = pl.ds(pl.multiple_of(i * REQ_LEN, REQ_LEN), REQ_LEN)

        @pl.when(length > 0)
        def _():
            for h in range(heads):
                cols = pl.ds(h * HD, HD)
                o, lse = attend(
                    q_ref[rows, cols], k_ref[node, :, cols], v_ref[node, :, cols],
                    length, REQ_LEN, cache_rows,
                )
                out_ref[rows, cols] = o.astype(out_ref.dtype)
                lse_ref[rows, pl.ds(h, 1)] = lse

        @pl.when(length == 0)
        def _():
            out_ref[rows, :] = jnp.zeros((REQ_LEN, width), out_ref.dtype)
            lse_ref[rows, :] = jnp.zeros((REQ_LEN, heads), lse_ref.dtype)

        return carry

    def one_group(g, carry):
        mode = mode_ref[g]
        rows = pl.ds(pl.multiple_of(g * span, span), span)

        @pl.when(mode == 0)
        def _():
            out_ref[rows, :] = jnp.zeros((span, width), out_ref.dtype)
            lse_ref[rows, :] = jnp.zeros((span, heads), lse_ref.dtype)

        @pl.when(mode == 1)
        def _():
            node = gnode_ref[g]
            length = glen_ref[g]
            for h in range(heads):
                cols = pl.ds(h * HD, HD)
                o, lse = attend(
                    q_ref[rows, cols], k_ref[node, :, cols], v_ref[node, :, cols],
                    length, span, cache_rows,
                )
                out_ref[rows, cols] = o.astype(out_ref.dtype)
                lse_ref[rows, pl.ds(h, 1)] = lse

        @pl.when(mode == 2)
        def _():
            lax.fori_loop(g * GROUP, (g + 1) * GROUP, one_slot, 0)

        return carry

    lax.fori_loop(0, groups, one_group, 0)


def node_attention(queries, key_cache, value_cache, local_slot, lengths, heads_local):
    slots, rows, width = queries.shape
    nodes, cache_rows, _ = key_cache.shape
    groups = slots // GROUP
    live = (lengths > 0).reshape(groups, GROUP)
    grouped_node = local_slot.reshape(groups, GROUP)
    grouped_len = lengths.reshape(groups, GROUP)
    group_node = jnp.max(jnp.where(live, grouped_node, 0), axis=1)
    group_len = jnp.max(grouped_len, axis=1)
    uniform = jnp.all(~live | (grouped_node == group_node[:, None]), axis=1)
    mode = jnp.where(jnp.any(live, axis=1), jnp.where(uniform, 1, 2), 0).astype(jnp.int32)
    vmem = pl.BlockSpec(memory_space=pltpu.VMEM)
    smem = pl.BlockSpec(memory_space=pltpu.SMEM)
    flops = 4 * slots * rows * cache_rows * width
    out, lse = pl.pallas_call(
        node_kernel,
        out_shape=(
            jax.ShapeDtypeStruct((slots * rows, width), jnp.bfloat16),
            jax.ShapeDtypeStruct((slots * rows, heads_local), jnp.float32),
        ),
        in_specs=[smem] * 5 + [vmem] * 3,
        out_specs=(vmem, vmem),
        cost_estimate=pl.CostEstimate(
            flops=flops,
            transcendentals=slots * rows * cache_rows * heads_local,
            bytes_accessed=2 * queries.size * 2 + 2 * key_cache.size * 2,
        ),
    )(
        local_slot, lengths, mode, group_node, group_len,
        queries.reshape(slots * rows, width), key_cache, value_cache,
    )
    return out.reshape(slots, rows, width), lse.reshape(slots, rows, heads_local)


def sum_kernel(x_ref, out_ref, recv, send_sem, recv_sem):
    n = recv.shape[0]
    me = lax.axis_index("mp")
    barrier = pltpu.get_barrier_semaphore()
    for d in range(1, n):
        pl.semaphore_signal(
            barrier, inc=1, device_id={"mp": lax.rem(me + d, n)},
            device_id_type=pl.DeviceIdType.MESH,
        )
    pl.semaphore_wait(barrier, n - 1)
    copies = []
    for d in range(1, n):
        copy = pltpu.make_async_remote_copy(
            src_ref=x_ref,
            dst_ref=recv.at[d],
            send_sem=send_sem.at[d],
            recv_sem=recv_sem.at[d],
            device_id={"mp": lax.rem(me + d, n)},
            device_id_type=pl.DeviceIdType.MESH,
        )
        copy.start()
        copies.append(copy)
    for copy in copies:
        copy.wait()
    total = x_ref[...]
    for d in range(1, n):
        total = total + recv[d]
    out_ref[...] = total


def mp_sum(x, n):
    vmem = pl.BlockSpec(memory_space=pltpu.VMEM)
    return pl.pallas_call(
        sum_kernel,
        out_shape=jax.ShapeDtypeStruct(x.shape, x.dtype),
        in_specs=[vmem],
        out_specs=vmem,
        scratch_shapes=[
            pltpu.VMEM((n,) + x.shape, x.dtype),
            pltpu.SemaphoreType.DMA((n,)),
            pltpu.SemaphoreType.DMA((n,)),
        ],
        compiler_params=pltpu.CompilerParams(collective_id=0, has_side_effects=True),
    )(x)


def self_attention(queries, keys, values):
    head_dim = queries.shape[-1]
    row_total = queries.shape[1]
    scores = jnp.einsum(
        "rqhd,rkhd->rhqk", queries, keys, preferred_element_type=jnp.float32
    ) * head_dim ** (-0.5)
    causal = jnp.arange(row_total)[:, None] >= jnp.arange(row_total)[None, :]
    scores = jnp.where(causal[None, None], scores, mask_value)
    highest = jnp.max(scores, axis=-1)
    weights = jnp.exp(scores - highest[..., None])
    totals = jnp.sum(weights, axis=-1)
    mixture = jnp.einsum(
        "rhqk,rkhd->rqhd", weights.astype(jnp.bfloat16), values, preferred_element_type=jnp.float32
    )
    return (
        mixture / jnp.transpose(totals, (0, 2, 1))[..., None],
        jnp.transpose(highest + jnp.log(totals), (0, 2, 1)),
    )


def self_part(q_ref, k_ref, v_ref, out_ref, lse_ref):
    tokens, width = q_ref.shape
    heads = width // HD
    causal = (
        lax.broadcasted_iota(jnp.int32, (REQ_LEN, REQ_LEN), 0)
        >= lax.broadcasted_iota(jnp.int32, (REQ_LEN, REQ_LEN), 1)
    )
    for r in range(tokens // REQ_LEN):
        rows = pl.ds(r * REQ_LEN, REQ_LEN)
        for h in range(heads):
            cols = pl.ds(h * HD, HD)
            s = lax.dot_general(
                q_ref[rows, cols], k_ref[rows, cols], (((1,), (1,)), ((), ())),
                preferred_element_type=jnp.float32,
            ) * HD ** (-0.5)
            s = jnp.where(causal, s, mask_value)
            m = jnp.max(s, axis=1, keepdims=True)
            p = jnp.exp(s - m)
            l = jnp.sum(p, axis=1, keepdims=True)
            o = jnp.dot(p.astype(jnp.bfloat16), v_ref[rows, cols], preferred_element_type=jnp.float32)
            out_ref[rows, cols] = o / l
            lse_ref[rows, pl.ds(h, 1)] = m + jnp.log(l)


def back_kernel(
    out_in, lse_in, q_ref, k_ref, v_ref,
    out_back, lse_back, self_out, self_lse,
    recv_out, recv_lse, send_sems, recv_sems, lse_send_sems, lse_recv_sems,
):
    n = recv_out.shape[0]
    me = lax.axis_index("leaf")
    mesh_ids = pl.DeviceIdType.MESH
    barrier = pltpu.get_barrier_semaphore()

    def greet(d, carry):
        pl.semaphore_signal(barrier, inc=1, device_id={"leaf": lax.rem(me + d, n)}, device_id_type=mesh_ids)
        return carry

    lax.fori_loop(1, n, greet, 0)
    pl.semaphore_wait(barrier, n - 1)

    def out_copy(d, peer):
        return pltpu.make_async_remote_copy(
            src_ref=out_in.at[peer], dst_ref=recv_out.at[me],
            send_sem=send_sems.at[d], recv_sem=recv_sems.at[d],
            device_id={"leaf": peer}, device_id_type=mesh_ids,
        )

    def lse_copy(d, peer):
        return pltpu.make_async_remote_copy(
            src_ref=lse_in.at[peer], dst_ref=recv_lse.at[me],
            send_sem=lse_send_sems.at[d], recv_sem=lse_recv_sems.at[d],
            device_id={"leaf": peer}, device_id_type=mesh_ids,
        )

    def send(d, carry):
        peer = lax.rem(me + d, n)
        out_copy(d, peer).start()
        lse_copy(d, peer).start()
        return carry

    lax.fori_loop(1, n, send, 0)
    recv_out[me] = out_in[me]
    recv_lse[me] = lse_in[me]
    self_part(q_ref, k_ref, v_ref, self_out, self_lse)

    def finish(d, carry):
        peer = lax.rem(me + d, n)
        out_copy(d, peer).wait_send()
        lse_copy(d, peer).wait_send()
        sender = lax.rem(me + n - d, n)
        pltpu.make_async_remote_copy(
            src_ref=out_in.at[sender], dst_ref=recv_out.at[sender],
            send_sem=send_sems.at[d], recv_sem=recv_sems.at[d],
            device_id={"leaf": sender}, device_id_type=mesh_ids,
        ).wait_recv()
        pltpu.make_async_remote_copy(
            src_ref=lse_in.at[sender], dst_ref=recv_lse.at[sender],
            send_sem=lse_send_sems.at[d], recv_sem=lse_recv_sems.at[d],
            device_id={"leaf": sender}, device_id_type=mesh_ids,
        ).wait_recv()
        return carry

    lax.fori_loop(1, n, finish, 0)
    out_back[...] = recv_out[...]
    lse_back[...] = recv_lse[...]


def back_exchange(out_payload, lse_payload, q_self, k_self, v_self, heads_local):
    n = out_payload.shape[0]
    tokens, width = q_self.shape
    vmem = pl.BlockSpec(memory_space=pltpu.VMEM)
    return pl.pallas_call(
        back_kernel,
        out_shape=(
            jax.ShapeDtypeStruct(out_payload.shape, out_payload.dtype),
            jax.ShapeDtypeStruct(lse_payload.shape, lse_payload.dtype),
            jax.ShapeDtypeStruct((tokens, width), jnp.float32),
            jax.ShapeDtypeStruct((tokens, heads_local), jnp.float32),
        ),
        in_specs=[vmem] * 5,
        out_specs=(vmem,) * 4,
        scratch_shapes=[
            pltpu.VMEM(out_payload.shape, out_payload.dtype),
            pltpu.VMEM(lse_payload.shape, lse_payload.dtype),
            pltpu.SemaphoreType.DMA((n,)),
            pltpu.SemaphoreType.DMA((n,)),
            pltpu.SemaphoreType.DMA((n,)),
            pltpu.SemaphoreType.DMA((n,)),
        ],
        compiler_params=pltpu.CompilerParams(collective_id=1, has_side_effects=True),
    )(out_payload, lse_payload, q_self, k_self, v_self)


def on_device(
    activations,
    w_query,
    w_key,
    w_value,
    w_out,
    norm_gain,
    key_cache,
    value_cache,
    parent,
    node_len,
    req_leaf,
):
    leaf_count = lax.axis_size("leaf")
    device = lax.axis_index("leaf")
    tok_rows = activations.shape[0]
    width_local = w_query.shape[1]
    heads_local = width_local // HD
    spread = leaf_count - TENANTS
    node_slots = 2 * ((REQ_DEV + spread - 1) // spread)
    all_slots = max(REQ_DEV // TENANTS, node_slots)
    block = REQ_LEN * width_local
    columns = lax.all_gather(activations, "mp", axis=1, tiled=True)
    query_f, key_f, value_f = tuple(
        (
            jnp.dot(columns, matrix, preferred_element_type=jnp.float32)
            for matrix in (w_query, w_key, w_value)
        )
    )
    middle_all = lookup(parent, req_leaf)
    root_all = lookup(parent, middle_all)
    len_of = lambda nodes: lookup(node_len, nodes)
    prefix = len_of(root_all) + len_of(middle_all) + len_of(req_leaf)
    mine_prefix = lax.dynamic_slice_in_dim(prefix, device * REQ_DEV, REQ_DEV)
    position = (mine_prefix[:, None] + jnp.arange(REQ_LEN, dtype=jnp.int32)[None, :]).reshape(
        tok_rows
    )
    queries = rotate(query_f.reshape(tok_rows, heads_local, HD), position).astype(jnp.bfloat16)
    keys = rotate(key_f.reshape(tok_rows, heads_local, HD), position).astype(jnp.bfloat16)
    values = value_f.astype(jnp.bfloat16)
    q_blocks = queries.reshape(REQ_DEV, block)
    levels_all = jnp.stack([root_all, middle_all, req_leaf], axis=0).reshape(3, leaf_count, REQ_DEV)
    level_count = levels_all.shape[0]
    items = level_count * REQ_DEV
    per_sender = jnp.transpose(levels_all, (1, 0, 2)).reshape(leaf_count, items)
    holders = per_sender // NODE_DEV
    earlier = jnp.arange(items)[:, None] > jnp.arange(items)[None, :]
    ranks = jnp.sum(
        earlier[None] & (holders[:, :, None] == holders[:, None, :]), axis=2
    ).astype(jnp.int32)
    slot_ids = jnp.arange(all_slots, dtype=jnp.int32)
    my_holders = lax.dynamic_index_in_dim(holders, device, 0, keepdims=False)
    my_ranks = lax.dynamic_index_in_dim(ranks, device, 0, keepdims=False)
    send_hit = (
        (my_holders[None, None, :] == jnp.arange(leaf_count, dtype=jnp.int32)[:, None, None])
        & (my_ranks[None, None, :] == slot_ids[None, :, None])
    )
    send_item = jnp.sum(jnp.where(send_hit, jnp.arange(items, dtype=jnp.int32), 0), axis=2)
    send_valid = jnp.any(send_hit, axis=2)
    pick = (
        send_valid[:, :, None] & (send_item[:, :, None] % REQ_DEV == jnp.arange(REQ_DEV))
    ).reshape(leaf_count * all_slots, REQ_DEV)
    outgoing = (
        jnp.dot(pick.astype(jnp.bfloat16), q_blocks, preferred_element_type=jnp.float32)
        .astype(jnp.bfloat16)
        .reshape(leaf_count, all_slots, REQ_LEN, width_local)
    )
    arrived = lax.all_to_all(outgoing, "leaf", split_axis=0, concat_axis=0, tiled=True)
    recv_hit = (holders[:, None, :] == device) & (ranks[:, None, :] == slot_ids[None, :, None])
    slot_nodes = jnp.sum(jnp.where(recv_hit, per_sender[:, None, :], 0), axis=2).reshape(-1)
    filled = jnp.any(recv_hit, axis=2).reshape(-1)
    local_slot = jnp.where(filled, slot_nodes - device * NODE_DEV, 0)
    lengths = jnp.where(filled, len_of(slot_nodes), 0)
    node_out, node_lse = node_attention(
        arrived.reshape(leaf_count * all_slots, REQ_LEN, width_local),
        key_cache,
        value_cache,
        local_slot,
        lengths,
        heads_local,
    )
    lse_rows = 8
    lse_payload = jnp.pad(
        node_lse.reshape(leaf_count, all_slots * REQ_LEN * heads_local // 128, 128),
        ((0, 0), (0, lse_rows - all_slots * REQ_LEN * heads_local // 128), (0, 0)),
    )
    back_out, back_lse, self_out, self_lse = back_exchange(
        node_out.reshape(leaf_count, all_slots * REQ_LEN, width_local),
        lse_payload,
        queries.reshape(tok_rows, width_local),
        keys.reshape(tok_rows, width_local),
        values.reshape(tok_rows, width_local),
        heads_local,
    )
    self_out = self_out.reshape(REQ_DEV, REQ_LEN, heads_local, HD)
    self_lse = self_lse.reshape(REQ_DEV, REQ_LEN, heads_local)
    take = (
        (my_holders * all_slots + my_ranks)[:, None]
        == jnp.arange(leaf_count * all_slots, dtype=jnp.int32)[None, :]
    ).astype(jnp.bfloat16)
    got_out = (
        jnp.dot(take, back_out.reshape(leaf_count * all_slots, block), preferred_element_type=jnp.float32)
        .reshape(level_count, REQ_DEV, REQ_LEN, heads_local, HD)
    )
    slot_lse = back_lse[:, : all_slots * REQ_LEN * heads_local // 128].reshape(
        leaf_count * all_slots, REQ_LEN * heads_local
    )
    got_lse = jnp.dot(
        take.astype(jnp.float32), slot_lse, precision=lax.Precision.HIGHEST,
        preferred_element_type=jnp.float32,
    ).reshape(level_count, REQ_DEV, REQ_LEN, heads_local)
    partial_out = jnp.concatenate([got_out, self_out[None]], axis=0)
    partial_lse = jnp.concatenate([got_lse, self_lse[None]], axis=0)
    highest = jnp.max(partial_lse, axis=0)
    factor = jnp.exp(partial_lse - highest[None])
    merged = jnp.sum(factor[..., None] * partial_out, axis=0) / jnp.sum(factor, axis=0)[..., None]
    attn = merged.astype(jnp.bfloat16).reshape(tok_rows, width_local)
    partial_value = jnp.dot(attn, w_out, preferred_element_type=jnp.float32)
    projected = lax.psum_scatter(
        partial_value.astype(jnp.bfloat16), "mp", scatter_dimension=1, tiled=True
    ).astype(jnp.float32)
    squares = mp_sum(
        jnp.sum(projected * projected, axis=1).reshape(1, tok_rows), lax.axis_size("mp")
    ).reshape(tok_rows)
    row_scale = lax.rsqrt(squares / D + norm_eps)
    return (
        activations.astype(jnp.float32) + norm_gain[None, :] * projected * row_scale[:, None]
    ).astype(jnp.bfloat16)


def solution(mesh):
    in_specs = (
        P("leaf", "mp"),
        P(None, "mp"),
        P(None, "mp"),
        P(None, "mp"),
        P("mp", None),
        P("mp"),
        P("leaf", None, "mp"),
        P("leaf", None, "mp"),
        P(),
        P(),
        P(),
    )
    out_specs = P("leaf", "mp")
    return jax.shard_map(
        on_device, mesh=mesh, in_specs=in_specs, out_specs=out_specs, check_vma=False
    )
```

```python
import math

import jax
import jax.numpy as jnp
from jax import lax
from jax.experimental import pallas as pl
from jax.experimental.pallas import tpu as pltpu
from jax.sharding import PartitionSpec as P

D = 4096
HD = 128
TENANTS = 4
NODE_DEV = 8
REQ_LEN = 64
REQ_DEV = 4


rope_base = 500000.0
mask_value = -1e30
norm_eps = 1e-06


def rotate(values, positions):
    half_width = values.shape[-1] // 2
    inverse_freq = jnp.exp(
        jnp.arange(half_width, dtype=jnp.float32) * (-2.0 * math.log(rope_base) / values.shape[-1])
    )
    angles = positions.astype(jnp.float32)[:, None] * inverse_freq[None, :]
    cosine = jnp.cos(angles)[:, None, :]
    sine_part = jnp.sin(angles)[:, None, :]
    front_half = values[..., :half_width]
    back_half = values[..., half_width:]
    return jnp.concatenate(
        [front_half * cosine - back_half * sine_part, back_half * cosine + front_half * sine_part],
        axis=-1,
    )


def lookup(table, index):
    hit = index[..., None] == jnp.arange(table.shape[0], dtype=index.dtype)
    return jnp.sum(jnp.where(hit, table, 0), axis=-1).astype(table.dtype)


GROUP = 8


def attend(q, k, v, length, rows, cache_rows):
    live = lax.broadcasted_iota(jnp.int32, (rows, cache_rows), 1) < length
    s = lax.dot_general(
        q, k, (((1,), (1,)), ((), ())), preferred_element_type=jnp.float32
    ) * HD ** (-0.5)
    s = jnp.where(live, s, mask_value)
    m = jnp.max(s, axis=1, keepdims=True)
    p = jnp.exp(s - m)
    l = jnp.sum(p, axis=1, keepdims=True)
    o = jnp.dot(p.astype(jnp.bfloat16), v, preferred_element_type=jnp.float32)
    return o / l, m + jnp.log(l)


def node_kernel(
    slot_ref, len_ref, mode_ref, gnode_ref, glen_ref, q_ref, k_ref, v_ref, out_ref, lse_ref
):
    total_rows, width = q_ref.shape
    cache_rows = k_ref.shape[1]
    heads = width // HD
    groups = mode_ref.shape[0]
    span = GROUP * REQ_LEN

    def one_slot(i, carry):
        node = slot_ref[i]
        length = len_ref[i]
        rows = pl.ds(pl.multiple_of(i * REQ_LEN, REQ_LEN), REQ_LEN)

        @pl.when(length > 0)
        def _():
            for h in range(heads):
                cols = pl.ds(h * HD, HD)
                o, lse = attend(
                    q_ref[rows, cols], k_ref[node, :, cols], v_ref[node, :, cols],
                    length, REQ_LEN, cache_rows,
                )
                out_ref[rows, cols] = o.astype(out_ref.dtype)
                lse_ref[rows, pl.ds(h, 1)] = lse

        @pl.when(length == 0)
        def _():
            out_ref[rows, :] = jnp.zeros((REQ_LEN, width), out_ref.dtype)
            lse_ref[rows, :] = jnp.zeros((REQ_LEN, heads), lse_ref.dtype)

        return carry

    def one_group(g, carry):
        mode = mode_ref[g]
        rows = pl.ds(pl.multiple_of(g * span, span), span)

        @pl.when(mode == 0)
        def _():
            out_ref[rows, :] = jnp.zeros((span, width), out_ref.dtype)
            lse_ref[rows, :] = jnp.zeros((span, heads), lse_ref.dtype)

        @pl.when(mode == 1)
        def _():
            node = gnode_ref[g]
            length = glen_ref[g]
            for h in range(heads):
                cols = pl.ds(h * HD, HD)
                o, lse = attend(
                    q_ref[rows, cols], k_ref[node, :, cols], v_ref[node, :, cols],
                    length, span, cache_rows,
                )
                out_ref[rows, cols] = o.astype(out_ref.dtype)
                lse_ref[rows, pl.ds(h, 1)] = lse

        @pl.when(mode == 2)
        def _():
            lax.fori_loop(g * GROUP, (g + 1) * GROUP, one_slot, 0)

        return carry

    lax.fori_loop(0, groups, one_group, 0)


def node_attention(queries, key_cache, value_cache, local_slot, lengths, heads_local):
    slots, rows, width = queries.shape
    nodes, cache_rows, _ = key_cache.shape
    groups = slots // GROUP
    live = (lengths > 0).reshape(groups, GROUP)
    grouped_node = local_slot.reshape(groups, GROUP)
    grouped_len = lengths.reshape(groups, GROUP)
    group_node = jnp.max(jnp.where(live, grouped_node, 0), axis=1)
    group_len = jnp.max(grouped_len, axis=1)
    uniform = jnp.all(~live | (grouped_node == group_node[:, None]), axis=1)
    mode = jnp.where(jnp.any(live, axis=1), jnp.where(uniform, 1, 2), 0).astype(jnp.int32)
    vmem = pl.BlockSpec(memory_space=pltpu.VMEM)
    smem = pl.BlockSpec(memory_space=pltpu.SMEM)
    flops = 4 * slots * rows * cache_rows * width
    out, lse = pl.pallas_call(
        node_kernel,
        out_shape=(
            jax.ShapeDtypeStruct((slots * rows, width), jnp.bfloat16),
            jax.ShapeDtypeStruct((slots * rows, heads_local), jnp.float32),
        ),
        in_specs=[smem] * 5 + [vmem] * 3,
        out_specs=(vmem, vmem),
        cost_estimate=pl.CostEstimate(
            flops=flops,
            transcendentals=slots * rows * cache_rows * heads_local,
            bytes_accessed=2 * queries.size * 2 + 2 * key_cache.size * 2,
        ),
    )(
        local_slot, lengths, mode, group_node, group_len,
        queries.reshape(slots * rows, width), key_cache, value_cache,
    )
    return out.reshape(slots, rows, width), lse.reshape(slots, rows, heads_local)


def sum_kernel(x_ref, out_ref, recv, send_sem, recv_sem):
    n = recv.shape[0]
    me = lax.axis_index("mp")
    barrier = pltpu.get_barrier_semaphore()
    for d in range(1, n):
        pl.semaphore_signal(
            barrier, inc=1, device_id={"mp": lax.rem(me + d, n)},
            device_id_type=pl.DeviceIdType.MESH,
        )
    pl.semaphore_wait(barrier, n - 1)
    copies = []
    for d in range(1, n):
        copy = pltpu.make_async_remote_copy(
            src_ref=x_ref,
            dst_ref=recv.at[d],
            send_sem=send_sem.at[d],
            recv_sem=recv_sem.at[d],
            device_id={"mp": lax.rem(me + d, n)},
            device_id_type=pl.DeviceIdType.MESH,
        )
        copy.start()
        copies.append(copy)
    for copy in copies:
        copy.wait()
    total = x_ref[...]
    for d in range(1, n):
        total = total + recv[d]
    out_ref[...] = total


def mp_sum(x, n):
    vmem = pl.BlockSpec(memory_space=pltpu.VMEM)
    return pl.pallas_call(
        sum_kernel,
        out_shape=jax.ShapeDtypeStruct(x.shape, x.dtype),
        in_specs=[vmem],
        out_specs=vmem,
        scratch_shapes=[
            pltpu.VMEM((n,) + x.shape, x.dtype),
            pltpu.SemaphoreType.DMA((n,)),
            pltpu.SemaphoreType.DMA((n,)),
        ],
        compiler_params=pltpu.CompilerParams(collective_id=0, has_side_effects=True),
    )(x)


def self_attention(queries, keys, values):
    head_dim = queries.shape[-1]
    row_total = queries.shape[1]
    scores = jnp.einsum(
        "rqhd,rkhd->rhqk", queries, keys, preferred_element_type=jnp.float32
    ) * head_dim ** (-0.5)
    causal = jnp.arange(row_total)[:, None] >= jnp.arange(row_total)[None, :]
    scores = jnp.where(causal[None, None], scores, mask_value)
    highest = jnp.max(scores, axis=-1)
    weights = jnp.exp(scores - highest[..., None])
    totals = jnp.sum(weights, axis=-1)
    mixture = jnp.einsum(
        "rhqk,rkhd->rqhd", weights.astype(jnp.bfloat16), values, preferred_element_type=jnp.float32
    )
    return (
        mixture / jnp.transpose(totals, (0, 2, 1))[..., None],
        jnp.transpose(highest + jnp.log(totals), (0, 2, 1)),
    )


def on_device(
    activations,
    w_query,
    w_key,
    w_value,
    w_out,
    norm_gain,
    key_cache,
    value_cache,
    parent,
    node_len,
    req_leaf,
):
    leaf_count = lax.axis_size("leaf")
    device = lax.axis_index("leaf")
    tok_rows = activations.shape[0]
    width_local = w_query.shape[1]
    heads_local = width_local // HD
    spread = leaf_count - TENANTS
    node_slots = 2 * ((REQ_DEV + spread - 1) // spread)
    all_slots = max(REQ_DEV // TENANTS, node_slots)
    block = REQ_LEN * width_local
    columns = lax.all_gather(activations, "mp", axis=1, tiled=True)
    query_f, key_f, value_f = tuple(
        (
            jnp.dot(columns, matrix, preferred_element_type=jnp.float32)
            for matrix in (w_query, w_key, w_value)
        )
    )
    middle_all = lookup(parent, req_leaf)
    root_all = lookup(parent, middle_all)
    len_of = lambda nodes: lookup(node_len, nodes)
    prefix = len_of(root_all) + len_of(middle_all) + len_of(req_leaf)
    mine_prefix = lax.dynamic_slice_in_dim(prefix, device * REQ_DEV, REQ_DEV)
    position = (mine_prefix[:, None] + jnp.arange(REQ_LEN, dtype=jnp.int32)[None, :]).reshape(
        tok_rows
    )
    queries = rotate(query_f.reshape(tok_rows, heads_local, HD), position).astype(jnp.bfloat16)
    keys = rotate(key_f.reshape(tok_rows, heads_local, HD), position).astype(jnp.bfloat16)
    values = value_f.astype(jnp.bfloat16)
    q_blocks = queries.reshape(REQ_DEV, block)
    self_out, self_lse = self_attention(
        queries.reshape(REQ_DEV, REQ_LEN, heads_local, HD),
        keys.reshape(REQ_DEV, REQ_LEN, heads_local, HD),
        values.reshape(REQ_DEV, REQ_LEN, heads_local, HD),
    )
    levels_all = jnp.stack([root_all, middle_all, req_leaf], axis=0).reshape(3, leaf_count, REQ_DEV)
    level_count = levels_all.shape[0]
    items = level_count * REQ_DEV
    per_sender = jnp.transpose(levels_all, (1, 0, 2)).reshape(leaf_count, items)
    holders = per_sender // NODE_DEV
    earlier = jnp.arange(items)[:, None] > jnp.arange(items)[None, :]
    ranks = jnp.sum(
        earlier[None] & (holders[:, :, None] == holders[:, None, :]), axis=2
    ).astype(jnp.int32)
    slot_ids = jnp.arange(all_slots, dtype=jnp.int32)
    my_holders = lax.dynamic_index_in_dim(holders, device, 0, keepdims=False)
    my_ranks = lax.dynamic_index_in_dim(ranks, device, 0, keepdims=False)
    send_hit = (
        (my_holders[None, None, :] == jnp.arange(leaf_count, dtype=jnp.int32)[:, None, None])
        & (my_ranks[None, None, :] == slot_ids[None, :, None])
    )
    send_item = jnp.sum(jnp.where(send_hit, jnp.arange(items, dtype=jnp.int32), 0), axis=2)
    send_valid = jnp.any(send_hit, axis=2)
    pick = (
        send_valid[:, :, None] & (send_item[:, :, None] % REQ_DEV == jnp.arange(REQ_DEV))
    ).reshape(leaf_count * all_slots, REQ_DEV)
    outgoing = (
        jnp.dot(pick.astype(jnp.bfloat16), q_blocks, preferred_element_type=jnp.float32)
        .astype(jnp.bfloat16)
        .reshape(leaf_count, all_slots, REQ_LEN, width_local)
    )
    arrived = lax.all_to_all(outgoing, "leaf", split_axis=0, concat_axis=0, tiled=True)
    recv_hit = (holders[:, None, :] == device) & (ranks[:, None, :] == slot_ids[None, :, None])
    slot_nodes = jnp.sum(jnp.where(recv_hit, per_sender[:, None, :], 0), axis=2).reshape(-1)
    filled = jnp.any(recv_hit, axis=2).reshape(-1)
    local_slot = jnp.where(filled, slot_nodes - device * NODE_DEV, 0)
    lengths = jnp.where(filled, len_of(slot_nodes), 0)
    node_out, node_lse = node_attention(
        arrived.reshape(leaf_count * all_slots, REQ_LEN, width_local),
        key_cache,
        value_cache,
        local_slot,
        lengths,
        heads_local,
    )
    flat_lse = node_lse.reshape(leaf_count * all_slots, REQ_LEN * heads_local)
    lse_high = lax.reduce_precision(flat_lse, exponent_bits=8, mantissa_bits=7)
    lse_low = flat_lse - lse_high
    lse_pair = jnp.stack([lse_high, lse_low], axis=1).astype(jnp.bfloat16)
    back_out = lax.all_to_all(
        node_out.reshape(leaf_count, all_slots, REQ_LEN, width_local),
        "leaf",
        split_axis=0,
        concat_axis=0,
        tiled=True,
    )
    back_lse = lax.all_to_all(
        lse_pair.reshape(leaf_count, all_slots, 2, REQ_LEN * heads_local),
        "leaf",
        split_axis=0,
        concat_axis=0,
        tiled=True,
    )
    take = (
        (my_holders * all_slots + my_ranks)[:, None]
        == jnp.arange(leaf_count * all_slots, dtype=jnp.int32)[None, :]
    ).astype(jnp.bfloat16)
    chosen = my_holders * all_slots + my_ranks
    got_out = jnp.take(
        back_out.reshape(leaf_count * all_slots, REQ_LEN, width_local), chosen, axis=0
    ).astype(jnp.float32).reshape(level_count, REQ_DEV, REQ_LEN, heads_local, HD)
    got_pair = jnp.dot(
        take,
        back_lse.reshape(leaf_count * all_slots, 2 * REQ_LEN * heads_local),
        preferred_element_type=jnp.float32,
    ).reshape(items, 2, REQ_LEN * heads_local)
    got_lse = (got_pair[:, 0] + got_pair[:, 1]).reshape(level_count, REQ_DEV, REQ_LEN, heads_local)
    partial_out = jnp.concatenate([got_out, self_out[None]], axis=0)
    partial_lse = jnp.concatenate([got_lse, self_lse[None]], axis=0)
    highest = jnp.max(partial_lse, axis=0)
    factor = jnp.exp(partial_lse - highest[None])
    merged = jnp.sum(factor[..., None] * partial_out, axis=0) / jnp.sum(factor, axis=0)[..., None]
    attn = merged.astype(jnp.bfloat16).reshape(tok_rows, width_local)
    partial_value = jnp.dot(attn, w_out, preferred_element_type=jnp.float32)
    projected = lax.psum_scatter(
        partial_value.astype(jnp.bfloat16), "mp", scatter_dimension=1, tiled=True
    ).astype(jnp.float32)
    squares = mp_sum(
        jnp.sum(projected * projected, axis=1).reshape(1, tok_rows), lax.axis_size("mp")
    ).reshape(tok_rows)
    row_scale = lax.rsqrt(squares / D + norm_eps)
    return (
        activations.astype(jnp.float32) + norm_gain[None, :] * projected * row_scale[:, None]
    ).astype(jnp.bfloat16)


def solution(mesh):
    in_specs = (
        P("leaf", "mp"),
        P(None, "mp"),
        P(None, "mp"),
        P(None, "mp"),
        P("mp", None),
        P("mp"),
        P("leaf", None, "mp"),
        P("leaf", None, "mp"),
        P(),
        P(),
        P(),
    )
    out_specs = P("leaf", "mp")
    return jax.shard_map(
        on_device, mesh=mesh, in_specs=in_specs, out_specs=out_specs, check_vma=False
    )
```

```python
import math

import jax
import jax.numpy as jnp
from jax import lax
from jax.experimental import pallas as pl
from jax.experimental.pallas import tpu as pltpu
from jax.sharding import PartitionSpec as P

D = 4096
HD = 128
TENANTS = 4
NODE_DEV = 8
REQ_LEN = 64
REQ_DEV = 4


rope_base = 500000.0
mask_value = -1e30
norm_eps = 1e-06


def rotate(values, positions):
    half_width = values.shape[-1] // 2
    inverse_freq = jnp.exp(
        jnp.arange(half_width, dtype=jnp.float32) * (-2.0 * math.log(rope_base) / values.shape[-1])
    )
    angles = positions.astype(jnp.float32)[:, None] * inverse_freq[None, :]
    cosine = jnp.cos(angles)[:, None, :]
    sine_part = jnp.sin(angles)[:, None, :]
    front_half = values[..., :half_width]
    back_half = values[..., half_width:]
    return jnp.concatenate(
        [front_half * cosine - back_half * sine_part, back_half * cosine + front_half * sine_part],
        axis=-1,
    )


def lookup(table, index):
    hit = index[..., None] == jnp.arange(table.shape[0], dtype=index.dtype)
    return jnp.sum(jnp.where(hit, table, 0), axis=-1).astype(table.dtype)


GROUP = 8
PAD_ROWS = 80


def attend(q, k, v, length, rows, cache_rows):
    live = lax.broadcasted_iota(jnp.int32, (rows, cache_rows), 1) < length
    s = lax.dot_general(
        q, k, (((1,), (1,)), ((), ())), preferred_element_type=jnp.float32
    ) * HD ** (-0.5)
    s = jnp.where(live, s, mask_value)
    m = jnp.max(s, axis=1, keepdims=True)
    p = jnp.exp(s - m)
    l = jnp.sum(p, axis=1, keepdims=True)
    o = jnp.dot(p.astype(jnp.bfloat16), v, preferred_element_type=jnp.float32)
    return o / l, m + jnp.log(l)


def node_kernel(
    slot_ref, len_ref, mode_ref, gnode_ref, glen_ref, q_ref, k_ref, v_ref, out_ref, lse_ref
):
    total_rows, width = q_ref.shape
    cache_rows = k_ref.shape[1]
    out_rows = out_ref.shape[1]
    heads = width // HD
    groups = mode_ref.shape[0]
    span = GROUP * REQ_LEN

    def one_slot(i, carry):
        node = slot_ref[i]
        length = len_ref[i]
        rows = pl.ds(pl.multiple_of(i * REQ_LEN, REQ_LEN), REQ_LEN)

        @pl.when(length > 0)
        def _():
            for h in range(heads):
                cols = pl.ds(h * HD, HD)
                o, lse = attend(
                    q_ref[rows, cols], k_ref[node, :, cols], v_ref[node, :, cols],
                    length, REQ_LEN, cache_rows,
                )
                out_ref[i, pl.ds(0, REQ_LEN), cols] = o.astype(out_ref.dtype)
                lse_ref[rows, pl.ds(h, 1)] = lse

        @pl.when(length == 0)
        def _():
            out_ref[i] = jnp.zeros((out_rows, width), out_ref.dtype)
            lse_ref[rows, :] = jnp.zeros((REQ_LEN, heads), lse_ref.dtype)

        return carry

    def one_group(g, carry):
        mode = mode_ref[g]
        rows = pl.ds(pl.multiple_of(g * span, span), span)

        @pl.when(mode == 0)
        def _():
            for j in range(GROUP):
                out_ref[g * GROUP + j] = jnp.zeros((out_rows, width), out_ref.dtype)
            lse_ref[rows, :] = jnp.zeros((span, heads), lse_ref.dtype)

        @pl.when(mode == 1)
        def _():
            node = gnode_ref[g]
            length = glen_ref[g]
            for h in range(heads):
                cols = pl.ds(h * HD, HD)
                o, lse = attend(
                    q_ref[rows, cols], k_ref[node, :, cols], v_ref[node, :, cols],
                    length, span, cache_rows,
                )
                for j in range(GROUP):
                    out_ref[g * GROUP + j, pl.ds(0, REQ_LEN), cols] = (
                        o[j * REQ_LEN : (j + 1) * REQ_LEN].astype(out_ref.dtype)
                    )
                lse_ref[rows, pl.ds(h, 1)] = lse

        @pl.when(mode == 2)
        def _():
            lax.fori_loop(g * GROUP, (g + 1) * GROUP, one_slot, 0)

        return carry

    lax.fori_loop(0, groups, one_group, 0)


def node_attention(queries, key_cache, value_cache, local_slot, lengths, heads_local):
    slots, rows, width = queries.shape
    nodes, cache_rows, _ = key_cache.shape
    groups = slots // GROUP
    live = (lengths > 0).reshape(groups, GROUP)
    grouped_node = local_slot.reshape(groups, GROUP)
    grouped_len = lengths.reshape(groups, GROUP)
    group_node = jnp.max(jnp.where(live, grouped_node, 0), axis=1)
    group_len = jnp.max(grouped_len, axis=1)
    uniform = jnp.all(~live | (grouped_node == group_node[:, None]), axis=1)
    mode = jnp.where(jnp.any(live, axis=1), jnp.where(uniform, 1, 2), 0).astype(jnp.int32)
    vmem = pl.BlockSpec(memory_space=pltpu.VMEM)
    smem = pl.BlockSpec(memory_space=pltpu.SMEM)
    flops = 4 * slots * rows * cache_rows * width
    out, lse = pl.pallas_call(
        node_kernel,
        out_shape=(
            jax.ShapeDtypeStruct((slots, PAD_ROWS, width), jnp.bfloat16),
            jax.ShapeDtypeStruct((slots * rows, heads_local), jnp.float32),
        ),
        in_specs=[smem] * 5 + [vmem] * 3,
        out_specs=(vmem, vmem),
        cost_estimate=pl.CostEstimate(
            flops=flops,
            transcendentals=slots * rows * cache_rows * heads_local,
            bytes_accessed=2 * queries.size * 2 + 2 * key_cache.size * 2,
        ),
    )(
        local_slot, lengths, mode, group_node, group_len,
        queries.reshape(slots * rows, width), key_cache, value_cache,
    )
    return out, lse.reshape(slots, rows, heads_local)


def sum_kernel(x_ref, out_ref, recv, send_sem, recv_sem):
    n = recv.shape[0]
    me = lax.axis_index("mp")
    barrier = pltpu.get_barrier_semaphore()
    for d in range(1, n):
        pl.semaphore_signal(
            barrier, inc=1, device_id={"mp": lax.rem(me + d, n)},
            device_id_type=pl.DeviceIdType.MESH,
        )
    pl.semaphore_wait(barrier, n - 1)
    copies = []
    for d in range(1, n):
        copy = pltpu.make_async_remote_copy(
            src_ref=x_ref,
            dst_ref=recv.at[d],
            send_sem=send_sem.at[d],
            recv_sem=recv_sem.at[d],
            device_id={"mp": lax.rem(me + d, n)},
            device_id_type=pl.DeviceIdType.MESH,
        )
        copy.start()
        copies.append(copy)
    for copy in copies:
        copy.wait()
    total = x_ref[...]
    for d in range(1, n):
        total = total + recv[d]
    out_ref[...] = total


def mp_sum(x, n):
    vmem = pl.BlockSpec(memory_space=pltpu.VMEM)
    return pl.pallas_call(
        sum_kernel,
        out_shape=jax.ShapeDtypeStruct(x.shape, x.dtype),
        in_specs=[vmem],
        out_specs=vmem,
        scratch_shapes=[
            pltpu.VMEM((n,) + x.shape, x.dtype),
            pltpu.SemaphoreType.DMA((n,)),
            pltpu.SemaphoreType.DMA((n,)),
        ],
        compiler_params=pltpu.CompilerParams(collective_id=0, has_side_effects=True),
    )(x)


def self_attention(queries, keys, values):
    head_dim = queries.shape[-1]
    row_total = queries.shape[1]
    scores = jnp.einsum(
        "rqhd,rkhd->rhqk", queries, keys, preferred_element_type=jnp.float32
    ) * head_dim ** (-0.5)
    causal = jnp.arange(row_total)[:, None] >= jnp.arange(row_total)[None, :]
    scores = jnp.where(causal[None, None], scores, mask_value)
    highest = jnp.max(scores, axis=-1)
    weights = jnp.exp(scores - highest[..., None])
    totals = jnp.sum(weights, axis=-1)
    mixture = jnp.einsum(
        "rhqk,rkhd->rqhd", weights.astype(jnp.bfloat16), values, preferred_element_type=jnp.float32
    )
    return (
        mixture / jnp.transpose(totals, (0, 2, 1))[..., None],
        jnp.transpose(highest + jnp.log(totals), (0, 2, 1)),
    )


def on_device(
    activations,
    w_query,
    w_key,
    w_value,
    w_out,
    norm_gain,
    key_cache,
    value_cache,
    parent,
    node_len,
    req_leaf,
):
    leaf_count = lax.axis_size("leaf")
    device = lax.axis_index("leaf")
    tok_rows = activations.shape[0]
    width_local = w_query.shape[1]
    heads_local = width_local // HD
    spread = leaf_count - TENANTS
    node_slots = 2 * ((REQ_DEV + spread - 1) // spread)
    all_slots = max(REQ_DEV // TENANTS, node_slots)
    block = REQ_LEN * width_local
    columns = lax.all_gather(activations, "mp", axis=1, tiled=True)
    query_f, key_f, value_f = tuple(
        (
            jnp.dot(columns, matrix, preferred_element_type=jnp.float32)
            for matrix in (w_query, w_key, w_value)
        )
    )
    middle_all = lookup(parent, req_leaf)
    root_all = lookup(parent, middle_all)
    len_of = lambda nodes: lookup(node_len, nodes)
    prefix = len_of(root_all) + len_of(middle_all) + len_of(req_leaf)
    mine_prefix = lax.dynamic_slice_in_dim(prefix, device * REQ_DEV, REQ_DEV)
    position = (mine_prefix[:, None] + jnp.arange(REQ_LEN, dtype=jnp.int32)[None, :]).reshape(
        tok_rows
    )
    queries = rotate(query_f.reshape(tok_rows, heads_local, HD), position).astype(jnp.bfloat16)
    keys = rotate(key_f.reshape(tok_rows, heads_local, HD), position).astype(jnp.bfloat16)
    values = value_f.astype(jnp.bfloat16)
    q_blocks = queries.reshape(REQ_DEV, block)
    self_out, self_lse = self_attention(
        queries.reshape(REQ_DEV, REQ_LEN, heads_local, HD),
        keys.reshape(REQ_DEV, REQ_LEN, heads_local, HD),
        values.reshape(REQ_DEV, REQ_LEN, heads_local, HD),
    )
    levels_all = jnp.stack([root_all, middle_all, req_leaf], axis=0).reshape(3, leaf_count, REQ_DEV)
    level_count = levels_all.shape[0]
    items = level_count * REQ_DEV
    per_sender = jnp.transpose(levels_all, (1, 0, 2)).reshape(leaf_count, items)
    holders = per_sender // NODE_DEV
    earlier = jnp.arange(items)[:, None] > jnp.arange(items)[None, :]
    ranks = jnp.sum(
        earlier[None] & (holders[:, :, None] == holders[:, None, :]), axis=2
    ).astype(jnp.int32)
    slot_ids = jnp.arange(all_slots, dtype=jnp.int32)
    my_holders = lax.dynamic_index_in_dim(holders, device, 0, keepdims=False)
    my_ranks = lax.dynamic_index_in_dim(ranks, device, 0, keepdims=False)
    send_hit = (
        (my_holders[None, None, :] == jnp.arange(leaf_count, dtype=jnp.int32)[:, None, None])
        & (my_ranks[None, None, :] == slot_ids[None, :, None])
    )
    send_item = jnp.sum(jnp.where(send_hit, jnp.arange(items, dtype=jnp.int32), 0), axis=2)
    send_valid = jnp.any(send_hit, axis=2)
    pick = (
        send_valid[:, :, None] & (send_item[:, :, None] % REQ_DEV == jnp.arange(REQ_DEV))
    ).reshape(leaf_count * all_slots, REQ_DEV)
    outgoing = (
        jnp.dot(pick.astype(jnp.bfloat16), q_blocks, preferred_element_type=jnp.float32)
        .astype(jnp.bfloat16)
        .reshape(leaf_count, all_slots, REQ_LEN, width_local)
    )
    arrived = lax.all_to_all(outgoing, "leaf", split_axis=0, concat_axis=0, tiled=True)
    recv_hit = (holders[:, None, :] == device) & (ranks[:, None, :] == slot_ids[None, :, None])
    slot_nodes = jnp.sum(jnp.where(recv_hit, per_sender[:, None, :], 0), axis=2).reshape(-1)
    filled = jnp.any(recv_hit, axis=2).reshape(-1)
    local_slot = jnp.where(filled, slot_nodes - device * NODE_DEV, 0)
    lengths = jnp.where(filled, len_of(slot_nodes), 0)
    node_out, node_lse = node_attention(
        arrived.reshape(leaf_count * all_slots, REQ_LEN, width_local),
        key_cache,
        value_cache,
        local_slot,
        lengths,
        heads_local,
    )
    slot_count = leaf_count * all_slots
    flat_lse = node_lse.reshape(slot_count, REQ_LEN * heads_local)
    lse_high = lax.reduce_precision(flat_lse, exponent_bits=8, mantissa_bits=7)
    lse_low = flat_lse - lse_high
    lse_rows = jnp.pad(
        jnp.concatenate([lse_high, lse_low], axis=1).astype(jnp.bfloat16).reshape(
            slot_count, 1, 2 * REQ_LEN * heads_local
        ),
        ((0, 0), (0, PAD_ROWS - REQ_LEN - 1), (0, width_local - 2 * REQ_LEN * heads_local)),
    )
    payload = lax.dynamic_update_slice(node_out, lse_rows, (0, REQ_LEN, 0))
    back_out = lax.all_to_all(
        payload.reshape(leaf_count, all_slots, PAD_ROWS, width_local),
        "leaf",
        split_axis=0,
        concat_axis=0,
        tiled=True,
    )
    chosen = my_holders * all_slots + my_ranks
    got = jnp.take(back_out.reshape(slot_count, PAD_ROWS, width_local), chosen, axis=0)
    got_out = got[:, :REQ_LEN].astype(jnp.float32).reshape(
        level_count, REQ_DEV, REQ_LEN, heads_local, HD
    )
    lse_width = REQ_LEN * heads_local
    got_pair = got[:, REQ_LEN, : 2 * lse_width].astype(jnp.float32)
    got_lse = (got_pair[:, :lse_width] + got_pair[:, lse_width:]).reshape(
        level_count, REQ_DEV, REQ_LEN, heads_local
    )
    partial_out = jnp.concatenate([got_out, self_out[None]], axis=0)
    partial_lse = jnp.concatenate([got_lse, self_lse[None]], axis=0)
    highest = jnp.max(partial_lse, axis=0)
    factor = jnp.exp(partial_lse - highest[None])
    merged = jnp.sum(factor[..., None] * partial_out, axis=0) / jnp.sum(factor, axis=0)[..., None]
    attn = merged.astype(jnp.bfloat16).reshape(tok_rows, width_local)
    partial_value = jnp.dot(attn, w_out, preferred_element_type=jnp.float32)
    projected = lax.psum_scatter(
        partial_value.astype(jnp.bfloat16), "mp", scatter_dimension=1, tiled=True
    ).astype(jnp.float32)
    squares = mp_sum(
        jnp.sum(projected * projected, axis=1).reshape(1, tok_rows), lax.axis_size("mp")
    ).reshape(tok_rows)
    row_scale = lax.rsqrt(squares / D + norm_eps)
    return (
        activations.astype(jnp.float32) + norm_gain[None, :] * projected * row_scale[:, None]
    ).astype(jnp.bfloat16)


def solution(mesh):
    in_specs = (
        P("leaf", "mp"),
        P(None, "mp"),
        P(None, "mp"),
        P(None, "mp"),
        P("mp", None),
        P("mp"),
        P("leaf", None, "mp"),
        P("leaf", None, "mp"),
        P(),
        P(),
        P(),
    )
    out_specs = P("leaf", "mp")
    return jax.shard_map(
        on_device, mesh=mesh, in_specs=in_specs, out_specs=out_specs, check_vma=False
    )
```

```python
import math

import jax
import jax.numpy as jnp
from jax import lax
from jax.experimental import pallas as pl
from jax.experimental.pallas import tpu as pltpu
from jax.sharding import PartitionSpec as P

D = 4096
HD = 128
TENANTS = 4
NODE_DEV = 8
REQ_LEN = 64
REQ_DEV = 4


rope_base = 500000.0
mask_value = -1e30
norm_eps = 1e-06


def rotate(values, positions):
    half_width = values.shape[-1] // 2
    inverse_freq = jnp.exp(
        jnp.arange(half_width, dtype=jnp.float32) * (-2.0 * math.log(rope_base) / values.shape[-1])
    )
    angles = positions.astype(jnp.float32)[:, None] * inverse_freq[None, :]
    cosine = jnp.cos(angles)[:, None, :]
    sine_part = jnp.sin(angles)[:, None, :]
    front_half = values[..., :half_width]
    back_half = values[..., half_width:]
    return jnp.concatenate(
        [front_half * cosine - back_half * sine_part, back_half * cosine + front_half * sine_part],
        axis=-1,
    )


def lookup(table, index):
    hit = index[..., None] == jnp.arange(table.shape[0], dtype=index.dtype)
    return jnp.sum(jnp.where(hit, table, 0), axis=-1).astype(table.dtype)


GROUP = 8


def attend(q, k, v, length, rows, cache_rows):
    live = lax.broadcasted_iota(jnp.int32, (rows, cache_rows), 1) < length
    s = lax.dot_general(
        q, k, (((1,), (1,)), ((), ())), preferred_element_type=jnp.float32
    ) * HD ** (-0.5)
    s = jnp.where(live, s, mask_value)
    m = jnp.max(s, axis=1, keepdims=True)
    p = jnp.exp(s - m)
    l = jnp.sum(p, axis=1, keepdims=True)
    o = jnp.dot(p.astype(jnp.bfloat16), v, preferred_element_type=jnp.float32)
    return o / l, m + jnp.log(l)


CHUNK = 4


def node_kernel(
    perm_ref, start_ref, count_ref, nlen_ref, total_ref, q_ref, k_ref, v_ref, out_ref, lse_ref, qbuf
):
    slots, rows, width = q_ref.shape
    nodes, cache_rows, _ = k_ref.shape
    heads = width // HD
    span = CHUNK * rows

    def per_node(n, carry):
        first = start_ref[n]
        count = count_ref[n]
        length = nlen_ref[n]
        last = first + count - 1

        def per_chunk(c, carry2):
            base = first + c * CHUNK
            picked = [perm_ref[jnp.minimum(base + j, last)] for j in range(CHUNK)]
            for j in range(CHUNK):
                qbuf[pl.ds(j * rows, rows), :] = q_ref[picked[j]]
            for h in range(heads):
                cols = pl.ds(h * HD, HD)
                o, lse = attend(
                    qbuf[:, cols], k_ref[n, :, cols], v_ref[n, :, cols], length, span, cache_rows
                )
                for j in range(CHUNK):

                    @pl.when(base + j <= last)
                    def _():
                        out_ref[picked[j], :, cols] = o[j * rows : (j + 1) * rows].astype(out_ref.dtype)
                        lse_ref[pl.ds(pl.multiple_of(picked[j] * rows, rows), rows), pl.ds(h, 1)] = (
                            lse[j * rows : (j + 1) * rows]
                        )

            return carry2

        lax.fori_loop(0, (count + CHUNK - 1) // CHUNK, per_chunk, 0)
        return carry

    lax.fori_loop(0, nodes, per_node, 0)

    def clear(p, carry):
        slot = perm_ref[p]
        out_ref[slot] = jnp.zeros((rows, width), out_ref.dtype)
        lse_ref[pl.ds(pl.multiple_of(slot * rows, rows), rows), :] = jnp.zeros(
            (rows, heads), lse_ref.dtype
        )
        return carry

    lax.fori_loop(total_ref[0], slots, clear, 0)


def node_attention(queries, key_cache, value_cache, local_slot, filled, local_len, heads_local):
    slots, rows, width = queries.shape
    nodes, cache_rows, _ = key_cache.shape
    order_key = jnp.where(filled, local_slot, nodes)
    index = jnp.arange(slots, dtype=jnp.int32)
    before = (order_key[None, :] < order_key[:, None]) | (
        (order_key[None, :] == order_key[:, None]) & (index[None, :] < index[:, None])
    )
    rank = jnp.sum(before, axis=1).astype(jnp.int32)
    perm = jnp.sum(
        jnp.where(rank[None, :] == index[:, None], index[None, :], 0), axis=1
    ).astype(jnp.int32)
    node_ids = jnp.arange(nodes, dtype=jnp.int32)
    count = jnp.sum(filled[None, :] & (local_slot[None, :] == node_ids[:, None]), axis=1).astype(jnp.int32)
    first = jnp.sum(filled[None, :] & (local_slot[None, :] < node_ids[:, None]), axis=1).astype(jnp.int32)
    total = jnp.sum(filled).astype(jnp.int32).reshape(1)
    vmem = pl.BlockSpec(memory_space=pltpu.VMEM)
    smem = pl.BlockSpec(memory_space=pltpu.SMEM)
    flops = 4 * slots * rows * cache_rows * width
    out, lse = pl.pallas_call(
        node_kernel,
        out_shape=(
            jax.ShapeDtypeStruct((slots, rows, width), jnp.bfloat16),
            jax.ShapeDtypeStruct((slots * rows, heads_local), jnp.float32),
        ),
        in_specs=[smem] * 5 + [vmem] * 3,
        out_specs=(vmem, vmem),
        scratch_shapes=[pltpu.VMEM((CHUNK * rows, width), queries.dtype)],
        cost_estimate=pl.CostEstimate(
            flops=flops,
            transcendentals=slots * rows * cache_rows * heads_local,
            bytes_accessed=2 * queries.size * 2 + 2 * key_cache.size * 2,
        ),
    )(perm, first, count, local_len, total, queries, key_cache, value_cache)
    return out, lse.reshape(slots, rows, heads_local)


def sum_kernel(x_ref, out_ref, recv, send_sem, recv_sem):
    n = recv.shape[0]
    me = lax.axis_index("mp")
    barrier = pltpu.get_barrier_semaphore()
    for d in range(1, n):
        pl.semaphore_signal(
            barrier, inc=1, device_id={"mp": lax.rem(me + d, n)},
            device_id_type=pl.DeviceIdType.MESH,
        )
    pl.semaphore_wait(barrier, n - 1)
    copies = []
    for d in range(1, n):
        copy = pltpu.make_async_remote_copy(
            src_ref=x_ref,
            dst_ref=recv.at[d],
            send_sem=send_sem.at[d],
            recv_sem=recv_sem.at[d],
            device_id={"mp": lax.rem(me + d, n)},
            device_id_type=pl.DeviceIdType.MESH,
        )
        copy.start()
        copies.append(copy)
    for copy in copies:
        copy.wait()
    total = x_ref[...]
    for d in range(1, n):
        total = total + recv[d]
    out_ref[...] = total


def mp_sum(x, n):
    vmem = pl.BlockSpec(memory_space=pltpu.VMEM)
    return pl.pallas_call(
        sum_kernel,
        out_shape=jax.ShapeDtypeStruct(x.shape, x.dtype),
        in_specs=[vmem],
        out_specs=vmem,
        scratch_shapes=[
            pltpu.VMEM((n,) + x.shape, x.dtype),
            pltpu.SemaphoreType.DMA((n,)),
            pltpu.SemaphoreType.DMA((n,)),
        ],
        compiler_params=pltpu.CompilerParams(collective_id=0, has_side_effects=True),
    )(x)


def self_attention(queries, keys, values):
    head_dim = queries.shape[-1]
    row_total = queries.shape[1]
    scores = jnp.einsum(
        "rqhd,rkhd->rhqk", queries, keys, preferred_element_type=jnp.float32
    ) * head_dim ** (-0.5)
    causal = jnp.arange(row_total)[:, None] >= jnp.arange(row_total)[None, :]
    scores = jnp.where(causal[None, None], scores, mask_value)
    highest = jnp.max(scores, axis=-1)
    weights = jnp.exp(scores - highest[..., None])
    totals = jnp.sum(weights, axis=-1)
    mixture = jnp.einsum(
        "rhqk,rkhd->rqhd", weights.astype(jnp.bfloat16), values, preferred_element_type=jnp.float32
    )
    return (
        mixture / jnp.transpose(totals, (0, 2, 1))[..., None],
        jnp.transpose(highest + jnp.log(totals), (0, 2, 1)),
    )


def on_device(
    activations,
    w_query,
    w_key,
    w_value,
    w_out,
    norm_gain,
    key_cache,
    value_cache,
    parent,
    node_len,
    req_leaf,
):
    leaf_count = lax.axis_size("leaf")
    device = lax.axis_index("leaf")
    tok_rows = activations.shape[0]
    width_local = w_query.shape[1]
    heads_local = width_local // HD
    spread = leaf_count - TENANTS
    node_slots = 2 * ((REQ_DEV + spread - 1) // spread)
    all_slots = max(REQ_DEV // TENANTS, node_slots)
    block = REQ_LEN * width_local
    columns = lax.all_gather(activations, "mp", axis=1, tiled=True)
    query_f, key_f, value_f = tuple(
        (
            jnp.dot(columns, matrix, preferred_element_type=jnp.float32)
            for matrix in (w_query, w_key, w_value)
        )
    )
    middle_all = lookup(parent, req_leaf)
    root_all = lookup(parent, middle_all)
    len_of = lambda nodes: lookup(node_len, nodes)
    prefix = len_of(root_all) + len_of(middle_all) + len_of(req_leaf)
    mine_prefix = lax.dynamic_slice_in_dim(prefix, device * REQ_DEV, REQ_DEV)
    position = (mine_prefix[:, None] + jnp.arange(REQ_LEN, dtype=jnp.int32)[None, :]).reshape(
        tok_rows
    )
    queries = rotate(query_f.reshape(tok_rows, heads_local, HD), position).astype(jnp.bfloat16)
    keys = rotate(key_f.reshape(tok_rows, heads_local, HD), position).astype(jnp.bfloat16)
    values = value_f.astype(jnp.bfloat16)
    q_blocks = queries.reshape(REQ_DEV, block)
    self_out, self_lse = self_attention(
        queries.reshape(REQ_DEV, REQ_LEN, heads_local, HD),
        keys.reshape(REQ_DEV, REQ_LEN, heads_local, HD),
        values.reshape(REQ_DEV, REQ_LEN, heads_local, HD),
    )
    levels_all = jnp.stack([root_all, middle_all, req_leaf], axis=0).reshape(3, leaf_count, REQ_DEV)
    level_count = levels_all.shape[0]
    items = level_count * REQ_DEV
    per_sender = jnp.transpose(levels_all, (1, 0, 2)).reshape(leaf_count, items)
    holders = per_sender // NODE_DEV
    earlier = jnp.arange(items)[:, None] > jnp.arange(items)[None, :]
    ranks = jnp.sum(
        earlier[None] & (holders[:, :, None] == holders[:, None, :]), axis=2
    ).astype(jnp.int32)
    slot_ids = jnp.arange(all_slots, dtype=jnp.int32)
    my_holders = lax.dynamic_index_in_dim(holders, device, 0, keepdims=False)
    my_ranks = lax.dynamic_index_in_dim(ranks, device, 0, keepdims=False)
    send_hit = (
        (my_holders[None, None, :] == jnp.arange(leaf_count, dtype=jnp.int32)[:, None, None])
        & (my_ranks[None, None, :] == slot_ids[None, :, None])
    )
    send_item = jnp.sum(jnp.where(send_hit, jnp.arange(items, dtype=jnp.int32), 0), axis=2)
    send_valid = jnp.any(send_hit, axis=2)
    pick = (
        send_valid[:, :, None] & (send_item[:, :, None] % REQ_DEV == jnp.arange(REQ_DEV))
    ).reshape(leaf_count * all_slots, REQ_DEV)
    outgoing = (
        jnp.dot(pick.astype(jnp.bfloat16), q_blocks, preferred_element_type=jnp.float32)
        .astype(jnp.bfloat16)
        .reshape(leaf_count, all_slots, REQ_LEN, width_local)
    )
    arrived = lax.all_to_all(outgoing, "leaf", split_axis=0, concat_axis=0, tiled=True)
    recv_hit = (holders[:, None, :] == device) & (ranks[:, None, :] == slot_ids[None, :, None])
    slot_nodes = jnp.sum(jnp.where(recv_hit, per_sender[:, None, :], 0), axis=2).reshape(-1)
    filled = jnp.any(recv_hit, axis=2).reshape(-1)
    local_slot = jnp.where(filled, slot_nodes - device * NODE_DEV, 0)
    lengths = jnp.where(filled, len_of(slot_nodes), 0)
    node_out, node_lse = node_attention(
        arrived.reshape(leaf_count * all_slots, REQ_LEN, width_local),
        key_cache,
        value_cache,
        local_slot,
        filled,
        lax.dynamic_slice_in_dim(node_len, device * NODE_DEV, NODE_DEV),
        heads_local,
    )
    flat_lse = node_lse.reshape(leaf_count * all_slots, REQ_LEN * heads_local)
    lse_high = lax.reduce_precision(flat_lse, exponent_bits=8, mantissa_bits=7)
    lse_low = flat_lse - lse_high
    lse_pair = jnp.stack([lse_high, lse_low], axis=1).astype(jnp.bfloat16)
    back_out = lax.all_to_all(
        node_out.reshape(leaf_count, all_slots, REQ_LEN, width_local),
        "leaf",
        split_axis=0,
        concat_axis=0,
        tiled=True,
    )
    back_lse = lax.all_to_all(
        lse_pair.reshape(leaf_count, all_slots, 2, REQ_LEN * heads_local),
        "leaf",
        split_axis=0,
        concat_axis=0,
        tiled=True,
    )
    take = (
        (my_holders * all_slots + my_ranks)[:, None]
        == jnp.arange(leaf_count * all_slots, dtype=jnp.int32)[None, :]
    ).astype(jnp.bfloat16)
    chosen = my_holders * all_slots + my_ranks
    got_out = jnp.take(
        back_out.reshape(leaf_count * all_slots, REQ_LEN, width_local), chosen, axis=0
    ).astype(jnp.float32).reshape(level_count, REQ_DEV, REQ_LEN, heads_local, HD)
    got_pair = jnp.dot(
        take,
        back_lse.reshape(leaf_count * all_slots, 2 * REQ_LEN * heads_local),
        preferred_element_type=jnp.float32,
    ).reshape(items, 2, REQ_LEN * heads_local)
    got_lse = (got_pair[:, 0] + got_pair[:, 1]).reshape(level_count, REQ_DEV, REQ_LEN, heads_local)
    partial_out = jnp.concatenate([got_out, self_out[None]], axis=0)
    partial_lse = jnp.concatenate([got_lse, self_lse[None]], axis=0)
    highest = jnp.max(partial_lse, axis=0)
    factor = jnp.exp(partial_lse - highest[None])
    merged = jnp.sum(factor[..., None] * partial_out, axis=0) / jnp.sum(factor, axis=0)[..., None]
    attn = merged.astype(jnp.bfloat16).reshape(tok_rows, width_local)
    partial_value = jnp.dot(attn, w_out, preferred_element_type=jnp.float32)
    projected = lax.psum_scatter(
        partial_value.astype(jnp.bfloat16), "mp", scatter_dimension=1, tiled=True
    ).astype(jnp.float32)
    squares = mp_sum(
        jnp.sum(projected * projected, axis=1).reshape(1, tok_rows), lax.axis_size("mp")
    ).reshape(tok_rows)
    row_scale = lax.rsqrt(squares / D + norm_eps)
    return (
        activations.astype(jnp.float32) + norm_gain[None, :] * projected * row_scale[:, None]
    ).astype(jnp.bfloat16)


def solution(mesh):
    in_specs = (
        P("leaf", "mp"),
        P(None, "mp"),
        P(None, "mp"),
        P(None, "mp"),
        P("mp", None),
        P("mp"),
        P("leaf", None, "mp"),
        P("leaf", None, "mp"),
        P(),
        P(),
        P(),
    )
    out_specs = P("leaf", "mp")
    return jax.shard_map(
        on_device, mesh=mesh, in_specs=in_specs, out_specs=out_specs, check_vma=False
    )
```

```python
import math

import jax
import jax.numpy as jnp
from jax import lax
from jax.experimental import pallas as pl
from jax.experimental.pallas import tpu as pltpu
from jax.sharding import PartitionSpec as P

D = 4096
HD = 128
TENANTS = 4
NODE_DEV = 8
REQ_LEN = 64
REQ_DEV = 4


rope_base = 500000.0
mask_value = -1e30
norm_eps = 1e-06


def rotate(values, positions):
    half_width = values.shape[-1] // 2
    inverse_freq = jnp.exp(
        jnp.arange(half_width, dtype=jnp.float32) * (-2.0 * math.log(rope_base) / values.shape[-1])
    )
    angles = positions.astype(jnp.float32)[:, None] * inverse_freq[None, :]
    cosine = jnp.cos(angles)[:, None, :]
    sine_part = jnp.sin(angles)[:, None, :]
    front_half = values[..., :half_width]
    back_half = values[..., half_width:]
    return jnp.concatenate(
        [front_half * cosine - back_half * sine_part, back_half * cosine + front_half * sine_part],
        axis=-1,
    )


def lookup(table, index):
    hit = index[..., None] == jnp.arange(table.shape[0], dtype=index.dtype)
    return jnp.sum(jnp.where(hit, table, 0), axis=-1).astype(table.dtype)


GROUP = 8


def attend(q, k, v, length, rows, cache_rows):
    live = lax.broadcasted_iota(jnp.int32, (rows, cache_rows), 1) < length
    s = lax.dot_general(
        q, k, (((1,), (1,)), ((), ())), preferred_element_type=jnp.float32
    ) * HD ** (-0.5)
    s = jnp.where(live, s, mask_value)
    m = jnp.max(s, axis=1, keepdims=True)
    p = jnp.exp(s - m)
    l = jnp.sum(p, axis=1, keepdims=True)
    o = jnp.dot(p.astype(jnp.bfloat16), v, preferred_element_type=jnp.float32)
    return o / l, m + jnp.log(l)


CHUNK = 4


def node_kernel(
    perm_ref, start_ref, count_ref, nlen_ref, total_ref, q_ref, k_ref, v_ref, out_ref, lse_ref, qbuf
):
    slots, rows, width = q_ref.shape
    nodes, cache_rows, _ = k_ref.shape
    heads = width // HD
    span = CHUNK * rows

    def per_node(n, carry):
        first = start_ref[n]
        count = count_ref[n]
        length = nlen_ref[n]
        last = first + count - 1

        def per_chunk(c, carry2):
            base = first + c * CHUNK
            picked = [perm_ref[jnp.minimum(base + j, last)] for j in range(CHUNK)]
            for j in range(CHUNK):
                qbuf[pl.ds(j * rows, rows), :] = q_ref[picked[j]]
            for h in range(heads):
                cols = pl.ds(h * HD, HD)
                o, lse = attend(
                    qbuf[:, cols], k_ref[n, :, cols], v_ref[n, :, cols], length, span, cache_rows
                )
                for j in range(CHUNK):

                    @pl.when(base + j <= last)
                    def _():
                        out_ref[picked[j] // 2, pl.ds(pl.multiple_of(picked[j] % 2 * rows, rows), rows), cols] = (
                            o[j * rows : (j + 1) * rows].astype(out_ref.dtype)
                        )
                        lse_ref[pl.ds(pl.multiple_of(picked[j] * rows, rows), rows), pl.ds(h, 1)] = (
                            lse[j * rows : (j + 1) * rows]
                        )

            return carry2

        lax.fori_loop(0, (count + CHUNK - 1) // CHUNK, per_chunk, 0)
        return carry

    lax.fori_loop(0, nodes, per_node, 0)

    def clear(p, carry):
        slot = perm_ref[p]
        out_ref[slot // 2, pl.ds(pl.multiple_of(slot % 2 * rows, rows), rows), :] = jnp.zeros(
            (rows, width), out_ref.dtype
        )
        lse_ref[pl.ds(pl.multiple_of(slot * rows, rows), rows), :] = jnp.zeros(
            (rows, heads), lse_ref.dtype
        )
        return carry

    lax.fori_loop(total_ref[0], slots, clear, 0)


def node_attention(queries, key_cache, value_cache, local_slot, filled, local_len, heads_local):
    slots, rows, width = queries.shape
    nodes, cache_rows, _ = key_cache.shape
    order_key = jnp.where(filled, local_slot, nodes)
    index = jnp.arange(slots, dtype=jnp.int32)
    before = (order_key[None, :] < order_key[:, None]) | (
        (order_key[None, :] == order_key[:, None]) & (index[None, :] < index[:, None])
    )
    rank = jnp.sum(before, axis=1).astype(jnp.int32)
    perm = jnp.sum(
        jnp.where(rank[None, :] == index[:, None], index[None, :], 0), axis=1
    ).astype(jnp.int32)
    node_ids = jnp.arange(nodes, dtype=jnp.int32)
    count = jnp.sum(filled[None, :] & (local_slot[None, :] == node_ids[:, None]), axis=1).astype(jnp.int32)
    first = jnp.sum(filled[None, :] & (local_slot[None, :] < node_ids[:, None]), axis=1).astype(jnp.int32)
    total = jnp.sum(filled).astype(jnp.int32).reshape(1)
    vmem = pl.BlockSpec(memory_space=pltpu.VMEM)
    smem = pl.BlockSpec(memory_space=pltpu.SMEM)
    flops = 4 * slots * rows * cache_rows * width
    out, lse = pl.pallas_call(
        node_kernel,
        out_shape=(
            jax.ShapeDtypeStruct((slots // 2, 2 * rows + 16, width), jnp.bfloat16),
            jax.ShapeDtypeStruct((slots * rows, heads_local), jnp.float32),
        ),
        in_specs=[smem] * 5 + [vmem] * 3,
        out_specs=(vmem, vmem),
        scratch_shapes=[pltpu.VMEM((CHUNK * rows, width), queries.dtype)],
        cost_estimate=pl.CostEstimate(
            flops=flops,
            transcendentals=slots * rows * cache_rows * heads_local,
            bytes_accessed=2 * queries.size * 2 + 2 * key_cache.size * 2,
        ),
    )(perm, first, count, local_len, total, queries, key_cache, value_cache)
    return out, lse.reshape(slots, rows, heads_local)


def sum_kernel(x_ref, out_ref, recv, send_sem, recv_sem):
    n = recv.shape[0]
    me = lax.axis_index("mp")
    barrier = pltpu.get_barrier_semaphore()
    for d in range(1, n):
        pl.semaphore_signal(
            barrier, inc=1, device_id={"mp": lax.rem(me + d, n)},
            device_id_type=pl.DeviceIdType.MESH,
        )
    pl.semaphore_wait(barrier, n - 1)
    copies = []
    for d in range(1, n):
        copy = pltpu.make_async_remote_copy(
            src_ref=x_ref,
            dst_ref=recv.at[d],
            send_sem=send_sem.at[d],
            recv_sem=recv_sem.at[d],
            device_id={"mp": lax.rem(me + d, n)},
            device_id_type=pl.DeviceIdType.MESH,
        )
        copy.start()
        copies.append(copy)
    for copy in copies:
        copy.wait()
    total = x_ref[...]
    for d in range(1, n):
        total = total + recv[d]
    out_ref[...] = total


def mp_sum(x, n):
    vmem = pl.BlockSpec(memory_space=pltpu.VMEM)
    return pl.pallas_call(
        sum_kernel,
        out_shape=jax.ShapeDtypeStruct(x.shape, x.dtype),
        in_specs=[vmem],
        out_specs=vmem,
        scratch_shapes=[
            pltpu.VMEM((n,) + x.shape, x.dtype),
            pltpu.SemaphoreType.DMA((n,)),
            pltpu.SemaphoreType.DMA((n,)),
        ],
        compiler_params=pltpu.CompilerParams(collective_id=0, has_side_effects=True),
    )(x)


def self_attention(queries, keys, values):
    head_dim = queries.shape[-1]
    row_total = queries.shape[1]
    scores = jnp.einsum(
        "rqhd,rkhd->rhqk", queries, keys, preferred_element_type=jnp.float32
    ) * head_dim ** (-0.5)
    causal = jnp.arange(row_total)[:, None] >= jnp.arange(row_total)[None, :]
    scores = jnp.where(causal[None, None], scores, mask_value)
    highest = jnp.max(scores, axis=-1)
    weights = jnp.exp(scores - highest[..., None])
    totals = jnp.sum(weights, axis=-1)
    mixture = jnp.einsum(
        "rhqk,rkhd->rqhd", weights.astype(jnp.bfloat16), values, preferred_element_type=jnp.float32
    )
    return (
        mixture / jnp.transpose(totals, (0, 2, 1))[..., None],
        jnp.transpose(highest + jnp.log(totals), (0, 2, 1)),
    )


def on_device(
    activations,
    w_query,
    w_key,
    w_value,
    w_out,
    norm_gain,
    key_cache,
    value_cache,
    parent,
    node_len,
    req_leaf,
):
    leaf_count = lax.axis_size("leaf")
    device = lax.axis_index("leaf")
    tok_rows = activations.shape[0]
    width_local = w_query.shape[1]
    heads_local = width_local // HD
    spread = leaf_count - TENANTS
    node_slots = 2 * ((REQ_DEV + spread - 1) // spread)
    all_slots = max(REQ_DEV // TENANTS, node_slots)
    block = REQ_LEN * width_local
    columns = lax.all_gather(activations, "mp", axis=1, tiled=True)
    query_f, key_f, value_f = tuple(
        (
            jnp.dot(columns, matrix, preferred_element_type=jnp.float32)
            for matrix in (w_query, w_key, w_value)
        )
    )
    middle_all = lookup(parent, req_leaf)
    root_all = lookup(parent, middle_all)
    len_of = lambda nodes: lookup(node_len, nodes)
    prefix = len_of(root_all) + len_of(middle_all) + len_of(req_leaf)
    mine_prefix = lax.dynamic_slice_in_dim(prefix, device * REQ_DEV, REQ_DEV)
    position = (mine_prefix[:, None] + jnp.arange(REQ_LEN, dtype=jnp.int32)[None, :]).reshape(
        tok_rows
    )
    queries = rotate(query_f.reshape(tok_rows, heads_local, HD), position).astype(jnp.bfloat16)
    keys = rotate(key_f.reshape(tok_rows, heads_local, HD), position).astype(jnp.bfloat16)
    values = value_f.astype(jnp.bfloat16)
    q_blocks = queries.reshape(REQ_DEV, block)
    self_out, self_lse = self_attention(
        queries.reshape(REQ_DEV, REQ_LEN, heads_local, HD),
        keys.reshape(REQ_DEV, REQ_LEN, heads_local, HD),
        values.reshape(REQ_DEV, REQ_LEN, heads_local, HD),
    )
    levels_all = jnp.stack([root_all, middle_all, req_leaf], axis=0).reshape(3, leaf_count, REQ_DEV)
    level_count = levels_all.shape[0]
    items = level_count * REQ_DEV
    per_sender = jnp.transpose(levels_all, (1, 0, 2)).reshape(leaf_count, items)
    holders = per_sender // NODE_DEV
    earlier = jnp.arange(items)[:, None] > jnp.arange(items)[None, :]
    ranks = jnp.sum(
        earlier[None] & (holders[:, :, None] == holders[:, None, :]), axis=2
    ).astype(jnp.int32)
    slot_ids = jnp.arange(all_slots, dtype=jnp.int32)
    my_holders = lax.dynamic_index_in_dim(holders, device, 0, keepdims=False)
    my_ranks = lax.dynamic_index_in_dim(ranks, device, 0, keepdims=False)
    send_hit = (
        (my_holders[None, None, :] == jnp.arange(leaf_count, dtype=jnp.int32)[:, None, None])
        & (my_ranks[None, None, :] == slot_ids[None, :, None])
    )
    send_item = jnp.sum(jnp.where(send_hit, jnp.arange(items, dtype=jnp.int32), 0), axis=2)
    send_valid = jnp.any(send_hit, axis=2)
    pick = (
        send_valid[:, :, None] & (send_item[:, :, None] % REQ_DEV == jnp.arange(REQ_DEV))
    ).reshape(leaf_count * all_slots, REQ_DEV)
    outgoing = (
        jnp.dot(pick.astype(jnp.bfloat16), q_blocks, preferred_element_type=jnp.float32)
        .astype(jnp.bfloat16)
        .reshape(leaf_count, all_slots, REQ_LEN, width_local)
    )
    arrived = lax.all_to_all(outgoing, "leaf", split_axis=0, concat_axis=0, tiled=True)
    recv_hit = (holders[:, None, :] == device) & (ranks[:, None, :] == slot_ids[None, :, None])
    slot_nodes = jnp.sum(jnp.where(recv_hit, per_sender[:, None, :], 0), axis=2).reshape(-1)
    filled = jnp.any(recv_hit, axis=2).reshape(-1)
    local_slot = jnp.where(filled, slot_nodes - device * NODE_DEV, 0)
    lengths = jnp.where(filled, len_of(slot_nodes), 0)
    node_out, node_lse = node_attention(
        arrived.reshape(leaf_count * all_slots, REQ_LEN, width_local),
        key_cache,
        value_cache,
        local_slot,
        filled,
        lax.dynamic_slice_in_dim(node_len, device * NODE_DEV, NODE_DEV),
        heads_local,
    )
    slot_count = leaf_count * all_slots
    flat_lse = node_lse.reshape(slot_count, REQ_LEN * heads_local)
    lse_high = lax.reduce_precision(flat_lse, exponent_bits=8, mantissa_bits=7)
    lse_low = flat_lse - lse_high
    pair_width = 2 * REQ_LEN * heads_local
    lse_rows = jnp.pad(
        jnp.concatenate([lse_high, lse_low], axis=1).astype(jnp.bfloat16).reshape(
            leaf_count, all_slots, pair_width
        ),
        ((0, 0), (0, 16 - all_slots), (0, width_local - pair_width)),
    )
    payload = lax.dynamic_update_slice(node_out, lse_rows, (0, all_slots * REQ_LEN, 0))
    back = lax.all_to_all(payload, "leaf", split_axis=0, concat_axis=0, tiled=True)
    got = jnp.take(back, my_holders, axis=0)
    second = (my_ranks == 1)[:, None, None]
    got_out = (
        jnp.where(second, got[:, REQ_LEN : 2 * REQ_LEN], got[:, :REQ_LEN])
        .astype(jnp.float32)
        .reshape(level_count, REQ_DEV, REQ_LEN, heads_local, HD)
    )
    lse_at = all_slots * REQ_LEN
    got_pair = jnp.where(
        second[:, 0], got[:, lse_at + 1, :pair_width], got[:, lse_at, :pair_width]
    ).astype(jnp.float32)
    lse_width = REQ_LEN * heads_local
    got_lse = (got_pair[:, :lse_width] + got_pair[:, lse_width:]).reshape(
        level_count, REQ_DEV, REQ_LEN, heads_local
    )
    partial_out = jnp.concatenate([got_out, self_out[None]], axis=0)
    partial_lse = jnp.concatenate([got_lse, self_lse[None]], axis=0)
    highest = jnp.max(partial_lse, axis=0)
    factor = jnp.exp(partial_lse - highest[None])
    merged = jnp.sum(factor[..., None] * partial_out, axis=0) / jnp.sum(factor, axis=0)[..., None]
    attn = merged.astype(jnp.bfloat16).reshape(tok_rows, width_local)
    partial_value = jnp.dot(attn, w_out, preferred_element_type=jnp.float32)
    projected = lax.psum_scatter(
        partial_value.astype(jnp.bfloat16), "mp", scatter_dimension=1, tiled=True
    ).astype(jnp.float32)
    squares = mp_sum(
        jnp.sum(projected * projected, axis=1).reshape(1, tok_rows), lax.axis_size("mp")
    ).reshape(tok_rows)
    row_scale = lax.rsqrt(squares / D + norm_eps)
    return (
        activations.astype(jnp.float32) + norm_gain[None, :] * projected * row_scale[:, None]
    ).astype(jnp.bfloat16)


def solution(mesh):
    in_specs = (
        P("leaf", "mp"),
        P(None, "mp"),
        P(None, "mp"),
        P(None, "mp"),
        P("mp", None),
        P("mp"),
        P("leaf", None, "mp"),
        P("leaf", None, "mp"),
        P(),
        P(),
        P(),
    )
    out_specs = P("leaf", "mp")
    return jax.shard_map(
        on_device, mesh=mesh, in_specs=in_specs, out_specs=out_specs, check_vma=False
    )
```

```python
import math

import jax
import jax.numpy as jnp
from jax import lax
from jax.experimental import pallas as pl
from jax.experimental.pallas import tpu as pltpu
from jax.sharding import PartitionSpec as P

D = 4096
HD = 128
TENANTS = 4
NODE_DEV = 8
REQ_LEN = 64
REQ_DEV = 4


rope_base = 500000.0
mask_value = -1e30
norm_eps = 1e-06


def rotate(values, positions):
    half_width = values.shape[-1] // 2
    inverse_freq = jnp.exp(
        jnp.arange(half_width, dtype=jnp.float32) * (-2.0 * math.log(rope_base) / values.shape[-1])
    )
    angles = positions.astype(jnp.float32)[:, None] * inverse_freq[None, :]
    cosine = jnp.cos(angles)[:, None, :]
    sine_part = jnp.sin(angles)[:, None, :]
    front_half = values[..., :half_width]
    back_half = values[..., half_width:]
    return jnp.concatenate(
        [front_half * cosine - back_half * sine_part, back_half * cosine + front_half * sine_part],
        axis=-1,
    )


def lookup(table, index):
    hit = index[..., None] == jnp.arange(table.shape[0], dtype=index.dtype)
    return jnp.sum(jnp.where(hit, table, 0), axis=-1).astype(table.dtype)


GROUP = 8


def attend(q, k, v, length, rows, cache_rows):
    live = lax.broadcasted_iota(jnp.int32, (rows, cache_rows), 1) < length
    s = lax.dot_general(
        q, k, (((1,), (1,)), ((), ())), preferred_element_type=jnp.float32
    ) * HD ** (-0.5)
    s = jnp.where(live, s, mask_value)
    m = jnp.max(s, axis=1, keepdims=True)
    p = jnp.exp(s - m)
    l = jnp.sum(p, axis=1, keepdims=True)
    o = jnp.dot(p.astype(jnp.bfloat16), v, preferred_element_type=jnp.float32)
    return o / l, m + jnp.log(l)


CHUNK = 4


def node_kernel(
    perm_ref, start_ref, count_ref, nlen_ref, total_ref, q_ref, k_ref, v_ref, out_ref, lse_ref, qbuf
):
    slots, rows, width = q_ref.shape
    nodes, cache_rows, _ = k_ref.shape
    heads = width // HD
    span = CHUNK * rows

    def per_node(n, carry):
        first = start_ref[n]
        count = count_ref[n]
        length = nlen_ref[n]
        last = first + count - 1

        def per_chunk(c, carry2):
            base = first + c * CHUNK
            picked = [perm_ref[jnp.minimum(base + j, last)] for j in range(CHUNK)]
            for j in range(CHUNK):
                qbuf[pl.ds(j * rows, rows), :] = q_ref[picked[j]]
            lse_cols = []
            for h in range(heads):
                cols = pl.ds(h * HD, HD)
                o, lse = attend(
                    qbuf[:, cols], k_ref[n, :, cols], v_ref[n, :, cols], length, span, cache_rows
                )
                lse_cols.append(lse)
                for j in range(CHUNK):

                    @pl.when(base + j <= last)
                    def _():
                        out_ref[picked[j] // 2, pl.ds(pl.multiple_of(picked[j] % 2 * rows, rows), rows), cols] = (
                            o[j * rows : (j + 1) * rows].astype(out_ref.dtype)
                        )

            lane = lax.broadcasted_iota(jnp.int32, (span, 128), 1)
            lse_tile = jnp.zeros((span, 128), jnp.float32)
            for h in range(heads):
                lse_tile = jnp.where(lane == h, lse_cols[h], lse_tile)
            lse_t = jnp.transpose(lse_tile)
            for j in range(CHUNK):

                @pl.when(base + j <= last)
                def _():
                    for h in range(heads):
                        lse_ref[pl.ds(picked[j], 1), pl.ds(h * rows, rows)] = (
                            lse_t[h : h + 1, j * rows : (j + 1) * rows]
                        )

            return carry2

        lax.fori_loop(0, (count + CHUNK - 1) // CHUNK, per_chunk, 0)
        return carry

    lax.fori_loop(0, nodes, per_node, 0)

    def clear(p, carry):
        slot = perm_ref[p]
        out_ref[slot // 2, pl.ds(pl.multiple_of(slot % 2 * rows, rows), rows), :] = jnp.zeros(
            (rows, width), out_ref.dtype
        )
        lse_ref[pl.ds(slot, 1), :] = jnp.zeros((1, rows * heads), lse_ref.dtype)
        return carry

    lax.fori_loop(total_ref[0], slots, clear, 0)


def node_attention(queries, key_cache, value_cache, local_slot, filled, local_len, heads_local):
    slots, rows, width = queries.shape
    nodes, cache_rows, _ = key_cache.shape
    order_key = jnp.where(filled, local_slot, nodes)
    index = jnp.arange(slots, dtype=jnp.int32)
    before = (order_key[None, :] < order_key[:, None]) | (
        (order_key[None, :] == order_key[:, None]) & (index[None, :] < index[:, None])
    )
    rank = jnp.sum(before, axis=1).astype(jnp.int32)
    perm = jnp.sum(
        jnp.where(rank[None, :] == index[:, None], index[None, :], 0), axis=1
    ).astype(jnp.int32)
    node_ids = jnp.arange(nodes, dtype=jnp.int32)
    count = jnp.sum(filled[None, :] & (local_slot[None, :] == node_ids[:, None]), axis=1).astype(jnp.int32)
    first = jnp.sum(filled[None, :] & (local_slot[None, :] < node_ids[:, None]), axis=1).astype(jnp.int32)
    total = jnp.sum(filled).astype(jnp.int32).reshape(1)
    vmem = pl.BlockSpec(memory_space=pltpu.VMEM)
    smem = pl.BlockSpec(memory_space=pltpu.SMEM)
    flops = 4 * slots * rows * cache_rows * width
    out, lse = pl.pallas_call(
        node_kernel,
        out_shape=(
            jax.ShapeDtypeStruct((slots // 2, 2 * rows + 16, width), jnp.bfloat16),
            jax.ShapeDtypeStruct((slots, rows * heads_local), jnp.float32),
        ),
        in_specs=[smem] * 5 + [vmem] * 3,
        out_specs=(vmem, vmem),
        scratch_shapes=[pltpu.VMEM((CHUNK * rows, width), queries.dtype)],
        cost_estimate=pl.CostEstimate(
            flops=flops,
            transcendentals=slots * rows * cache_rows * heads_local,
            bytes_accessed=2 * queries.size * 2 + 2 * key_cache.size * 2,
        ),
    )(perm, first, count, local_len, total, queries, key_cache, value_cache)
    return out, lse


def sum_kernel(x_ref, out_ref, recv, send_sem, recv_sem):
    n = recv.shape[0]
    me = lax.axis_index("mp")
    barrier = pltpu.get_barrier_semaphore()
    for d in range(1, n):
        pl.semaphore_signal(
            barrier, inc=1, device_id={"mp": lax.rem(me + d, n)},
            device_id_type=pl.DeviceIdType.MESH,
        )
    pl.semaphore_wait(barrier, n - 1)
    copies = []
    for d in range(1, n):
        copy = pltpu.make_async_remote_copy(
            src_ref=x_ref,
            dst_ref=recv.at[d],
            send_sem=send_sem.at[d],
            recv_sem=recv_sem.at[d],
            device_id={"mp": lax.rem(me + d, n)},
            device_id_type=pl.DeviceIdType.MESH,
        )
        copy.start()
        copies.append(copy)
    for copy in copies:
        copy.wait()
    total = x_ref[...]
    for d in range(1, n):
        total = total + recv[d]
    out_ref[...] = total


def mp_sum(x, n):
    vmem = pl.BlockSpec(memory_space=pltpu.VMEM)
    return pl.pallas_call(
        sum_kernel,
        out_shape=jax.ShapeDtypeStruct(x.shape, x.dtype),
        in_specs=[vmem],
        out_specs=vmem,
        scratch_shapes=[
            pltpu.VMEM((n,) + x.shape, x.dtype),
            pltpu.SemaphoreType.DMA((n,)),
            pltpu.SemaphoreType.DMA((n,)),
        ],
        compiler_params=pltpu.CompilerParams(collective_id=0, has_side_effects=True),
    )(x)


def self_attention(queries, keys, values):
    head_dim = queries.shape[-1]
    row_total = queries.shape[1]
    scores = jnp.einsum(
        "rqhd,rkhd->rhqk", queries, keys, preferred_element_type=jnp.float32
    ) * head_dim ** (-0.5)
    causal = jnp.arange(row_total)[:, None] >= jnp.arange(row_total)[None, :]
    scores = jnp.where(causal[None, None], scores, mask_value)
    highest = jnp.max(scores, axis=-1)
    weights = jnp.exp(scores - highest[..., None])
    totals = jnp.sum(weights, axis=-1)
    mixture = jnp.einsum(
        "rhqk,rkhd->rqhd", weights.astype(jnp.bfloat16), values, preferred_element_type=jnp.float32
    )
    return (
        mixture / jnp.transpose(totals, (0, 2, 1))[..., None],
        jnp.transpose(highest + jnp.log(totals), (0, 2, 1)),
    )


def on_device(
    activations,
    w_query,
    w_key,
    w_value,
    w_out,
    norm_gain,
    key_cache,
    value_cache,
    parent,
    node_len,
    req_leaf,
):
    leaf_count = lax.axis_size("leaf")
    device = lax.axis_index("leaf")
    tok_rows = activations.shape[0]
    width_local = w_query.shape[1]
    heads_local = width_local // HD
    spread = leaf_count - TENANTS
    node_slots = 2 * ((REQ_DEV + spread - 1) // spread)
    all_slots = max(REQ_DEV // TENANTS, node_slots)
    block = REQ_LEN * width_local
    columns = lax.all_gather(activations, "mp", axis=1, tiled=True)
    query_f, key_f, value_f = tuple(
        (
            jnp.dot(columns, matrix, preferred_element_type=jnp.float32)
            for matrix in (w_query, w_key, w_value)
        )
    )
    middle_all = lookup(parent, req_leaf)
    root_all = lookup(parent, middle_all)
    len_of = lambda nodes: lookup(node_len, nodes)
    prefix = len_of(root_all) + len_of(middle_all) + len_of(req_leaf)
    mine_prefix = lax.dynamic_slice_in_dim(prefix, device * REQ_DEV, REQ_DEV)
    position = (mine_prefix[:, None] + jnp.arange(REQ_LEN, dtype=jnp.int32)[None, :]).reshape(
        tok_rows
    )
    queries = rotate(query_f.reshape(tok_rows, heads_local, HD), position).astype(jnp.bfloat16)
    keys = rotate(key_f.reshape(tok_rows, heads_local, HD), position).astype(jnp.bfloat16)
    values = value_f.astype(jnp.bfloat16)
    q_blocks = queries.reshape(REQ_DEV, block)
    self_out, self_lse = self_attention(
        queries.reshape(REQ_DEV, REQ_LEN, heads_local, HD),
        keys.reshape(REQ_DEV, REQ_LEN, heads_local, HD),
        values.reshape(REQ_DEV, REQ_LEN, heads_local, HD),
    )
    levels_all = jnp.stack([root_all, middle_all, req_leaf], axis=0).reshape(3, leaf_count, REQ_DEV)
    level_count = levels_all.shape[0]
    items = level_count * REQ_DEV
    per_sender = jnp.transpose(levels_all, (1, 0, 2)).reshape(leaf_count, items)
    holders = per_sender // NODE_DEV
    earlier = jnp.arange(items)[:, None] > jnp.arange(items)[None, :]
    ranks = jnp.sum(
        earlier[None] & (holders[:, :, None] == holders[:, None, :]), axis=2
    ).astype(jnp.int32)
    slot_ids = jnp.arange(all_slots, dtype=jnp.int32)
    my_holders = lax.dynamic_index_in_dim(holders, device, 0, keepdims=False)
    my_ranks = lax.dynamic_index_in_dim(ranks, device, 0, keepdims=False)
    send_hit = (
        (my_holders[None, None, :] == jnp.arange(leaf_count, dtype=jnp.int32)[:, None, None])
        & (my_ranks[None, None, :] == slot_ids[None, :, None])
    )
    send_item = jnp.sum(jnp.where(send_hit, jnp.arange(items, dtype=jnp.int32), 0), axis=2)
    send_valid = jnp.any(send_hit, axis=2)
    pick = (
        send_valid[:, :, None] & (send_item[:, :, None] % REQ_DEV == jnp.arange(REQ_DEV))
    ).reshape(leaf_count * all_slots, REQ_DEV)
    outgoing = (
        jnp.dot(pick.astype(jnp.bfloat16), q_blocks, preferred_element_type=jnp.float32)
        .astype(jnp.bfloat16)
        .reshape(leaf_count, all_slots, REQ_LEN, width_local)
    )
    arrived = lax.all_to_all(outgoing, "leaf", split_axis=0, concat_axis=0, tiled=True)
    recv_hit = (holders[:, None, :] == device) & (ranks[:, None, :] == slot_ids[None, :, None])
    slot_nodes = jnp.sum(jnp.where(recv_hit, per_sender[:, None, :], 0), axis=2).reshape(-1)
    filled = jnp.any(recv_hit, axis=2).reshape(-1)
    local_slot = jnp.where(filled, slot_nodes - device * NODE_DEV, 0)
    lengths = jnp.where(filled, len_of(slot_nodes), 0)
    node_out, node_lse = node_attention(
        arrived.reshape(leaf_count * all_slots, REQ_LEN, width_local),
        key_cache,
        value_cache,
        local_slot,
        filled,
        lax.dynamic_slice_in_dim(node_len, device * NODE_DEV, NODE_DEV),
        heads_local,
    )
    slot_count = leaf_count * all_slots
    flat_lse = node_lse.reshape(slot_count, REQ_LEN * heads_local)
    lse_high = lax.reduce_precision(flat_lse, exponent_bits=8, mantissa_bits=7)
    lse_low = flat_lse - lse_high
    pair_width = 2 * REQ_LEN * heads_local
    lse_rows = jnp.pad(
        jnp.concatenate([lse_high, lse_low], axis=1).astype(jnp.bfloat16).reshape(
            leaf_count, all_slots, pair_width
        ),
        ((0, 0), (0, 16 - all_slots), (0, width_local - pair_width)),
    )
    payload = lax.dynamic_update_slice(node_out, lse_rows, (0, all_slots * REQ_LEN, 0))
    back = lax.all_to_all(payload, "leaf", split_axis=0, concat_axis=0, tiled=True)
    got = jnp.take(back, my_holders, axis=0)
    second = (my_ranks == 1)[:, None, None]
    got_out = (
        jnp.where(second, got[:, REQ_LEN : 2 * REQ_LEN], got[:, :REQ_LEN])
        .astype(jnp.float32)
        .reshape(level_count, REQ_DEV, REQ_LEN, heads_local, HD)
    )
    lse_at = all_slots * REQ_LEN
    got_pair = jnp.where(
        second[:, 0], got[:, lse_at + 1, :pair_width], got[:, lse_at, :pair_width]
    ).astype(jnp.float32)
    lse_width = REQ_LEN * heads_local
    got_lse = jnp.swapaxes(
        (got_pair[:, :lse_width] + got_pair[:, lse_width:]).reshape(items, heads_local, REQ_LEN),
        1,
        2,
    ).reshape(level_count, REQ_DEV, REQ_LEN, heads_local)
    partial_out = jnp.concatenate([got_out, self_out[None]], axis=0)
    partial_lse = jnp.concatenate([got_lse, self_lse[None]], axis=0)
    highest = jnp.max(partial_lse, axis=0)
    factor = jnp.exp(partial_lse - highest[None])
    merged = jnp.sum(factor[..., None] * partial_out, axis=0) / jnp.sum(factor, axis=0)[..., None]
    attn = merged.astype(jnp.bfloat16).reshape(tok_rows, width_local)
    partial_value = jnp.dot(attn, w_out, preferred_element_type=jnp.float32)
    projected = lax.psum_scatter(
        partial_value.astype(jnp.bfloat16), "mp", scatter_dimension=1, tiled=True
    ).astype(jnp.float32)
    squares = mp_sum(
        jnp.sum(projected * projected, axis=1).reshape(1, tok_rows), lax.axis_size("mp")
    ).reshape(tok_rows)
    row_scale = lax.rsqrt(squares / D + norm_eps)
    return (
        activations.astype(jnp.float32) + norm_gain[None, :] * projected * row_scale[:, None]
    ).astype(jnp.bfloat16)


def solution(mesh):
    in_specs = (
        P("leaf", "mp"),
        P(None, "mp"),
        P(None, "mp"),
        P(None, "mp"),
        P("mp", None),
        P("mp"),
        P("leaf", None, "mp"),
        P("leaf", None, "mp"),
        P(),
        P(),
        P(),
    )
    out_specs = P("leaf", "mp")
    return jax.shard_map(
        on_device, mesh=mesh, in_specs=in_specs, out_specs=out_specs, check_vma=False
    )
```

```python
import math

import jax
import jax.numpy as jnp
from jax import lax
from jax.experimental import pallas as pl
from jax.experimental.pallas import tpu as pltpu
from jax.sharding import PartitionSpec as P

D = 4096
HD = 128
TENANTS = 4
NODE_DEV = 8
REQ_LEN = 64
REQ_DEV = 4


rope_base = 500000.0
mask_value = -1e30
norm_eps = 1e-06


def rotate(values, positions):
    half_width = values.shape[-1] // 2
    inverse_freq = jnp.exp(
        jnp.arange(half_width, dtype=jnp.float32) * (-2.0 * math.log(rope_base) / values.shape[-1])
    )
    angles = positions.astype(jnp.float32)[:, None] * inverse_freq[None, :]
    cosine = jnp.cos(angles)[:, None, :]
    sine_part = jnp.sin(angles)[:, None, :]
    front_half = values[..., :half_width]
    back_half = values[..., half_width:]
    return jnp.concatenate(
        [front_half * cosine - back_half * sine_part, back_half * cosine + front_half * sine_part],
        axis=-1,
    )


def lookup(table, index):
    hit = index[..., None] == jnp.arange(table.shape[0], dtype=index.dtype)
    return jnp.sum(jnp.where(hit, table, 0), axis=-1).astype(table.dtype)


GROUP = 8


def attend(q, k, v, length, rows, cache_rows):
    live = lax.broadcasted_iota(jnp.int32, (rows, cache_rows), 1) < length
    s = lax.dot_general(
        q, k, (((1,), (1,)), ((), ())), preferred_element_type=jnp.float32
    ) * HD ** (-0.5)
    s = jnp.where(live, s, mask_value)
    m = jnp.max(s, axis=1, keepdims=True)
    p = jnp.exp(s - m)
    l = jnp.sum(p, axis=1, keepdims=True)
    o = jnp.dot(p.astype(jnp.bfloat16), v, preferred_element_type=jnp.float32)
    return o / l, m + jnp.log(l)


CHUNK = 4


def node_kernel(
    perm_ref, start_ref, count_ref, nlen_ref, total_ref, q_ref, k_ref, v_ref, out_ref, lse_ref, qbuf
):
    slots, rows, width = q_ref.shape
    nodes, cache_rows, _ = k_ref.shape
    heads = width // HD
    span = CHUNK * rows

    def per_node(n, carry):
        first = start_ref[n]
        count = count_ref[n]
        length = nlen_ref[n]
        last = first + count - 1

        def per_chunk(c, carry2):
            base = first + c * CHUNK
            picked = [perm_ref[jnp.minimum(base + j, last)] for j in range(CHUNK)]
            for j in range(CHUNK):
                qbuf[pl.ds(j * rows, rows), :] = q_ref[picked[j]]
            lse_cols = []
            for h in range(heads):
                cols = pl.ds(h * HD, HD)
                o, lse = attend(
                    qbuf[:, cols], k_ref[n, :, cols], v_ref[n, :, cols], length, span, cache_rows
                )
                lse_cols.append(lse)
                for j in range(CHUNK):

                    @pl.when(base + j <= last)
                    def _():
                        out_ref[picked[j] // 2, pl.ds(pl.multiple_of(picked[j] % 2 * rows, rows), rows), cols] = (
                            o[j * rows : (j + 1) * rows].astype(out_ref.dtype)
                        )

            lane = lax.broadcasted_iota(jnp.int32, (span, 128), 1)
            lse_tile = jnp.zeros((span, 128), jnp.float32)
            for h in range(heads):
                lse_tile = jnp.where(lane == h, lse_cols[h], lse_tile)
            lse_t = jnp.transpose(lse_tile)
            for j in range(CHUNK):

                @pl.when(base + j <= last)
                def _():
                    for h in range(heads):
                        lse_ref[pl.ds(picked[j], 1), pl.ds(h * rows, rows)] = (
                            lse_t[h : h + 1, j * rows : (j + 1) * rows]
                        )

            return carry2

        lax.fori_loop(0, (count + CHUNK - 1) // CHUNK, per_chunk, 0)
        return carry

    lax.fori_loop(0, nodes, per_node, 0)

    def clear(p, carry):
        slot = perm_ref[p]
        out_ref[slot // 2, pl.ds(pl.multiple_of(slot % 2 * rows, rows), rows), :] = jnp.zeros(
            (rows, width), out_ref.dtype
        )
        lse_ref[pl.ds(slot, 1), :] = jnp.zeros((1, rows * heads), lse_ref.dtype)
        return carry

    lax.fori_loop(total_ref[0], slots, clear, 0)


def node_attention(queries, key_cache, value_cache, local_slot, filled, local_len, heads_local):
    slots, rows, width = queries.shape
    nodes, cache_rows, _ = key_cache.shape
    order_key = jnp.where(filled, local_slot, nodes)
    index = jnp.arange(slots, dtype=jnp.int32)
    before = (order_key[None, :] < order_key[:, None]) | (
        (order_key[None, :] == order_key[:, None]) & (index[None, :] < index[:, None])
    )
    rank = jnp.sum(before, axis=1).astype(jnp.int32)
    perm = jnp.sum(
        jnp.where(rank[None, :] == index[:, None], index[None, :], 0), axis=1
    ).astype(jnp.int32)
    node_ids = jnp.arange(nodes, dtype=jnp.int32)
    count = jnp.sum(filled[None, :] & (local_slot[None, :] == node_ids[:, None]), axis=1).astype(jnp.int32)
    first = jnp.sum(filled[None, :] & (local_slot[None, :] < node_ids[:, None]), axis=1).astype(jnp.int32)
    total = jnp.sum(filled).astype(jnp.int32).reshape(1)
    vmem = pl.BlockSpec(memory_space=pltpu.VMEM)
    smem = pl.BlockSpec(memory_space=pltpu.SMEM)
    flops = 4 * slots * rows * cache_rows * width
    out, lse = pl.pallas_call(
        node_kernel,
        out_shape=(
            jax.ShapeDtypeStruct((slots // 2, 2 * rows + 16, width), jnp.bfloat16),
            jax.ShapeDtypeStruct((slots, rows * heads_local), jnp.float32),
        ),
        in_specs=[smem] * 5 + [vmem] * 3,
        out_specs=(vmem, vmem),
        scratch_shapes=[pltpu.VMEM((CHUNK * rows, width), queries.dtype)],
        cost_estimate=pl.CostEstimate(
            flops=flops,
            transcendentals=slots * rows * cache_rows * heads_local,
            bytes_accessed=2 * queries.size * 2 + 2 * key_cache.size * 2,
        ),
    )(perm, first, count, local_len, total, queries, key_cache, value_cache)
    return out, lse


def sum_kernel(x_ref, out_ref, recv, send_sem, recv_sem):
    n = recv.shape[0]
    me = lax.axis_index("mp")
    barrier = pltpu.get_barrier_semaphore()
    for d in range(1, n):
        pl.semaphore_signal(
            barrier, inc=1, device_id={"mp": lax.rem(me + d, n)},
            device_id_type=pl.DeviceIdType.MESH,
        )
    pl.semaphore_wait(barrier, n - 1)
    copies = []
    for d in range(1, n):
        copy = pltpu.make_async_remote_copy(
            src_ref=x_ref,
            dst_ref=recv.at[d],
            send_sem=send_sem.at[d],
            recv_sem=recv_sem.at[d],
            device_id={"mp": lax.rem(me + d, n)},
            device_id_type=pl.DeviceIdType.MESH,
        )
        copy.start()
        copies.append(copy)
    for copy in copies:
        copy.wait()
    total = x_ref[...]
    for d in range(1, n):
        total = total + recv[d]
    out_ref[...] = total


def mp_sum(x, n):
    vmem = pl.BlockSpec(memory_space=pltpu.VMEM)
    return pl.pallas_call(
        sum_kernel,
        out_shape=jax.ShapeDtypeStruct(x.shape, x.dtype),
        in_specs=[vmem],
        out_specs=vmem,
        scratch_shapes=[
            pltpu.VMEM((n,) + x.shape, x.dtype),
            pltpu.SemaphoreType.DMA((n,)),
            pltpu.SemaphoreType.DMA((n,)),
        ],
        compiler_params=pltpu.CompilerParams(collective_id=0, has_side_effects=True),
    )(x)


def self_attention(queries, keys, values):
    head_dim = queries.shape[-1]
    row_total = queries.shape[1]
    scores = jnp.einsum(
        "rqhd,rkhd->rhqk", queries, keys, preferred_element_type=jnp.float32
    ) * head_dim ** (-0.5)
    causal = jnp.arange(row_total)[:, None] >= jnp.arange(row_total)[None, :]
    scores = jnp.where(causal[None, None], scores, mask_value)
    highest = jnp.max(scores, axis=-1)
    weights = jnp.exp(scores - highest[..., None])
    totals = jnp.sum(weights, axis=-1)
    mixture = jnp.einsum(
        "rhqk,rkhd->rqhd", weights.astype(jnp.bfloat16), values, preferred_element_type=jnp.float32
    )
    return (
        mixture / jnp.transpose(totals, (0, 2, 1))[..., None],
        jnp.transpose(highest + jnp.log(totals), (0, 2, 1)),
    )


def on_device(
    activations,
    w_query,
    w_key,
    w_value,
    w_out,
    norm_gain,
    key_cache,
    value_cache,
    parent,
    node_len,
    req_leaf,
):
    leaf_count = lax.axis_size("leaf")
    device = lax.axis_index("leaf")
    tok_rows = activations.shape[0]
    width_local = w_query.shape[1]
    heads_local = width_local // HD
    spread = leaf_count - TENANTS
    node_slots = 2 * ((REQ_DEV + spread - 1) // spread)
    all_slots = max(REQ_DEV // TENANTS, node_slots)
    block = REQ_LEN * width_local
    columns = lax.all_gather(activations, "mp", axis=1, tiled=True)
    query_f, key_f, value_f = tuple(
        (
            jnp.dot(columns, matrix, preferred_element_type=jnp.float32)
            for matrix in (w_query, w_key, w_value)
        )
    )
    middle_all = lookup(parent, req_leaf)
    root_all = lookup(parent, middle_all)
    len_of = lambda nodes: lookup(node_len, nodes)
    prefix = len_of(root_all) + len_of(middle_all) + len_of(req_leaf)
    mine_prefix = lax.dynamic_slice_in_dim(prefix, device * REQ_DEV, REQ_DEV)
    position = (mine_prefix[:, None] + jnp.arange(REQ_LEN, dtype=jnp.int32)[None, :]).reshape(
        tok_rows
    )
    queries = rotate(query_f.reshape(tok_rows, heads_local, HD), position).astype(jnp.bfloat16)
    keys = rotate(key_f.reshape(tok_rows, heads_local, HD), position).astype(jnp.bfloat16)
    values = value_f.astype(jnp.bfloat16)
    q_blocks = queries.reshape(REQ_DEV, block)
    self_out, self_lse = self_attention(
        queries.reshape(REQ_DEV, REQ_LEN, heads_local, HD),
        keys.reshape(REQ_DEV, REQ_LEN, heads_local, HD),
        values.reshape(REQ_DEV, REQ_LEN, heads_local, HD),
    )
    levels_all = jnp.stack([root_all, middle_all, req_leaf], axis=0).reshape(3, leaf_count, REQ_DEV)
    level_count = levels_all.shape[0]
    items = level_count * REQ_DEV
    per_sender = jnp.transpose(levels_all, (1, 0, 2)).reshape(leaf_count, items)
    holders = per_sender // NODE_DEV
    earlier = jnp.arange(items)[:, None] > jnp.arange(items)[None, :]
    ranks = jnp.sum(
        earlier[None] & (holders[:, :, None] == holders[:, None, :]), axis=2
    ).astype(jnp.int32)
    slot_ids = jnp.arange(all_slots, dtype=jnp.int32)
    my_holders = lax.dynamic_index_in_dim(holders, device, 0, keepdims=False)
    my_ranks = lax.dynamic_index_in_dim(ranks, device, 0, keepdims=False)
    send_hit = (
        (my_holders[None, None, :] == jnp.arange(leaf_count, dtype=jnp.int32)[:, None, None])
        & (my_ranks[None, None, :] == slot_ids[None, :, None])
    )
    send_item = jnp.sum(jnp.where(send_hit, jnp.arange(items, dtype=jnp.int32), 0), axis=2)
    send_valid = jnp.any(send_hit, axis=2)
    pick = (
        send_valid[:, :, None] & (send_item[:, :, None] % REQ_DEV == jnp.arange(REQ_DEV))
    ).reshape(leaf_count * all_slots, REQ_DEV)
    outgoing = jnp.sum(
        jnp.where(
            pick[:, :, None, None],
            q_blocks.reshape(REQ_DEV, REQ_LEN, width_local)[None],
            jnp.zeros((), jnp.bfloat16),
        ),
        axis=1,
    ).reshape(leaf_count, all_slots, REQ_LEN, width_local)
    arrived = lax.all_to_all(outgoing, "leaf", split_axis=0, concat_axis=0, tiled=True)
    recv_hit = (holders[:, None, :] == device) & (ranks[:, None, :] == slot_ids[None, :, None])
    slot_nodes = jnp.sum(jnp.where(recv_hit, per_sender[:, None, :], 0), axis=2).reshape(-1)
    filled = jnp.any(recv_hit, axis=2).reshape(-1)
    local_slot = jnp.where(filled, slot_nodes - device * NODE_DEV, 0)
    lengths = jnp.where(filled, len_of(slot_nodes), 0)
    node_out, node_lse = node_attention(
        arrived.reshape(leaf_count * all_slots, REQ_LEN, width_local),
        key_cache,
        value_cache,
        local_slot,
        filled,
        lax.dynamic_slice_in_dim(node_len, device * NODE_DEV, NODE_DEV),
        heads_local,
    )
    slot_count = leaf_count * all_slots
    flat_lse = node_lse.reshape(slot_count, REQ_LEN * heads_local)
    lse_high = lax.reduce_precision(flat_lse, exponent_bits=8, mantissa_bits=7)
    lse_low = flat_lse - lse_high
    pair_width = 2 * REQ_LEN * heads_local
    lse_rows = jnp.pad(
        jnp.concatenate([lse_high, lse_low], axis=1).astype(jnp.bfloat16).reshape(
            leaf_count, all_slots, pair_width
        ),
        ((0, 0), (0, 16 - all_slots), (0, width_local - pair_width)),
    )
    payload = lax.dynamic_update_slice(node_out, lse_rows, (0, all_slots * REQ_LEN, 0))
    back = lax.all_to_all(payload, "leaf", split_axis=0, concat_axis=0, tiled=True)
    got = jnp.take(back, my_holders, axis=0)
    second = (my_ranks == 1)[:, None, None]
    got_out = (
        jnp.where(second, got[:, REQ_LEN : 2 * REQ_LEN], got[:, :REQ_LEN])
        .astype(jnp.float32)
        .reshape(level_count, REQ_DEV, REQ_LEN, heads_local, HD)
    )
    lse_at = all_slots * REQ_LEN
    got_pair = jnp.where(
        second[:, 0], got[:, lse_at + 1, :pair_width], got[:, lse_at, :pair_width]
    ).astype(jnp.float32)
    lse_width = REQ_LEN * heads_local
    got_lse = jnp.swapaxes(
        (got_pair[:, :lse_width] + got_pair[:, lse_width:]).reshape(items, heads_local, REQ_LEN),
        1,
        2,
    ).reshape(level_count, REQ_DEV, REQ_LEN, heads_local)
    partial_out = jnp.concatenate([got_out, self_out[None]], axis=0)
    partial_lse = jnp.concatenate([got_lse, self_lse[None]], axis=0)
    highest = jnp.max(partial_lse, axis=0)
    factor = jnp.exp(partial_lse - highest[None])
    merged = jnp.sum(factor[..., None] * partial_out, axis=0) / jnp.sum(factor, axis=0)[..., None]
    attn = merged.astype(jnp.bfloat16).reshape(tok_rows, width_local)
    partial_value = jnp.dot(attn, w_out, preferred_element_type=jnp.float32)
    projected = lax.psum_scatter(
        partial_value.astype(jnp.bfloat16), "mp", scatter_dimension=1, tiled=True
    ).astype(jnp.float32)
    squares = mp_sum(
        jnp.sum(projected * projected, axis=1).reshape(1, tok_rows), lax.axis_size("mp")
    ).reshape(tok_rows)
    row_scale = lax.rsqrt(squares / D + norm_eps)
    return (
        activations.astype(jnp.float32) + norm_gain[None, :] * projected * row_scale[:, None]
    ).astype(jnp.bfloat16)


def solution(mesh):
    in_specs = (
        P("leaf", "mp"),
        P(None, "mp"),
        P(None, "mp"),
        P(None, "mp"),
        P("mp", None),
        P("mp"),
        P("leaf", None, "mp"),
        P("leaf", None, "mp"),
        P(),
        P(),
        P(),
    )
    out_specs = P("leaf", "mp")
    return jax.shard_map(
        on_device, mesh=mesh, in_specs=in_specs, out_specs=out_specs, check_vma=False
    )
```

```python
import math

import jax
import jax.numpy as jnp
from jax import lax
from jax.experimental import pallas as pl
from jax.experimental.pallas import tpu as pltpu
from jax.sharding import PartitionSpec as P

D = 4096
HD = 128
TENANTS = 4
NODE_DEV = 8
REQ_LEN = 64
REQ_DEV = 4


rope_base = 500000.0
mask_value = -1e30
norm_eps = 1e-06


def rotate(values, positions):
    half_width = values.shape[-1] // 2
    inverse_freq = jnp.exp(
        jnp.arange(half_width, dtype=jnp.float32) * (-2.0 * math.log(rope_base) / values.shape[-1])
    )
    angles = positions.astype(jnp.float32)[:, None] * inverse_freq[None, :]
    cosine = jnp.cos(angles)[:, None, :]
    sine_part = jnp.sin(angles)[:, None, :]
    front_half = values[..., :half_width]
    back_half = values[..., half_width:]
    return jnp.concatenate(
        [front_half * cosine - back_half * sine_part, back_half * cosine + front_half * sine_part],
        axis=-1,
    )


def lookup(table, index):
    hit = index[..., None] == jnp.arange(table.shape[0], dtype=index.dtype)
    return jnp.sum(jnp.where(hit, table, 0), axis=-1).astype(table.dtype)


GROUP = 8


def attend(q, k, v, length, rows, cache_rows):
    live = lax.broadcasted_iota(jnp.int32, (rows, cache_rows), 1) < length
    s = lax.dot_general(
        q, k, (((1,), (1,)), ((), ())), preferred_element_type=jnp.float32
    ) * HD ** (-0.5)
    s = jnp.where(live, s, mask_value)
    m = jnp.max(s, axis=1, keepdims=True)
    p = jnp.exp(s - m)
    l = jnp.sum(p, axis=1, keepdims=True)
    o = jnp.dot(p.astype(jnp.bfloat16), v, preferred_element_type=jnp.float32)
    return o / l, m + jnp.log(l)


CHUNK = 4


def node_kernel(
    perm_ref, start_ref, count_ref, nlen_ref, total_ref, q_ref, k_ref, v_ref, out_ref, lse_ref, qbuf
):
    slots, rows, width = q_ref.shape
    nodes, cache_rows, _ = k_ref.shape
    heads = width // HD
    span = CHUNK * rows

    def per_node(n, carry):
        first = start_ref[n]
        count = count_ref[n]
        length = nlen_ref[n]
        last = first + count - 1

        def per_chunk(c, carry2):
            base = first + c * CHUNK
            picked = [perm_ref[jnp.minimum(base + j, last)] for j in range(CHUNK)]
            for j in range(CHUNK):
                qbuf[pl.ds(j * rows, rows), :] = q_ref[picked[j]]
            lse_cols = []
            for h in range(heads):
                cols = pl.ds(h * HD, HD)
                o, lse = attend(
                    qbuf[:, cols], k_ref[n, :, cols], v_ref[n, :, cols], length, span, cache_rows
                )
                lse_cols.append(lse)
                for j in range(CHUNK):

                    @pl.when(base + j <= last)
                    def _():
                        out_ref[picked[j] // 2, pl.ds(pl.multiple_of(picked[j] % 2 * rows, rows), rows), cols] = (
                            o[j * rows : (j + 1) * rows].astype(out_ref.dtype)
                        )

            lane = lax.broadcasted_iota(jnp.int32, (span, 128), 1)
            lse_tile = jnp.zeros((span, 128), jnp.float32)
            for h in range(heads):
                lse_tile = jnp.where(lane == h, lse_cols[h], lse_tile)
            lse_t = jnp.transpose(lse_tile)
            for j in range(CHUNK):

                @pl.when(base + j <= last)
                def _():
                    for h in range(heads):
                        lse_ref[pl.ds(picked[j], 1), pl.ds(h * rows, rows)] = (
                            lse_t[h : h + 1, j * rows : (j + 1) * rows]
                        )

            return carry2

        lax.fori_loop(0, (count + CHUNK - 1) // CHUNK, per_chunk, 0)
        return carry

    lax.fori_loop(0, nodes, per_node, 0)

    def clear(p, carry):
        slot = perm_ref[p]
        out_ref[slot // 2, pl.ds(pl.multiple_of(slot % 2 * rows, rows), rows), :] = jnp.zeros(
            (rows, width), out_ref.dtype
        )
        lse_ref[pl.ds(slot, 1), :] = jnp.zeros((1, rows * heads), lse_ref.dtype)
        return carry

    lax.fori_loop(total_ref[0], slots, clear, 0)


def node_attention(queries, key_cache, value_cache, local_slot, filled, local_len, heads_local):
    slots, rows, width = queries.shape
    nodes, cache_rows, _ = key_cache.shape
    order_key = jnp.where(filled, local_slot, nodes)
    index = jnp.arange(slots, dtype=jnp.int32)
    before = (order_key[None, :] < order_key[:, None]) | (
        (order_key[None, :] == order_key[:, None]) & (index[None, :] < index[:, None])
    )
    rank = jnp.sum(before, axis=1).astype(jnp.int32)
    perm = jnp.sum(
        jnp.where(rank[None, :] == index[:, None], index[None, :], 0), axis=1
    ).astype(jnp.int32)
    node_ids = jnp.arange(nodes, dtype=jnp.int32)
    count = jnp.sum(filled[None, :] & (local_slot[None, :] == node_ids[:, None]), axis=1).astype(jnp.int32)
    first = jnp.sum(filled[None, :] & (local_slot[None, :] < node_ids[:, None]), axis=1).astype(jnp.int32)
    total = jnp.sum(filled).astype(jnp.int32).reshape(1)
    vmem = pl.BlockSpec(memory_space=pltpu.VMEM)
    smem = pl.BlockSpec(memory_space=pltpu.SMEM)
    flops = 4 * slots * rows * cache_rows * width
    out, lse = pl.pallas_call(
        node_kernel,
        out_shape=(
            jax.ShapeDtypeStruct((slots // 2, 2 * rows + 16, width), jnp.bfloat16),
            jax.ShapeDtypeStruct((slots, rows * heads_local), jnp.float32),
        ),
        in_specs=[smem] * 5 + [vmem] * 3,
        out_specs=(vmem, vmem),
        scratch_shapes=[pltpu.VMEM((CHUNK * rows, width), queries.dtype)],
        cost_estimate=pl.CostEstimate(
            flops=flops,
            transcendentals=slots * rows * cache_rows * heads_local,
            bytes_accessed=2 * queries.size * 2 + 2 * key_cache.size * 2,
        ),
    )(perm, first, count, local_len, total, queries, key_cache, value_cache)
    return out, lse


def sum_kernel(x_ref, out_ref, recv, send_sem, recv_sem):
    n = recv.shape[0]
    me = lax.axis_index("mp")
    barrier = pltpu.get_barrier_semaphore()
    for d in range(1, n):
        pl.semaphore_signal(
            barrier, inc=1, device_id={"mp": lax.rem(me + d, n)},
            device_id_type=pl.DeviceIdType.MESH,
        )
    pl.semaphore_wait(barrier, n - 1)
    copies = []
    for d in range(1, n):
        copy = pltpu.make_async_remote_copy(
            src_ref=x_ref,
            dst_ref=recv.at[d],
            send_sem=send_sem.at[d],
            recv_sem=recv_sem.at[d],
            device_id={"mp": lax.rem(me + d, n)},
            device_id_type=pl.DeviceIdType.MESH,
        )
        copy.start()
        copies.append(copy)
    for copy in copies:
        copy.wait()
    total = x_ref[...]
    for d in range(1, n):
        total = total + recv[d]
    out_ref[...] = total


def mp_sum(x, n):
    vmem = pl.BlockSpec(memory_space=pltpu.VMEM)
    return pl.pallas_call(
        sum_kernel,
        out_shape=jax.ShapeDtypeStruct(x.shape, x.dtype),
        in_specs=[vmem],
        out_specs=vmem,
        scratch_shapes=[
            pltpu.VMEM((n,) + x.shape, x.dtype),
            pltpu.SemaphoreType.DMA((n,)),
            pltpu.SemaphoreType.DMA((n,)),
        ],
        compiler_params=pltpu.CompilerParams(collective_id=0, has_side_effects=True),
    )(x)


def self_attention(queries, keys, values):
    head_dim = queries.shape[-1]
    row_total = queries.shape[1]
    scores = jnp.einsum(
        "rqhd,rkhd->rhqk", queries, keys, preferred_element_type=jnp.float32
    ) * head_dim ** (-0.5)
    causal = jnp.arange(row_total)[:, None] >= jnp.arange(row_total)[None, :]
    scores = jnp.where(causal[None, None], scores, mask_value)
    highest = jnp.max(scores, axis=-1)
    weights = jnp.exp(scores - highest[..., None])
    totals = jnp.sum(weights, axis=-1)
    mixture = jnp.einsum(
        "rhqk,rkhd->rqhd", weights.astype(jnp.bfloat16), values, preferred_element_type=jnp.float32
    )
    return (
        mixture / jnp.transpose(totals, (0, 2, 1))[..., None],
        jnp.transpose(highest + jnp.log(totals), (0, 2, 1)),
    )


def on_device(
    activations,
    w_query,
    w_key,
    w_value,
    w_out,
    norm_gain,
    key_cache,
    value_cache,
    parent,
    node_len,
    req_leaf,
):
    leaf_count = lax.axis_size("leaf")
    device = lax.axis_index("leaf")
    tok_rows = activations.shape[0]
    width_local = w_query.shape[1]
    heads_local = width_local // HD
    spread = leaf_count - TENANTS
    node_slots = 2 * ((REQ_DEV + spread - 1) // spread)
    all_slots = max(REQ_DEV // TENANTS, node_slots)
    block = REQ_LEN * width_local
    columns = lax.all_gather(activations, "mp", axis=1, tiled=True)
    query_f, key_f, value_f = tuple(
        (
            jnp.dot(columns, matrix, preferred_element_type=jnp.float32)
            for matrix in (w_query, w_key, w_value)
        )
    )
    middle_all = lookup(parent, req_leaf)
    root_all = lookup(parent, middle_all)
    len_of = lambda nodes: lookup(node_len, nodes)
    prefix = len_of(root_all) + len_of(middle_all) + len_of(req_leaf)
    mine_prefix = lax.dynamic_slice_in_dim(prefix, device * REQ_DEV, REQ_DEV)
    position = (mine_prefix[:, None] + jnp.arange(REQ_LEN, dtype=jnp.int32)[None, :]).reshape(
        tok_rows
    )
    queries = rotate(query_f.reshape(tok_rows, heads_local, HD), position).astype(jnp.bfloat16)
    keys = rotate(key_f.reshape(tok_rows, heads_local, HD), position).astype(jnp.bfloat16)
    values = value_f.astype(jnp.bfloat16)
    q_blocks = queries.reshape(REQ_DEV, block)
    self_out, self_lse = self_attention(
        queries.reshape(REQ_DEV, REQ_LEN, heads_local, HD),
        keys.reshape(REQ_DEV, REQ_LEN, heads_local, HD),
        values.reshape(REQ_DEV, REQ_LEN, heads_local, HD),
    )
    levels_all = jnp.stack([root_all, middle_all, req_leaf], axis=0).reshape(3, leaf_count, REQ_DEV)
    level_count = levels_all.shape[0]
    items = level_count * REQ_DEV
    per_sender = jnp.transpose(levels_all, (1, 0, 2)).reshape(leaf_count, items)
    holders = per_sender // NODE_DEV
    earlier = jnp.arange(items)[:, None] > jnp.arange(items)[None, :]
    ranks = jnp.sum(
        earlier[None] & (holders[:, :, None] == holders[:, None, :]), axis=2
    ).astype(jnp.int32)
    slot_ids = jnp.arange(all_slots, dtype=jnp.int32)
    my_holders = lax.dynamic_index_in_dim(holders, device, 0, keepdims=False)
    my_ranks = lax.dynamic_index_in_dim(ranks, device, 0, keepdims=False)
    send_hit = (
        (my_holders[None, None, :] == jnp.arange(leaf_count, dtype=jnp.int32)[:, None, None])
        & (my_ranks[None, None, :] == slot_ids[None, :, None])
    )
    send_item = jnp.sum(jnp.where(send_hit, jnp.arange(items, dtype=jnp.int32), 0), axis=2)
    send_valid = jnp.any(send_hit, axis=2)
    pick = (
        send_valid[:, :, None] & (send_item[:, :, None] % REQ_DEV == jnp.arange(REQ_DEV))
    ).reshape(leaf_count * all_slots, REQ_DEV)
    outgoing = (
        jnp.take(
            q_blocks.reshape(REQ_DEV, REQ_LEN, width_local),
            (send_item % REQ_DEV).reshape(-1),
            axis=0,
        )
        * send_valid.reshape(-1, 1, 1).astype(jnp.bfloat16)
    ).reshape(leaf_count, all_slots, REQ_LEN, width_local)
    arrived = lax.all_to_all(outgoing, "leaf", split_axis=0, concat_axis=0, tiled=True)
    recv_hit = (holders[:, None, :] == device) & (ranks[:, None, :] == slot_ids[None, :, None])
    slot_nodes = jnp.sum(jnp.where(recv_hit, per_sender[:, None, :], 0), axis=2).reshape(-1)
    filled = jnp.any(recv_hit, axis=2).reshape(-1)
    local_slot = jnp.where(filled, slot_nodes - device * NODE_DEV, 0)
    lengths = jnp.where(filled, len_of(slot_nodes), 0)
    node_out, node_lse = node_attention(
        arrived.reshape(leaf_count * all_slots, REQ_LEN, width_local),
        key_cache,
        value_cache,
        local_slot,
        filled,
        lax.dynamic_slice_in_dim(node_len, device * NODE_DEV, NODE_DEV),
        heads_local,
    )
    slot_count = leaf_count * all_slots
    flat_lse = node_lse.reshape(slot_count, REQ_LEN * heads_local)
    lse_high = lax.reduce_precision(flat_lse, exponent_bits=8, mantissa_bits=7)
    lse_low = flat_lse - lse_high
    pair_width = 2 * REQ_LEN * heads_local
    lse_rows = jnp.pad(
        jnp.concatenate([lse_high, lse_low], axis=1).astype(jnp.bfloat16).reshape(
            leaf_count, all_slots, pair_width
        ),
        ((0, 0), (0, 16 - all_slots), (0, width_local - pair_width)),
    )
    payload = lax.dynamic_update_slice(node_out, lse_rows, (0, all_slots * REQ_LEN, 0))
    back = lax.all_to_all(payload, "leaf", split_axis=0, concat_axis=0, tiled=True)
    got = jnp.take(back, my_holders, axis=0)
    second = (my_ranks == 1)[:, None, None]
    got_out = (
        jnp.where(second, got[:, REQ_LEN : 2 * REQ_LEN], got[:, :REQ_LEN])
        .astype(jnp.float32)
        .reshape(level_count, REQ_DEV, REQ_LEN, heads_local, HD)
    )
    lse_at = all_slots * REQ_LEN
    got_pair = jnp.where(
        second[:, 0], got[:, lse_at + 1, :pair_width], got[:, lse_at, :pair_width]
    ).astype(jnp.float32)
    lse_width = REQ_LEN * heads_local
    got_lse = jnp.swapaxes(
        (got_pair[:, :lse_width] + got_pair[:, lse_width:]).reshape(items, heads_local, REQ_LEN),
        1,
        2,
    ).reshape(level_count, REQ_DEV, REQ_LEN, heads_local)
    partial_out = jnp.concatenate([got_out, self_out[None]], axis=0)
    partial_lse = jnp.concatenate([got_lse, self_lse[None]], axis=0)
    highest = jnp.max(partial_lse, axis=0)
    factor = jnp.exp(partial_lse - highest[None])
    merged = jnp.sum(factor[..., None] * partial_out, axis=0) / jnp.sum(factor, axis=0)[..., None]
    attn = merged.astype(jnp.bfloat16).reshape(tok_rows, width_local)
    partial_value = jnp.dot(attn, w_out, preferred_element_type=jnp.float32)
    projected = lax.psum_scatter(
        partial_value.astype(jnp.bfloat16), "mp", scatter_dimension=1, tiled=True
    ).astype(jnp.float32)
    squares = mp_sum(
        jnp.sum(projected * projected, axis=1).reshape(1, tok_rows), lax.axis_size("mp")
    ).reshape(tok_rows)
    row_scale = lax.rsqrt(squares / D + norm_eps)
    return (
        activations.astype(jnp.float32) + norm_gain[None, :] * projected * row_scale[:, None]
    ).astype(jnp.bfloat16)


def solution(mesh):
    in_specs = (
        P("leaf", "mp"),
        P(None, "mp"),
        P(None, "mp"),
        P(None, "mp"),
        P("mp", None),
        P("mp"),
        P("leaf", None, "mp"),
        P("leaf", None, "mp"),
        P(),
        P(),
        P(),
    )
    out_specs = P("leaf", "mp")
    return jax.shard_map(
        on_device, mesh=mesh, in_specs=in_specs, out_specs=out_specs, check_vma=False
    )
```

```python
import math

import jax
import jax.numpy as jnp
from jax import lax
from jax.experimental import pallas as pl
from jax.experimental.pallas import tpu as pltpu
from jax.sharding import PartitionSpec as P

D = 4096
HD = 128
TENANTS = 4
NODE_DEV = 8
REQ_LEN = 64
REQ_DEV = 4


rope_base = 500000.0
mask_value = -1e30
norm_eps = 1e-06


def rotate(values, positions):
    half_width = values.shape[-1] // 2
    inverse_freq = jnp.exp(
        jnp.arange(half_width, dtype=jnp.float32) * (-2.0 * math.log(rope_base) / values.shape[-1])
    )
    angles = positions.astype(jnp.float32)[:, None] * inverse_freq[None, :]
    cosine = jnp.cos(angles)[:, None, :]
    sine_part = jnp.sin(angles)[:, None, :]
    front_half = values[..., :half_width]
    back_half = values[..., half_width:]
    return jnp.concatenate(
        [front_half * cosine - back_half * sine_part, back_half * cosine + front_half * sine_part],
        axis=-1,
    )


def lookup(table, index):
    hit = index[..., None] == jnp.arange(table.shape[0], dtype=index.dtype)
    return jnp.sum(jnp.where(hit, table, 0), axis=-1).astype(table.dtype)


GROUP = 8


def attend(q, k, v, length, rows, cache_rows):
    live = lax.broadcasted_iota(jnp.int32, (rows, cache_rows), 1) < length
    s = lax.dot_general(
        q, k, (((1,), (1,)), ((), ())), preferred_element_type=jnp.float32
    ) * HD ** (-0.5)
    s = jnp.where(live, s, mask_value)
    m = jnp.max(s, axis=1, keepdims=True)
    p = jnp.exp(s - m)
    l = jnp.sum(p, axis=1, keepdims=True)
    o = jnp.dot(p.astype(jnp.bfloat16), v, preferred_element_type=jnp.float32)
    return o / l, m + jnp.log(l)


CHUNK = 4


def node_kernel(
    perm_ref, start_ref, count_ref, nlen_ref, total_ref, q_ref, k_ref, v_ref, out_ref, lse_ref, qbuf
):
    slots, rows, width = q_ref.shape
    nodes, cache_rows, _ = k_ref.shape
    heads = width // HD
    span = CHUNK * rows

    def per_node(n, carry):
        first = start_ref[n]
        count = count_ref[n]
        length = nlen_ref[n]
        last = first + count - 1

        def per_chunk(c, carry2):
            base = first + c * CHUNK
            picked = [perm_ref[jnp.minimum(base + j, last)] for j in range(CHUNK)]
            for j in range(CHUNK):
                qbuf[pl.ds(j * rows, rows), :] = q_ref[picked[j]]
            lse_cols = []
            for h in range(heads):
                cols = pl.ds(h * HD, HD)
                o, lse = attend(
                    qbuf[:, cols], k_ref[n, :, cols], v_ref[n, :, cols], length, span, cache_rows
                )
                lse_cols.append(lse)
                for j in range(CHUNK):

                    @pl.when(base + j <= last)
                    def _():
                        out_ref[picked[j] // 2, pl.ds(pl.multiple_of(picked[j] % 2 * rows, rows), rows), cols] = (
                            o[j * rows : (j + 1) * rows].astype(out_ref.dtype)
                        )

            lane = lax.broadcasted_iota(jnp.int32, (span, 128), 1)
            lse_tile = jnp.zeros((span, 128), jnp.float32)
            for h in range(heads):
                lse_tile = jnp.where(lane == h, lse_cols[h], lse_tile)
            lse_t = jnp.transpose(lse_tile)
            for j in range(CHUNK):

                @pl.when(base + j <= last)
                def _():
                    for h in range(heads):
                        lse_ref[pl.ds(picked[j], 1), pl.ds(h * rows, rows)] = (
                            lse_t[h : h + 1, j * rows : (j + 1) * rows]
                        )

            return carry2

        lax.fori_loop(0, (count + CHUNK - 1) // CHUNK, per_chunk, 0)
        return carry

    lax.fori_loop(0, nodes, per_node, 0)

    def clear(p, carry):
        slot = perm_ref[p]
        out_ref[slot // 2, pl.ds(pl.multiple_of(slot % 2 * rows, rows), rows), :] = jnp.zeros(
            (rows, width), out_ref.dtype
        )
        lse_ref[pl.ds(slot, 1), :] = jnp.zeros((1, rows * heads), lse_ref.dtype)
        return carry

    lax.fori_loop(total_ref[0], slots, clear, 0)


def node_attention(queries, key_cache, value_cache, local_slot, filled, local_len, heads_local):
    slots, rows, width = queries.shape
    nodes, cache_rows, _ = key_cache.shape
    order_key = jnp.where(filled, local_slot, nodes)
    index = jnp.arange(slots, dtype=jnp.int32)
    before = (order_key[None, :] < order_key[:, None]) | (
        (order_key[None, :] == order_key[:, None]) & (index[None, :] < index[:, None])
    )
    rank = jnp.sum(before, axis=1).astype(jnp.int32)
    perm = jnp.sum(
        jnp.where(rank[None, :] == index[:, None], index[None, :], 0), axis=1
    ).astype(jnp.int32)
    node_ids = jnp.arange(nodes, dtype=jnp.int32)
    count = jnp.sum(filled[None, :] & (local_slot[None, :] == node_ids[:, None]), axis=1).astype(jnp.int32)
    first = jnp.sum(filled[None, :] & (local_slot[None, :] < node_ids[:, None]), axis=1).astype(jnp.int32)
    total = jnp.sum(filled).astype(jnp.int32).reshape(1)
    vmem = pl.BlockSpec(memory_space=pltpu.VMEM)
    smem = pl.BlockSpec(memory_space=pltpu.SMEM)
    flops = 4 * slots * rows * cache_rows * width
    out, lse = pl.pallas_call(
        node_kernel,
        out_shape=(
            jax.ShapeDtypeStruct((slots // 2, 2 * rows + 16, width), jnp.bfloat16),
            jax.ShapeDtypeStruct((slots, rows * heads_local), jnp.float32),
        ),
        in_specs=[smem] * 5 + [vmem] * 3,
        out_specs=(vmem, vmem),
        scratch_shapes=[pltpu.VMEM((CHUNK * rows, width), queries.dtype)],
        cost_estimate=pl.CostEstimate(
            flops=flops,
            transcendentals=slots * rows * cache_rows * heads_local,
            bytes_accessed=2 * queries.size * 2 + 2 * key_cache.size * 2,
        ),
    )(perm, first, count, local_len, total, queries, key_cache, value_cache)
    return out, lse


def norm_kernel(x_ref, proj_ref, act_ref, gain_ref, out_ref, recv, send_sem, recv_sem):
    n = recv.shape[0]
    me = lax.axis_index("mp")
    barrier = pltpu.get_barrier_semaphore()
    for d in range(1, n):
        pl.semaphore_signal(
            barrier, inc=1, device_id={"mp": lax.rem(me + d, n)},
            device_id_type=pl.DeviceIdType.MESH,
        )
    pl.semaphore_wait(barrier, n - 1)
    copies = []
    for d in range(1, n):
        copy = pltpu.make_async_remote_copy(
            src_ref=x_ref,
            dst_ref=recv.at[d],
            send_sem=send_sem.at[d],
            recv_sem=recv_sem.at[d],
            device_id={"mp": lax.rem(me + d, n)},
            device_id_type=pl.DeviceIdType.MESH,
        )
        copy.start()
        copies.append(copy)
    for copy in copies:
        copy.wait()
    total = x_ref[...]
    for d in range(1, n):
        total = total + recv[d]
    scale_row = lax.rsqrt(total / D + norm_eps)
    scale = jnp.transpose(jnp.broadcast_to(scale_row, (128, scale_row.shape[1])))[:, 0:1]
    out_ref[...] = (
        act_ref[...].astype(jnp.float32) + gain_ref[...] * proj_ref[...] * scale
    ).astype(out_ref.dtype)


def mp_norm(x, projected, activations, gain, n):
    vmem = pl.BlockSpec(memory_space=pltpu.VMEM)
    return pl.pallas_call(
        norm_kernel,
        out_shape=jax.ShapeDtypeStruct(activations.shape, activations.dtype),
        in_specs=[vmem] * 4,
        out_specs=vmem,
        scratch_shapes=[
            pltpu.VMEM((n,) + x.shape, x.dtype),
            pltpu.SemaphoreType.DMA((n,)),
            pltpu.SemaphoreType.DMA((n,)),
        ],
        compiler_params=pltpu.CompilerParams(collective_id=0, has_side_effects=True),
    )(x, projected, activations, gain)


def mp_sum(x, n):
    vmem = pl.BlockSpec(memory_space=pltpu.VMEM)
    return pl.pallas_call(
        sum_kernel,
        out_shape=jax.ShapeDtypeStruct(x.shape, x.dtype),
        in_specs=[vmem],
        out_specs=vmem,
        scratch_shapes=[
            pltpu.VMEM((n,) + x.shape, x.dtype),
            pltpu.SemaphoreType.DMA((n,)),
            pltpu.SemaphoreType.DMA((n,)),
        ],
        compiler_params=pltpu.CompilerParams(collective_id=0, has_side_effects=True),
    )(x)


def self_attention(queries, keys, values):
    head_dim = queries.shape[-1]
    row_total = queries.shape[1]
    scores = jnp.einsum(
        "rqhd,rkhd->rhqk", queries, keys, preferred_element_type=jnp.float32
    ) * head_dim ** (-0.5)
    causal = jnp.arange(row_total)[:, None] >= jnp.arange(row_total)[None, :]
    scores = jnp.where(causal[None, None], scores, mask_value)
    highest = jnp.max(scores, axis=-1)
    weights = jnp.exp(scores - highest[..., None])
    totals = jnp.sum(weights, axis=-1)
    mixture = jnp.einsum(
        "rhqk,rkhd->rqhd", weights.astype(jnp.bfloat16), values, preferred_element_type=jnp.float32
    )
    return (
        mixture / jnp.transpose(totals, (0, 2, 1))[..., None],
        jnp.transpose(highest + jnp.log(totals), (0, 2, 1)),
    )


def on_device(
    activations,
    w_query,
    w_key,
    w_value,
    w_out,
    norm_gain,
    key_cache,
    value_cache,
    parent,
    node_len,
    req_leaf,
):
    leaf_count = lax.axis_size("leaf")
    device = lax.axis_index("leaf")
    tok_rows = activations.shape[0]
    width_local = w_query.shape[1]
    heads_local = width_local // HD
    spread = leaf_count - TENANTS
    node_slots = 2 * ((REQ_DEV + spread - 1) // spread)
    all_slots = max(REQ_DEV // TENANTS, node_slots)
    block = REQ_LEN * width_local
    columns = lax.all_gather(activations, "mp", axis=1, tiled=True)
    query_f, key_f, value_f = tuple(
        (
            jnp.dot(columns, matrix, preferred_element_type=jnp.float32)
            for matrix in (w_query, w_key, w_value)
        )
    )
    middle_all = lookup(parent, req_leaf)
    root_all = lookup(parent, middle_all)
    len_of = lambda nodes: lookup(node_len, nodes)
    prefix = len_of(root_all) + len_of(middle_all) + len_of(req_leaf)
    mine_prefix = lax.dynamic_slice_in_dim(prefix, device * REQ_DEV, REQ_DEV)
    position = (mine_prefix[:, None] + jnp.arange(REQ_LEN, dtype=jnp.int32)[None, :]).reshape(
        tok_rows
    )
    queries = rotate(query_f.reshape(tok_rows, heads_local, HD), position).astype(jnp.bfloat16)
    keys = rotate(key_f.reshape(tok_rows, heads_local, HD), position).astype(jnp.bfloat16)
    values = value_f.astype(jnp.bfloat16)
    q_blocks = queries.reshape(REQ_DEV, block)
    self_out, self_lse = self_attention(
        queries.reshape(REQ_DEV, REQ_LEN, heads_local, HD),
        keys.reshape(REQ_DEV, REQ_LEN, heads_local, HD),
        values.reshape(REQ_DEV, REQ_LEN, heads_local, HD),
    )
    levels_all = jnp.stack([root_all, middle_all, req_leaf], axis=0).reshape(3, leaf_count, REQ_DEV)
    level_count = levels_all.shape[0]
    items = level_count * REQ_DEV
    per_sender = jnp.transpose(levels_all, (1, 0, 2)).reshape(leaf_count, items)
    holders = per_sender // NODE_DEV
    earlier = jnp.arange(items)[:, None] > jnp.arange(items)[None, :]
    ranks = jnp.sum(
        earlier[None] & (holders[:, :, None] == holders[:, None, :]), axis=2
    ).astype(jnp.int32)
    slot_ids = jnp.arange(all_slots, dtype=jnp.int32)
    my_holders = lax.dynamic_index_in_dim(holders, device, 0, keepdims=False)
    my_ranks = lax.dynamic_index_in_dim(ranks, device, 0, keepdims=False)
    send_hit = (
        (my_holders[None, None, :] == jnp.arange(leaf_count, dtype=jnp.int32)[:, None, None])
        & (my_ranks[None, None, :] == slot_ids[None, :, None])
    )
    send_item = jnp.sum(jnp.where(send_hit, jnp.arange(items, dtype=jnp.int32), 0), axis=2)
    send_valid = jnp.any(send_hit, axis=2)
    pick = (
        send_valid[:, :, None] & (send_item[:, :, None] % REQ_DEV == jnp.arange(REQ_DEV))
    ).reshape(leaf_count * all_slots, REQ_DEV)
    outgoing = jnp.sum(
        jnp.where(
            pick[:, :, None, None],
            q_blocks.reshape(REQ_DEV, REQ_LEN, width_local)[None],
            jnp.zeros((), jnp.bfloat16),
        ),
        axis=1,
    ).reshape(leaf_count, all_slots, REQ_LEN, width_local)
    arrived = lax.all_to_all(outgoing, "leaf", split_axis=0, concat_axis=0, tiled=True)
    recv_hit = (holders[:, None, :] == device) & (ranks[:, None, :] == slot_ids[None, :, None])
    slot_nodes = jnp.sum(jnp.where(recv_hit, per_sender[:, None, :], 0), axis=2).reshape(-1)
    filled = jnp.any(recv_hit, axis=2).reshape(-1)
    local_slot = jnp.where(filled, slot_nodes - device * NODE_DEV, 0)
    lengths = jnp.where(filled, len_of(slot_nodes), 0)
    node_out, node_lse = node_attention(
        arrived.reshape(leaf_count * all_slots, REQ_LEN, width_local),
        key_cache,
        value_cache,
        local_slot,
        filled,
        lax.dynamic_slice_in_dim(node_len, device * NODE_DEV, NODE_DEV),
        heads_local,
    )
    slot_count = leaf_count * all_slots
    flat_lse = node_lse.reshape(slot_count, REQ_LEN * heads_local)
    lse_high = lax.reduce_precision(flat_lse, exponent_bits=8, mantissa_bits=7)
    lse_low = flat_lse - lse_high
    pair_width = 2 * REQ_LEN * heads_local
    lse_rows = jnp.pad(
        jnp.concatenate([lse_high, lse_low], axis=1).astype(jnp.bfloat16).reshape(
            leaf_count, all_slots, pair_width
        ),
        ((0, 0), (0, 16 - all_slots), (0, width_local - pair_width)),
    )
    payload = lax.dynamic_update_slice(node_out, lse_rows, (0, all_slots * REQ_LEN, 0))
    back = lax.all_to_all(payload, "leaf", split_axis=0, concat_axis=0, tiled=True)
    got = jnp.take(back, my_holders, axis=0)
    second = (my_ranks == 1)[:, None, None]
    got_out = (
        jnp.where(second, got[:, REQ_LEN : 2 * REQ_LEN], got[:, :REQ_LEN])
        .astype(jnp.float32)
        .reshape(level_count, REQ_DEV, REQ_LEN, heads_local, HD)
    )
    lse_at = all_slots * REQ_LEN
    got_pair = jnp.where(
        second[:, 0], got[:, lse_at + 1, :pair_width], got[:, lse_at, :pair_width]
    ).astype(jnp.float32)
    lse_width = REQ_LEN * heads_local
    got_lse = jnp.swapaxes(
        (got_pair[:, :lse_width] + got_pair[:, lse_width:]).reshape(items, heads_local, REQ_LEN),
        1,
        2,
    ).reshape(level_count, REQ_DEV, REQ_LEN, heads_local)
    partial_out = jnp.concatenate([got_out, self_out[None]], axis=0)
    partial_lse = jnp.concatenate([got_lse, self_lse[None]], axis=0)
    highest = jnp.max(partial_lse, axis=0)
    factor = jnp.exp(partial_lse - highest[None])
    merged = jnp.sum(factor[..., None] * partial_out, axis=0) / jnp.sum(factor, axis=0)[..., None]
    attn = merged.astype(jnp.bfloat16).reshape(tok_rows, width_local)
    partial_value = jnp.dot(attn, w_out, preferred_element_type=jnp.float32)
    projected = lax.psum_scatter(
        partial_value.astype(jnp.bfloat16), "mp", scatter_dimension=1, tiled=True
    ).astype(jnp.float32)
    return mp_norm(
        jnp.sum(projected * projected, axis=1).reshape(1, tok_rows),
        projected,
        activations,
        norm_gain.reshape(1, -1),
        lax.axis_size("mp"),
    )


def solution(mesh):
    in_specs = (
        P("leaf", "mp"),
        P(None, "mp"),
        P(None, "mp"),
        P(None, "mp"),
        P("mp", None),
        P("mp"),
        P("leaf", None, "mp"),
        P("leaf", None, "mp"),
        P(),
        P(),
        P(),
    )
    out_specs = P("leaf", "mp")
    return jax.shard_map(
        on_device, mesh=mesh, in_specs=in_specs, out_specs=out_specs, check_vma=False
    )
```

```python
import math

import jax
import jax.numpy as jnp
from jax import lax
from jax.experimental import pallas as pl
from jax.experimental.pallas import tpu as pltpu
from jax.sharding import PartitionSpec as P

D = 4096
HD = 128
TENANTS = 4
NODE_DEV = 8
REQ_LEN = 64
REQ_DEV = 4


rope_base = 500000.0
mask_value = -1e30
norm_eps = 1e-06


def rotate(values, positions):
    half_width = values.shape[-1] // 2
    inverse_freq = jnp.exp(
        jnp.arange(half_width, dtype=jnp.float32) * (-2.0 * math.log(rope_base) / values.shape[-1])
    )
    angles = positions.astype(jnp.float32)[:, None] * inverse_freq[None, :]
    cosine = jnp.cos(angles)[:, None, :]
    sine_part = jnp.sin(angles)[:, None, :]
    front_half = values[..., :half_width]
    back_half = values[..., half_width:]
    return jnp.concatenate(
        [front_half * cosine - back_half * sine_part, back_half * cosine + front_half * sine_part],
        axis=-1,
    )


def lookup(table, index):
    hit = index[..., None] == jnp.arange(table.shape[0], dtype=index.dtype)
    return jnp.sum(jnp.where(hit, table, 0), axis=-1).astype(table.dtype)


GROUP = 8


def attend(q, k, v, length, rows, cache_rows):
    live = lax.broadcasted_iota(jnp.int32, (rows, cache_rows), 1) < length
    s = lax.dot_general(
        q, k, (((1,), (1,)), ((), ())), preferred_element_type=jnp.float32
    ) * HD ** (-0.5)
    s = jnp.where(live, s, mask_value)
    m = jnp.max(s, axis=1, keepdims=True)
    p = jnp.exp(s - m)
    l = jnp.sum(p, axis=1, keepdims=True)
    o = jnp.dot(p.astype(jnp.bfloat16), v, preferred_element_type=jnp.float32)
    return o / l, m + jnp.log(l)


CHUNK = 4


def node_kernel(
    perm_ref, start_ref, count_ref, nlen_ref, total_ref, q_ref, k_ref, v_ref, out_ref, lse_ref, qbuf
):
    slots, rows, width = q_ref.shape
    nodes, cache_rows, _ = k_ref.shape
    heads = width // HD
    span = CHUNK * rows

    def per_node(n, carry):
        first = start_ref[n]
        count = count_ref[n]
        length = nlen_ref[n]
        last = first + count - 1

        def per_chunk(c, carry2):
            base = first + c * CHUNK
            picked = [perm_ref[jnp.minimum(base + j, last)] for j in range(CHUNK)]
            for j in range(CHUNK):
                qbuf[pl.ds(j * rows, rows), :] = q_ref[picked[j]]
            lse_cols = []
            for h in range(heads):
                cols = pl.ds(h * HD, HD)
                o, lse = attend(
                    qbuf[:, cols], k_ref[n, :, cols], v_ref[n, :, cols], length, span, cache_rows
                )
                lse_cols.append(lse)
                for j in range(CHUNK):

                    @pl.when(base + j <= last)
                    def _():
                        out_ref[picked[j] // 2, pl.ds(pl.multiple_of(picked[j] % 2 * rows, rows), rows), cols] = (
                            o[j * rows : (j + 1) * rows].astype(out_ref.dtype)
                        )

            lane = lax.broadcasted_iota(jnp.int32, (span, 128), 1)
            lse_tile = jnp.zeros((span, 128), jnp.float32)
            for h in range(heads):
                lse_tile = jnp.where(lane == h, lse_cols[h], lse_tile)
            lse_t = jnp.transpose(lse_tile)
            for j in range(CHUNK):

                @pl.when(base + j <= last)
                def _():
                    for h in range(heads):
                        lse_ref[pl.ds(picked[j], 1), pl.ds(h * rows, rows)] = (
                            lse_t[h : h + 1, j * rows : (j + 1) * rows]
                        )

            return carry2

        lax.fori_loop(0, (count + CHUNK - 1) // CHUNK, per_chunk, 0)
        return carry

    lax.fori_loop(0, nodes, per_node, 0)

    def clear(p, carry):
        slot = perm_ref[p]
        out_ref[slot // 2, pl.ds(pl.multiple_of(slot % 2 * rows, rows), rows), :] = jnp.zeros(
            (rows, width), out_ref.dtype
        )
        lse_ref[pl.ds(slot, 1), :] = jnp.zeros((1, rows * heads), lse_ref.dtype)
        return carry

    lax.fori_loop(total_ref[0], slots, clear, 0)


def node_attention(queries, key_cache, value_cache, local_slot, filled, local_len, heads_local):
    slots, rows, width = queries.shape
    nodes, cache_rows, _ = key_cache.shape
    order_key = jnp.where(filled, local_slot, nodes)
    index = jnp.arange(slots, dtype=jnp.int32)
    before = (order_key[None, :] < order_key[:, None]) | (
        (order_key[None, :] == order_key[:, None]) & (index[None, :] < index[:, None])
    )
    rank = jnp.sum(before, axis=1).astype(jnp.int32)
    perm = jnp.sum(
        jnp.where(rank[None, :] == index[:, None], index[None, :], 0), axis=1
    ).astype(jnp.int32)
    node_ids = jnp.arange(nodes, dtype=jnp.int32)
    count = jnp.sum(filled[None, :] & (local_slot[None, :] == node_ids[:, None]), axis=1).astype(jnp.int32)
    first = jnp.sum(filled[None, :] & (local_slot[None, :] < node_ids[:, None]), axis=1).astype(jnp.int32)
    total = jnp.sum(filled).astype(jnp.int32).reshape(1)
    vmem = pl.BlockSpec(memory_space=pltpu.VMEM)
    smem = pl.BlockSpec(memory_space=pltpu.SMEM)
    flops = 4 * slots * rows * cache_rows * width
    out, lse = pl.pallas_call(
        node_kernel,
        out_shape=(
            jax.ShapeDtypeStruct((slots // 2, 2 * rows + 16, width), jnp.bfloat16),
            jax.ShapeDtypeStruct((slots, rows * heads_local), jnp.float32),
        ),
        in_specs=[smem] * 5 + [vmem] * 3,
        out_specs=(vmem, vmem),
        scratch_shapes=[pltpu.VMEM((CHUNK * rows, width), queries.dtype)],
        cost_estimate=pl.CostEstimate(
            flops=flops,
            transcendentals=slots * rows * cache_rows * heads_local,
            bytes_accessed=2 * queries.size * 2 + 2 * key_cache.size * 2,
        ),
    )(perm, first, count, local_len, total, queries, key_cache, value_cache)
    return out, lse


def sum_kernel(x_ref, out_ref, recv, send_sem, recv_sem):
    n = recv.shape[0]
    me = lax.axis_index("mp")
    barrier = pltpu.get_barrier_semaphore()
    for d in range(1, n):
        pl.semaphore_signal(
            barrier, inc=1, device_id={"mp": lax.rem(me + d, n)},
            device_id_type=pl.DeviceIdType.MESH,
        )
    pl.semaphore_wait(barrier, n - 1)
    copies = []
    for d in range(1, n):
        copy = pltpu.make_async_remote_copy(
            src_ref=x_ref,
            dst_ref=recv.at[d],
            send_sem=send_sem.at[d],
            recv_sem=recv_sem.at[d],
            device_id={"mp": lax.rem(me + d, n)},
            device_id_type=pl.DeviceIdType.MESH,
        )
        copy.start()
        copies.append(copy)
    for copy in copies:
        copy.wait()
    total = x_ref[...]
    for d in range(1, n):
        total = total + recv[d]
    out_ref[...] = total


def mp_sum(x, n):
    vmem = pl.BlockSpec(memory_space=pltpu.VMEM)
    return pl.pallas_call(
        sum_kernel,
        out_shape=jax.ShapeDtypeStruct(x.shape, x.dtype),
        in_specs=[vmem],
        out_specs=vmem,
        scratch_shapes=[
            pltpu.VMEM((n,) + x.shape, x.dtype),
            pltpu.SemaphoreType.DMA((n,)),
            pltpu.SemaphoreType.DMA((n,)),
        ],
        compiler_params=pltpu.CompilerParams(collective_id=0, has_side_effects=True),
    )(x)


def self_attention(queries, keys, values):
    head_dim = queries.shape[-1]
    row_total = queries.shape[1]
    scores = jnp.einsum(
        "rqhd,rkhd->rhqk", queries, keys, preferred_element_type=jnp.float32
    ) * head_dim ** (-0.5)
    causal = jnp.arange(row_total)[:, None] >= jnp.arange(row_total)[None, :]
    scores = jnp.where(causal[None, None], scores, mask_value)
    highest = jnp.max(scores, axis=-1)
    weights = jnp.exp(scores - highest[..., None])
    totals = jnp.sum(weights, axis=-1)
    mixture = jnp.einsum(
        "rhqk,rkhd->rqhd", weights.astype(jnp.bfloat16), values, preferred_element_type=jnp.float32
    )
    return (
        mixture / jnp.transpose(totals, (0, 2, 1))[..., None],
        jnp.transpose(highest + jnp.log(totals), (0, 2, 1)),
    )


def on_device(
    activations,
    w_query,
    w_key,
    w_value,
    w_out,
    norm_gain,
    key_cache,
    value_cache,
    parent,
    node_len,
    req_leaf,
):
    leaf_count = lax.axis_size("leaf")
    device = lax.axis_index("leaf")
    tok_rows = activations.shape[0]
    width_local = w_query.shape[1]
    heads_local = width_local // HD
    spread = leaf_count - TENANTS
    node_slots = 2 * ((REQ_DEV + spread - 1) // spread)
    all_slots = max(REQ_DEV // TENANTS, node_slots)
    block = REQ_LEN * width_local
    columns = lax.all_gather(activations, "mp", axis=1, tiled=True)
    query_f = jnp.dot(columns, w_query, preferred_element_type=jnp.float32)
    middle_all = lookup(parent, req_leaf)
    root_all = lookup(parent, middle_all)
    len_of = lambda nodes: lookup(node_len, nodes)
    prefix = len_of(root_all) + len_of(middle_all) + len_of(req_leaf)
    mine_prefix = lax.dynamic_slice_in_dim(prefix, device * REQ_DEV, REQ_DEV)
    position = (mine_prefix[:, None] + jnp.arange(REQ_LEN, dtype=jnp.int32)[None, :]).reshape(
        tok_rows
    )
    queries = rotate(query_f.reshape(tok_rows, heads_local, HD), position).astype(jnp.bfloat16)
    q_blocks = queries.reshape(REQ_DEV, block)
    levels_all = jnp.stack([root_all, middle_all, req_leaf], axis=0).reshape(3, leaf_count, REQ_DEV)
    level_count = levels_all.shape[0]
    items = level_count * REQ_DEV
    per_sender = jnp.transpose(levels_all, (1, 0, 2)).reshape(leaf_count, items)
    holders = per_sender // NODE_DEV
    earlier = jnp.arange(items)[:, None] > jnp.arange(items)[None, :]
    ranks = jnp.sum(
        earlier[None] & (holders[:, :, None] == holders[:, None, :]), axis=2
    ).astype(jnp.int32)
    slot_ids = jnp.arange(all_slots, dtype=jnp.int32)
    my_holders = lax.dynamic_index_in_dim(holders, device, 0, keepdims=False)
    my_ranks = lax.dynamic_index_in_dim(ranks, device, 0, keepdims=False)
    send_hit = (
        (my_holders[None, None, :] == jnp.arange(leaf_count, dtype=jnp.int32)[:, None, None])
        & (my_ranks[None, None, :] == slot_ids[None, :, None])
    )
    send_item = jnp.sum(jnp.where(send_hit, jnp.arange(items, dtype=jnp.int32), 0), axis=2)
    send_valid = jnp.any(send_hit, axis=2)
    pick = (
        send_valid[:, :, None] & (send_item[:, :, None] % REQ_DEV == jnp.arange(REQ_DEV))
    ).reshape(leaf_count * all_slots, REQ_DEV)
    outgoing = jnp.sum(
        jnp.where(
            pick[:, :, None, None],
            q_blocks.reshape(REQ_DEV, REQ_LEN, width_local)[None],
            jnp.zeros((), jnp.bfloat16),
        ),
        axis=1,
    ).reshape(leaf_count, all_slots, REQ_LEN, width_local)
    arrived = lax.all_to_all(outgoing, "leaf", split_axis=0, concat_axis=0, tiled=True)
    columns_late = lax.optimization_barrier((columns, outgoing))[0]
    key_f, value_f = (
        jnp.dot(columns_late, matrix, preferred_element_type=jnp.float32)
        for matrix in (w_key, w_value)
    )
    keys = rotate(key_f.reshape(tok_rows, heads_local, HD), position).astype(jnp.bfloat16)
    values = value_f.astype(jnp.bfloat16)
    self_out, self_lse = self_attention(
        queries.reshape(REQ_DEV, REQ_LEN, heads_local, HD),
        keys.reshape(REQ_DEV, REQ_LEN, heads_local, HD),
        values.reshape(REQ_DEV, REQ_LEN, heads_local, HD),
    )
    recv_hit = (holders[:, None, :] == device) & (ranks[:, None, :] == slot_ids[None, :, None])
    slot_nodes = jnp.sum(jnp.where(recv_hit, per_sender[:, None, :], 0), axis=2).reshape(-1)
    filled = jnp.any(recv_hit, axis=2).reshape(-1)
    local_slot = jnp.where(filled, slot_nodes - device * NODE_DEV, 0)
    lengths = jnp.where(filled, len_of(slot_nodes), 0)
    node_out, node_lse = node_attention(
        arrived.reshape(leaf_count * all_slots, REQ_LEN, width_local),
        key_cache,
        value_cache,
        local_slot,
        filled,
        lax.dynamic_slice_in_dim(node_len, device * NODE_DEV, NODE_DEV),
        heads_local,
    )
    slot_count = leaf_count * all_slots
    flat_lse = node_lse.reshape(slot_count, REQ_LEN * heads_local)
    lse_high = lax.reduce_precision(flat_lse, exponent_bits=8, mantissa_bits=7)
    lse_low = flat_lse - lse_high
    pair_width = 2 * REQ_LEN * heads_local
    lse_rows = jnp.pad(
        jnp.concatenate([lse_high, lse_low], axis=1).astype(jnp.bfloat16).reshape(
            leaf_count, all_slots, pair_width
        ),
        ((0, 0), (0, 16 - all_slots), (0, width_local - pair_width)),
    )
    payload = lax.dynamic_update_slice(node_out, lse_rows, (0, all_slots * REQ_LEN, 0))
    back = lax.all_to_all(payload, "leaf", split_axis=0, concat_axis=0, tiled=True)
    got = jnp.take(back, my_holders, axis=0)
    second = (my_ranks == 1)[:, None, None]
    got_out = (
        jnp.where(second, got[:, REQ_LEN : 2 * REQ_LEN], got[:, :REQ_LEN])
        .astype(jnp.float32)
        .reshape(level_count, REQ_DEV, REQ_LEN, heads_local, HD)
    )
    lse_at = all_slots * REQ_LEN
    got_pair = jnp.where(
        second[:, 0], got[:, lse_at + 1, :pair_width], got[:, lse_at, :pair_width]
    ).astype(jnp.float32)
    lse_width = REQ_LEN * heads_local
    got_lse = jnp.swapaxes(
        (got_pair[:, :lse_width] + got_pair[:, lse_width:]).reshape(items, heads_local, REQ_LEN),
        1,
        2,
    ).reshape(level_count, REQ_DEV, REQ_LEN, heads_local)
    partial_out = jnp.concatenate([got_out, self_out[None]], axis=0)
    partial_lse = jnp.concatenate([got_lse, self_lse[None]], axis=0)
    highest = jnp.max(partial_lse, axis=0)
    factor = jnp.exp(partial_lse - highest[None])
    merged = jnp.sum(factor[..., None] * partial_out, axis=0) / jnp.sum(factor, axis=0)[..., None]
    attn = merged.astype(jnp.bfloat16).reshape(tok_rows, width_local)
    partial_value = jnp.dot(attn, w_out, preferred_element_type=jnp.float32)
    projected = lax.psum_scatter(
        partial_value.astype(jnp.bfloat16), "mp", scatter_dimension=1, tiled=True
    ).astype(jnp.float32)
    squares = mp_sum(
        jnp.sum(projected * projected, axis=1).reshape(1, tok_rows), lax.axis_size("mp")
    ).reshape(tok_rows)
    row_scale = lax.rsqrt(squares / D + norm_eps)
    return (
        activations.astype(jnp.float32) + norm_gain[None, :] * projected * row_scale[:, None]
    ).astype(jnp.bfloat16)


def solution(mesh):
    in_specs = (
        P("leaf", "mp"),
        P(None, "mp"),
        P(None, "mp"),
        P(None, "mp"),
        P("mp", None),
        P("mp"),
        P("leaf", None, "mp"),
        P("leaf", None, "mp"),
        P(),
        P(),
        P(),
    )
    out_specs = P("leaf", "mp")
    return jax.shard_map(
        on_device, mesh=mesh, in_specs=in_specs, out_specs=out_specs, check_vma=False
    )
```

```python
import math

import jax
import jax.numpy as jnp
from jax import lax
from jax.experimental import pallas as pl
from jax.experimental.pallas import tpu as pltpu
from jax.sharding import PartitionSpec as P

D = 4096
HD = 128
TENANTS = 4
NODE_DEV = 8
REQ_LEN = 64
REQ_DEV = 4


rope_base = 500000.0
mask_value = -1e30
norm_eps = 1e-06


def rotate(values, positions):
    half_width = values.shape[-1] // 2
    inverse_freq = jnp.exp(
        jnp.arange(half_width, dtype=jnp.float32) * (-2.0 * math.log(rope_base) / values.shape[-1])
    )
    angles = positions.astype(jnp.float32)[:, None] * inverse_freq[None, :]
    cosine = jnp.cos(angles)[:, None, :]
    sine_part = jnp.sin(angles)[:, None, :]
    front_half = values[..., :half_width]
    back_half = values[..., half_width:]
    return jnp.concatenate(
        [front_half * cosine - back_half * sine_part, back_half * cosine + front_half * sine_part],
        axis=-1,
    )


def lookup(table, index):
    hit = index[..., None] == jnp.arange(table.shape[0], dtype=index.dtype)
    return jnp.sum(jnp.where(hit, table, 0), axis=-1).astype(table.dtype)


GROUP = 8


def attend(q, k, v, length, rows, cache_rows):
    live = lax.broadcasted_iota(jnp.int32, (rows, cache_rows), 1) < length
    s = lax.dot_general(
        q, k, (((1,), (1,)), ((), ())), preferred_element_type=jnp.float32
    ) * HD ** (-0.5)
    s = jnp.where(live, s, mask_value)
    m = jnp.max(s, axis=1, keepdims=True)
    p = jnp.exp(s - m)
    l = jnp.sum(p, axis=1, keepdims=True)
    o = jnp.dot(p.astype(jnp.bfloat16), v, preferred_element_type=jnp.float32)
    return o / l, m + jnp.log(l)


CHUNK = 4


def node_kernel(
    perm_ref, start_ref, count_ref, nlen_ref, total_ref, q_ref, k_ref, v_ref, out_ref, lse_ref, qbuf
):
    slots, rows, width = q_ref.shape
    nodes, cache_rows, _ = k_ref.shape
    heads = width // HD
    span = CHUNK * rows

    def per_node(n, carry):
        first = start_ref[n]
        count = count_ref[n]
        length = nlen_ref[n]
        last = first + count - 1

        def per_chunk(c, carry2):
            base = first + c * CHUNK
            picked = [perm_ref[jnp.minimum(base + j, last)] for j in range(CHUNK)]
            for j in range(CHUNK):
                qbuf[pl.ds(j * rows, rows), :] = q_ref[picked[j]]
            lse_cols = []
            for h in range(heads):
                cols = pl.ds(h * HD, HD)
                o, lse = attend(
                    qbuf[:, cols], k_ref[n, :, cols], v_ref[n, :, cols], length, span, cache_rows
                )
                lse_cols.append(lse)
                for j in range(CHUNK):

                    @pl.when(base + j <= last)
                    def _():
                        out_ref[picked[j] // 2, pl.ds(pl.multiple_of(picked[j] % 2 * rows, rows), rows), cols] = (
                            o[j * rows : (j + 1) * rows].astype(out_ref.dtype)
                        )

            lane = lax.broadcasted_iota(jnp.int32, (span, 128), 1)
            lse_tile = jnp.zeros((span, 128), jnp.float32)
            for h in range(heads):
                lse_tile = jnp.where(lane == h, lse_cols[h], lse_tile)
            lse_t = jnp.transpose(lse_tile)
            for j in range(CHUNK):

                @pl.when(base + j <= last)
                def _():
                    for h in range(heads):
                        lse_ref[pl.ds(picked[j], 1), pl.ds(h * rows, rows)] = (
                            lse_t[h : h + 1, j * rows : (j + 1) * rows]
                        )

            return carry2

        lax.fori_loop(0, (count + CHUNK - 1) // CHUNK, per_chunk, 0)
        return carry

    lax.fori_loop(0, nodes, per_node, 0)

    def clear(p, carry):
        slot = perm_ref[p]
        out_ref[slot // 2, pl.ds(pl.multiple_of(slot % 2 * rows, rows), rows), :] = jnp.zeros(
            (rows, width), out_ref.dtype
        )
        lse_ref[pl.ds(slot, 1), :] = jnp.zeros((1, rows * heads), lse_ref.dtype)
        return carry

    lax.fori_loop(total_ref[0], slots, clear, 0)


def node_attention(queries, key_cache, value_cache, local_slot, filled, local_len, heads_local):
    slots, rows, width = queries.shape
    nodes, cache_rows, _ = key_cache.shape
    order_key = jnp.where(filled, local_slot, nodes)
    index = jnp.arange(slots, dtype=jnp.int32)
    before = (order_key[None, :] < order_key[:, None]) | (
        (order_key[None, :] == order_key[:, None]) & (index[None, :] < index[:, None])
    )
    rank = jnp.sum(before, axis=1).astype(jnp.int32)
    perm = jnp.sum(
        jnp.where(rank[None, :] == index[:, None], index[None, :], 0), axis=1
    ).astype(jnp.int32)
    node_ids = jnp.arange(nodes, dtype=jnp.int32)
    count = jnp.sum(filled[None, :] & (local_slot[None, :] == node_ids[:, None]), axis=1).astype(jnp.int32)
    first = jnp.sum(filled[None, :] & (local_slot[None, :] < node_ids[:, None]), axis=1).astype(jnp.int32)
    total = jnp.sum(filled).astype(jnp.int32).reshape(1)
    vmem = pl.BlockSpec(memory_space=pltpu.VMEM)
    smem = pl.BlockSpec(memory_space=pltpu.SMEM)
    flops = 4 * slots * rows * cache_rows * width
    out, lse = pl.pallas_call(
        node_kernel,
        out_shape=(
            jax.ShapeDtypeStruct((slots // 2, 2 * rows + 16, width), jnp.bfloat16),
            jax.ShapeDtypeStruct((slots, rows * heads_local), jnp.float32),
        ),
        in_specs=[smem] * 5 + [vmem] * 3,
        out_specs=(vmem, vmem),
        scratch_shapes=[pltpu.VMEM((CHUNK * rows, width), queries.dtype)],
        cost_estimate=pl.CostEstimate(
            flops=flops,
            transcendentals=slots * rows * cache_rows * heads_local,
            bytes_accessed=2 * queries.size * 2 + 2 * key_cache.size * 2,
        ),
    )(perm, first, count, local_len, total, queries, key_cache, value_cache)
    return out, lse


def sum_kernel(x_ref, out_ref, recv, send_sem, recv_sem):
    n = recv.shape[0]
    me = lax.axis_index("mp")
    barrier = pltpu.get_barrier_semaphore()
    for d in range(1, n):
        pl.semaphore_signal(
            barrier, inc=1, device_id={"mp": lax.rem(me + d, n)},
            device_id_type=pl.DeviceIdType.MESH,
        )
    pl.semaphore_wait(barrier, n - 1)
    copies = []
    for d in range(1, n):
        copy = pltpu.make_async_remote_copy(
            src_ref=x_ref,
            dst_ref=recv.at[d],
            send_sem=send_sem.at[d],
            recv_sem=recv_sem.at[d],
            device_id={"mp": lax.rem(me + d, n)},
            device_id_type=pl.DeviceIdType.MESH,
        )
        copy.start()
        copies.append(copy)
    for copy in copies:
        copy.wait()
    total = x_ref[...]
    for d in range(1, n):
        total = total + recv[d]
    out_ref[...] = total


def mp_sum(x, n):
    vmem = pl.BlockSpec(memory_space=pltpu.VMEM)
    return pl.pallas_call(
        sum_kernel,
        out_shape=jax.ShapeDtypeStruct(x.shape, x.dtype),
        in_specs=[vmem],
        out_specs=vmem,
        scratch_shapes=[
            pltpu.VMEM((n,) + x.shape, x.dtype),
            pltpu.SemaphoreType.DMA((n,)),
            pltpu.SemaphoreType.DMA((n,)),
        ],
        compiler_params=pltpu.CompilerParams(collective_id=0, has_side_effects=True),
    )(x)


def self_attention(queries, keys, values):
    head_dim = queries.shape[-1]
    row_total = queries.shape[1]
    scores = jnp.einsum(
        "rqhd,rkhd->rhqk", queries, keys, preferred_element_type=jnp.float32
    ) * head_dim ** (-0.5)
    causal = jnp.arange(row_total)[:, None] >= jnp.arange(row_total)[None, :]
    scores = jnp.where(causal[None, None], scores, mask_value)
    highest = jnp.max(scores, axis=-1)
    weights = jnp.exp(scores - highest[..., None])
    totals = jnp.sum(weights, axis=-1)
    mixture = jnp.einsum(
        "rhqk,rkhd->rqhd", weights.astype(jnp.bfloat16), values, preferred_element_type=jnp.float32
    )
    return (
        mixture / jnp.transpose(totals, (0, 2, 1))[..., None],
        jnp.transpose(highest + jnp.log(totals), (0, 2, 1)),
    )


def on_device(
    activations,
    w_query,
    w_key,
    w_value,
    w_out,
    norm_gain,
    key_cache,
    value_cache,
    parent,
    node_len,
    req_leaf,
):
    leaf_count = lax.axis_size("leaf")
    device = lax.axis_index("leaf")
    tok_rows = activations.shape[0]
    width_local = w_query.shape[1]
    heads_local = width_local // HD
    spread = leaf_count - TENANTS
    node_slots = 2 * ((REQ_DEV + spread - 1) // spread)
    all_slots = max(REQ_DEV // TENANTS, node_slots)
    block = REQ_LEN * width_local
    columns = lax.all_gather(activations, "mp", axis=1, tiled=True)
    query_f = jnp.dot(columns, w_query, preferred_element_type=jnp.float32)
    middle_all = lookup(parent, req_leaf)
    root_all = lookup(parent, middle_all)
    len_of = lambda nodes: lookup(node_len, nodes)
    prefix = len_of(root_all) + len_of(middle_all) + len_of(req_leaf)
    mine_prefix = lax.dynamic_slice_in_dim(prefix, device * REQ_DEV, REQ_DEV)
    position = (mine_prefix[:, None] + jnp.arange(REQ_LEN, dtype=jnp.int32)[None, :]).reshape(
        tok_rows
    )
    queries = rotate(query_f.reshape(tok_rows, heads_local, HD), position).astype(jnp.bfloat16)
    q_blocks = queries.reshape(REQ_DEV, block)
    levels_all = jnp.stack([root_all, middle_all, req_leaf], axis=0).reshape(3, leaf_count, REQ_DEV)
    level_count = levels_all.shape[0]
    items = level_count * REQ_DEV
    per_sender = jnp.transpose(levels_all, (1, 0, 2)).reshape(leaf_count, items)
    holders = per_sender // NODE_DEV
    earlier = jnp.arange(items)[:, None] > jnp.arange(items)[None, :]
    ranks = jnp.sum(
        earlier[None] & (holders[:, :, None] == holders[:, None, :]), axis=2
    ).astype(jnp.int32)
    slot_ids = jnp.arange(all_slots, dtype=jnp.int32)
    my_holders = lax.dynamic_index_in_dim(holders, device, 0, keepdims=False)
    my_ranks = lax.dynamic_index_in_dim(ranks, device, 0, keepdims=False)
    send_hit = (
        (my_holders[None, None, :] == jnp.arange(leaf_count, dtype=jnp.int32)[:, None, None])
        & (my_ranks[None, None, :] == slot_ids[None, :, None])
    )
    send_item = jnp.sum(jnp.where(send_hit, jnp.arange(items, dtype=jnp.int32), 0), axis=2)
    send_valid = jnp.any(send_hit, axis=2)
    pick = (
        send_valid[:, :, None] & (send_item[:, :, None] % REQ_DEV == jnp.arange(REQ_DEV))
    ).reshape(leaf_count * all_slots, REQ_DEV)
    outgoing = jnp.sum(
        jnp.where(
            pick[:, :, None, None],
            q_blocks.reshape(REQ_DEV, REQ_LEN, width_local)[None],
            jnp.zeros((), jnp.bfloat16),
        ),
        axis=1,
    ).reshape(leaf_count, all_slots, REQ_LEN, width_local)
    arrived = lax.all_to_all(outgoing, "leaf", split_axis=0, concat_axis=0, tiled=True)
    columns_late = lax.optimization_barrier((columns, outgoing))[0]
    key_f, value_f = (
        jnp.dot(columns_late, matrix, preferred_element_type=jnp.float32)
        for matrix in (w_key, w_value)
    )
    keys = rotate(key_f.reshape(tok_rows, heads_local, HD), position).astype(jnp.bfloat16)
    values = value_f.astype(jnp.bfloat16)
    self_out, self_lse = self_attention(
        queries.reshape(REQ_DEV, REQ_LEN, heads_local, HD),
        keys.reshape(REQ_DEV, REQ_LEN, heads_local, HD),
        values.reshape(REQ_DEV, REQ_LEN, heads_local, HD),
    )
    recv_hit = (holders[:, None, :] == device) & (ranks[:, None, :] == slot_ids[None, :, None])
    slot_nodes = jnp.sum(jnp.where(recv_hit, per_sender[:, None, :], 0), axis=2).reshape(-1)
    filled = jnp.any(recv_hit, axis=2).reshape(-1)
    local_slot = jnp.where(filled, slot_nodes - device * NODE_DEV, 0)
    lengths = jnp.where(filled, len_of(slot_nodes), 0)
    node_out, node_lse = node_attention(
        arrived.reshape(leaf_count * all_slots, REQ_LEN, width_local),
        key_cache,
        value_cache,
        local_slot,
        filled,
        lax.dynamic_slice_in_dim(node_len, device * NODE_DEV, NODE_DEV),
        heads_local,
    )
    slot_count = leaf_count * all_slots
    flat_lse = node_lse.reshape(slot_count, REQ_LEN * heads_local)
    lse_high = lax.reduce_precision(flat_lse, exponent_bits=8, mantissa_bits=7)
    lse_low = flat_lse - lse_high
    pair_width = 2 * REQ_LEN * heads_local
    lse_rows = jnp.pad(
        jnp.concatenate([lse_high, lse_low], axis=1).astype(jnp.bfloat16).reshape(
            leaf_count, all_slots, pair_width
        ),
        ((0, 0), (0, 16 - all_slots), (0, width_local - pair_width)),
    )
    payload = lax.dynamic_update_slice(node_out, lse_rows, (0, all_slots * REQ_LEN, 0))
    back = lax.all_to_all(payload, "leaf", split_axis=0, concat_axis=0, tiled=True)
    got = jnp.take(back, my_holders, axis=0)
    second = (my_ranks == 1)[:, None, None]
    got_out = (
        jnp.where(second, got[:, REQ_LEN : 2 * REQ_LEN], got[:, :REQ_LEN])
        .reshape(level_count, REQ_DEV, REQ_LEN, heads_local, HD)
    )
    lse_at = all_slots * REQ_LEN
    got_pair = jnp.where(
        second[:, 0], got[:, lse_at + 1, :pair_width], got[:, lse_at, :pair_width]
    ).astype(jnp.float32)
    lse_width = REQ_LEN * heads_local
    got_lse = jnp.swapaxes(
        (got_pair[:, :lse_width] + got_pair[:, lse_width:]).reshape(items, heads_local, REQ_LEN),
        1,
        2,
    ).reshape(level_count, REQ_DEV, REQ_LEN, heads_local)
    partial_lse = jnp.concatenate([got_lse, self_lse[None]], axis=0)
    highest = jnp.max(partial_lse, axis=0)
    factor = jnp.exp(partial_lse - highest[None])
    weighted = factor[3][..., None] * self_out
    for level in range(level_count):
        weighted = weighted + factor[level][..., None] * got_out[level].astype(jnp.float32)
    merged = weighted / jnp.sum(factor, axis=0)[..., None]
    attn = merged.astype(jnp.bfloat16).reshape(tok_rows, width_local)
    partial_value = jnp.dot(attn, w_out, preferred_element_type=jnp.float32)
    projected = lax.psum_scatter(
        partial_value.astype(jnp.bfloat16), "mp", scatter_dimension=1, tiled=True
    ).astype(jnp.float32)
    squares = mp_sum(
        jnp.sum(projected * projected, axis=1).reshape(1, tok_rows), lax.axis_size("mp")
    ).reshape(tok_rows)
    row_scale = lax.rsqrt(squares / D + norm_eps)
    return (
        activations.astype(jnp.float32) + norm_gain[None, :] * projected * row_scale[:, None]
    ).astype(jnp.bfloat16)


def solution(mesh):
    in_specs = (
        P("leaf", "mp"),
        P(None, "mp"),
        P(None, "mp"),
        P(None, "mp"),
        P("mp", None),
        P("mp"),
        P("leaf", None, "mp"),
        P("leaf", None, "mp"),
        P(),
        P(),
        P(),
    )
    out_specs = P("leaf", "mp")
    return jax.shard_map(
        on_device, mesh=mesh, in_specs=in_specs, out_specs=out_specs, check_vma=False
    )
```

```python
import math

import jax
import jax.numpy as jnp
from jax import lax
from jax.experimental import pallas as pl
from jax.experimental.pallas import tpu as pltpu
from jax.sharding import PartitionSpec as P

D = 4096
HD = 128
TENANTS = 4
NODE_DEV = 8
REQ_LEN = 64
REQ_DEV = 4


rope_base = 500000.0
mask_value = -1e30
norm_eps = 1e-06


def rotate(values, positions):
    half_width = values.shape[-1] // 2
    inverse_freq = jnp.exp(
        jnp.arange(half_width, dtype=jnp.float32) * (-2.0 * math.log(rope_base) / values.shape[-1])
    )
    angles = positions.astype(jnp.float32)[:, None] * inverse_freq[None, :]
    cosine = jnp.cos(angles)[:, None, :]
    sine_part = jnp.sin(angles)[:, None, :]
    front_half = values[..., :half_width]
    back_half = values[..., half_width:]
    return jnp.concatenate(
        [front_half * cosine - back_half * sine_part, back_half * cosine + front_half * sine_part],
        axis=-1,
    )


def lookup(table, index):
    hit = index[..., None] == jnp.arange(table.shape[0], dtype=index.dtype)
    return jnp.sum(jnp.where(hit, table, 0), axis=-1).astype(table.dtype)


GROUP = 8


def attend(q, k, v, length, rows, cache_rows):
    live = lax.broadcasted_iota(jnp.int32, (rows, cache_rows), 1) < length
    s = lax.dot_general(
        q, k, (((1,), (1,)), ((), ())), preferred_element_type=jnp.float32
    ) * HD ** (-0.5)
    s = jnp.where(live, s, mask_value)
    m = jnp.max(s, axis=1, keepdims=True)
    p = jnp.exp(s - m)
    l = jnp.sum(p, axis=1, keepdims=True)
    o = jnp.dot(p.astype(jnp.bfloat16), v, preferred_element_type=jnp.float32)
    return o / l, m + jnp.log(l)


CHUNK = 4


def node_kernel(
    perm_ref, start_ref, count_ref, nlen_ref, total_ref, q_ref, k_ref, v_ref, out_ref, lse_ref, qbuf
):
    slots, rows, width = q_ref.shape
    nodes, cache_rows, _ = k_ref.shape
    heads = width // HD
    span = CHUNK * rows

    def per_node(n, carry):
        first = start_ref[n]
        count = count_ref[n]
        length = nlen_ref[n]
        last = first + count - 1

        def per_chunk(c, carry2):
            base = first + c * CHUNK
            picked = [perm_ref[jnp.minimum(base + j, last)] for j in range(CHUNK)]
            for j in range(CHUNK):
                qbuf[pl.ds(j * rows, rows), :] = q_ref[picked[j]]
            lse_cols = []
            for h in range(heads):
                cols = pl.ds(h * HD, HD)
                o, lse = attend(
                    qbuf[:, cols], k_ref[n, :, cols], v_ref[n, :, cols], length, span, cache_rows
                )
                lse_cols.append(lse)
                for j in range(CHUNK):

                    @pl.when(base + j <= last)
                    def _():
                        out_ref[picked[j] // 2, pl.ds(pl.multiple_of(picked[j] % 2 * rows, rows), rows), cols] = (
                            o[j * rows : (j + 1) * rows].astype(out_ref.dtype)
                        )

            lane = lax.broadcasted_iota(jnp.int32, (span, 128), 1)
            lse_tile = jnp.zeros((span, 128), jnp.float32)
            for h in range(heads):
                lse_tile = jnp.where(lane == h, lse_cols[h], lse_tile)
            lse_t = jnp.transpose(lse_tile)
            for j in range(CHUNK):

                @pl.when(base + j <= last)
                def _():
                    for h in range(heads):
                        lse_ref[pl.ds(picked[j], 1), pl.ds(h * rows, rows)] = (
                            lse_t[h : h + 1, j * rows : (j + 1) * rows]
                        )

            return carry2

        lax.fori_loop(0, (count + CHUNK - 1) // CHUNK, per_chunk, 0)
        return carry

    lax.fori_loop(0, nodes, per_node, 0)

    def clear(p, carry):
        slot = perm_ref[p]
        out_ref[slot // 2, pl.ds(pl.multiple_of(slot % 2 * rows, rows), rows), :] = jnp.zeros(
            (rows, width), out_ref.dtype
        )
        lse_ref[pl.ds(slot, 1), :] = jnp.zeros((1, rows * heads), lse_ref.dtype)
        return carry

    lax.fori_loop(total_ref[0], slots, clear, 0)


def node_attention(queries, key_cache, value_cache, local_slot, filled, local_len, heads_local):
    slots, rows, width = queries.shape
    nodes, cache_rows, _ = key_cache.shape
    order_key = jnp.where(filled, local_slot, nodes)
    index = jnp.arange(slots, dtype=jnp.int32)
    before = (order_key[None, :] < order_key[:, None]) | (
        (order_key[None, :] == order_key[:, None]) & (index[None, :] < index[:, None])
    )
    rank = jnp.sum(before, axis=1).astype(jnp.int32)
    perm = jnp.sum(
        jnp.where(rank[None, :] == index[:, None], index[None, :], 0), axis=1
    ).astype(jnp.int32)
    node_ids = jnp.arange(nodes, dtype=jnp.int32)
    count = jnp.sum(filled[None, :] & (local_slot[None, :] == node_ids[:, None]), axis=1).astype(jnp.int32)
    first = jnp.sum(filled[None, :] & (local_slot[None, :] < node_ids[:, None]), axis=1).astype(jnp.int32)
    total = jnp.sum(filled).astype(jnp.int32).reshape(1)
    vmem = pl.BlockSpec(memory_space=pltpu.VMEM)
    smem = pl.BlockSpec(memory_space=pltpu.SMEM)
    flops = 4 * slots * rows * cache_rows * width
    out, lse = pl.pallas_call(
        node_kernel,
        out_shape=(
            jax.ShapeDtypeStruct((slots // 2, 2 * rows + 16, width), jnp.bfloat16),
            jax.ShapeDtypeStruct((slots, rows * heads_local), jnp.float32),
        ),
        in_specs=[smem] * 5 + [vmem] * 3,
        out_specs=(vmem, vmem),
        scratch_shapes=[pltpu.VMEM((CHUNK * rows, width), queries.dtype)],
        cost_estimate=pl.CostEstimate(
            flops=flops,
            transcendentals=slots * rows * cache_rows * heads_local,
            bytes_accessed=2 * queries.size * 2 + 2 * key_cache.size * 2,
        ),
    )(perm, first, count, local_len, total, queries, key_cache, value_cache)
    return out, lse


def sum_kernel(x_ref, out_ref, recv, send_sem, recv_sem):
    n = recv.shape[0]
    me = lax.axis_index("mp")
    barrier = pltpu.get_barrier_semaphore()
    for d in range(1, n):
        pl.semaphore_signal(
            barrier, inc=1, device_id={"mp": lax.rem(me + d, n)},
            device_id_type=pl.DeviceIdType.MESH,
        )
    pl.semaphore_wait(barrier, n - 1)
    copies = []
    for d in range(1, n):
        copy = pltpu.make_async_remote_copy(
            src_ref=x_ref,
            dst_ref=recv.at[d],
            send_sem=send_sem.at[d],
            recv_sem=recv_sem.at[d],
            device_id={"mp": lax.rem(me + d, n)},
            device_id_type=pl.DeviceIdType.MESH,
        )
        copy.start()
        copies.append(copy)
    for copy in copies:
        copy.wait()
    total = x_ref[...]
    for d in range(1, n):
        total = total + recv[d]
    out_ref[...] = total


def mp_sum(x, n):
    vmem = pl.BlockSpec(memory_space=pltpu.VMEM)
    return pl.pallas_call(
        sum_kernel,
        out_shape=jax.ShapeDtypeStruct(x.shape, x.dtype),
        in_specs=[vmem],
        out_specs=vmem,
        scratch_shapes=[
            pltpu.VMEM((n,) + x.shape, x.dtype),
            pltpu.SemaphoreType.DMA((n,)),
            pltpu.SemaphoreType.DMA((n,)),
        ],
        compiler_params=pltpu.CompilerParams(collective_id=0, has_side_effects=True),
    )(x)


def self_attention(queries, keys, values):
    head_dim = queries.shape[-1]
    row_total = queries.shape[1]
    scores = jnp.einsum(
        "rqhd,rkhd->rhqk", queries, keys, preferred_element_type=jnp.float32
    ) * head_dim ** (-0.5)
    causal = jnp.arange(row_total)[:, None] >= jnp.arange(row_total)[None, :]
    scores = jnp.where(causal[None, None], scores, mask_value)
    highest = jnp.max(scores, axis=-1)
    weights = jnp.exp(scores - highest[..., None])
    totals = jnp.sum(weights, axis=-1)
    mixture = jnp.einsum(
        "rhqk,rkhd->rqhd", weights.astype(jnp.bfloat16), values, preferred_element_type=jnp.float32
    )
    return (
        mixture / jnp.transpose(totals, (0, 2, 1))[..., None],
        jnp.transpose(highest + jnp.log(totals), (0, 2, 1)),
    )


def on_device(
    activations,
    w_query,
    w_key,
    w_value,
    w_out,
    norm_gain,
    key_cache,
    value_cache,
    parent,
    node_len,
    req_leaf,
):
    leaf_count = lax.axis_size("leaf")
    device = lax.axis_index("leaf")
    tok_rows = activations.shape[0]
    width_local = w_query.shape[1]
    heads_local = width_local // HD
    spread = leaf_count - TENANTS
    node_slots = 2 * ((REQ_DEV + spread - 1) // spread)
    all_slots = max(REQ_DEV // TENANTS, node_slots)
    block = REQ_LEN * width_local
    columns = lax.all_gather(activations, "mp", axis=1, tiled=True)
    query_f = jnp.dot(columns, w_query, preferred_element_type=jnp.float32)
    middle_all = lookup(parent, req_leaf)
    root_all = lookup(parent, middle_all)
    len_of = lambda nodes: lookup(node_len, nodes)
    prefix = len_of(root_all) + len_of(middle_all) + len_of(req_leaf)
    mine_prefix = lax.dynamic_slice_in_dim(prefix, device * REQ_DEV, REQ_DEV)
    position = (mine_prefix[:, None] + jnp.arange(REQ_LEN, dtype=jnp.int32)[None, :]).reshape(
        tok_rows
    )
    queries = rotate(query_f.reshape(tok_rows, heads_local, HD), position).astype(jnp.bfloat16)
    q_blocks = queries.reshape(REQ_DEV, block)
    levels_all = jnp.stack([root_all, middle_all, req_leaf], axis=0).reshape(3, leaf_count, REQ_DEV)
    level_count = levels_all.shape[0]
    items = level_count * REQ_DEV
    per_sender = jnp.transpose(levels_all, (1, 0, 2)).reshape(leaf_count, items)
    holders = per_sender // NODE_DEV
    earlier = jnp.arange(items)[:, None] > jnp.arange(items)[None, :]
    ranks = jnp.sum(
        earlier[None] & (holders[:, :, None] == holders[:, None, :]), axis=2
    ).astype(jnp.int32)
    slot_ids = jnp.arange(all_slots, dtype=jnp.int32)
    my_holders = lax.dynamic_index_in_dim(holders, device, 0, keepdims=False)
    my_ranks = lax.dynamic_index_in_dim(ranks, device, 0, keepdims=False)
    send_hit = (
        (my_holders[None, None, :] == jnp.arange(leaf_count, dtype=jnp.int32)[:, None, None])
        & (my_ranks[None, None, :] == slot_ids[None, :, None])
    )
    send_item = jnp.sum(jnp.where(send_hit, jnp.arange(items, dtype=jnp.int32), 0), axis=2)
    send_valid = jnp.any(send_hit, axis=2)
    pick = (
        send_valid[:, :, None] & (send_item[:, :, None] % REQ_DEV == jnp.arange(REQ_DEV))
    ).reshape(leaf_count * all_slots, REQ_DEV)
    outgoing = jnp.sum(
        jnp.where(
            pick[:, :, None, None],
            q_blocks.reshape(REQ_DEV, REQ_LEN, width_local)[None],
            jnp.zeros((), jnp.bfloat16),
        ),
        axis=1,
    ).reshape(leaf_count, all_slots, REQ_LEN, width_local)
    arrived = lax.all_to_all(outgoing, "leaf", split_axis=0, concat_axis=0, tiled=True)
    columns_late = lax.optimization_barrier((columns, outgoing))[0]
    key_f, value_f = (
        jnp.dot(columns_late, matrix, preferred_element_type=jnp.float32)
        for matrix in (w_key, w_value)
    )
    keys = rotate(key_f.reshape(tok_rows, heads_local, HD), position).astype(jnp.bfloat16)
    values = value_f.astype(jnp.bfloat16)
    self_out, self_lse = self_attention(
        queries.reshape(REQ_DEV, REQ_LEN, heads_local, HD),
        keys.reshape(REQ_DEV, REQ_LEN, heads_local, HD),
        values.reshape(REQ_DEV, REQ_LEN, heads_local, HD),
    )
    recv_hit = (holders[:, None, :] == device) & (ranks[:, None, :] == slot_ids[None, :, None])
    slot_nodes = jnp.sum(jnp.where(recv_hit, per_sender[:, None, :], 0), axis=2).reshape(-1)
    filled = jnp.any(recv_hit, axis=2).reshape(-1)
    local_slot = jnp.where(filled, slot_nodes - device * NODE_DEV, 0)
    lengths = jnp.where(filled, len_of(slot_nodes), 0)
    node_out, node_lse = node_attention(
        arrived.reshape(leaf_count * all_slots, REQ_LEN, width_local),
        key_cache,
        value_cache,
        local_slot,
        filled,
        lax.dynamic_slice_in_dim(node_len, device * NODE_DEV, NODE_DEV),
        heads_local,
    )
    slot_count = leaf_count * all_slots
    flat_lse = node_lse.reshape(slot_count, REQ_LEN * heads_local)
    lse_high = lax.reduce_precision(flat_lse, exponent_bits=8, mantissa_bits=7)
    lse_low = flat_lse - lse_high
    pair_width = 2 * REQ_LEN * heads_local
    lse_rows = jnp.pad(
        jnp.concatenate([lse_high, lse_low], axis=1).astype(jnp.bfloat16).reshape(
            leaf_count, all_slots, pair_width
        ),
        ((0, 0), (0, 16 - all_slots), (0, width_local - pair_width)),
    )
    payload = lax.dynamic_update_slice(node_out, lse_rows, (0, all_slots * REQ_LEN, 0))
    back = lax.all_to_all(payload, "leaf", split_axis=0, concat_axis=0, tiled=True)
    got = jnp.take(back, my_holders, axis=0)
    second = (my_ranks == 1)[:, None, None]
    got_out = jax.vmap(
        lambda h, r: lax.dynamic_slice(back, (h, r * REQ_LEN, 0), (1, REQ_LEN, width_local))[0]
    )(my_holders, my_ranks).reshape(level_count, REQ_DEV, REQ_LEN, heads_local, HD)
    lse_at = all_slots * REQ_LEN
    got_pair = jnp.where(
        second[:, 0], got[:, lse_at + 1, :pair_width], got[:, lse_at, :pair_width]
    ).astype(jnp.float32)
    lse_width = REQ_LEN * heads_local
    got_lse = jnp.swapaxes(
        (got_pair[:, :lse_width] + got_pair[:, lse_width:]).reshape(items, heads_local, REQ_LEN),
        1,
        2,
    ).reshape(level_count, REQ_DEV, REQ_LEN, heads_local)
    partial_lse = jnp.concatenate([got_lse, self_lse[None]], axis=0)
    highest = jnp.max(partial_lse, axis=0)
    factor = jnp.exp(partial_lse - highest[None])
    weighted = factor[3][..., None] * self_out
    for level in range(level_count):
        weighted = weighted + factor[level][..., None] * got_out[level].astype(jnp.float32)
    merged = weighted / jnp.sum(factor, axis=0)[..., None]
    attn = merged.astype(jnp.bfloat16).reshape(tok_rows, width_local)
    partial_value = jnp.dot(attn, w_out, preferred_element_type=jnp.float32)
    projected = lax.psum_scatter(
        partial_value.astype(jnp.bfloat16), "mp", scatter_dimension=1, tiled=True
    ).astype(jnp.float32)
    squares = mp_sum(
        jnp.sum(projected * projected, axis=1).reshape(1, tok_rows), lax.axis_size("mp")
    ).reshape(tok_rows)
    row_scale = lax.rsqrt(squares / D + norm_eps)
    return (
        activations.astype(jnp.float32) + norm_gain[None, :] * projected * row_scale[:, None]
    ).astype(jnp.bfloat16)


def solution(mesh):
    in_specs = (
        P("leaf", "mp"),
        P(None, "mp"),
        P(None, "mp"),
        P(None, "mp"),
        P("mp", None),
        P("mp"),
        P("leaf", None, "mp"),
        P("leaf", None, "mp"),
        P(),
        P(),
        P(),
    )
    out_specs = P("leaf", "mp")
    return jax.shard_map(
        on_device, mesh=mesh, in_specs=in_specs, out_specs=out_specs, check_vma=False
    )
```
